256 devices in a mesh: det: 64 (over z, x, core), exp: 4 (over y).
Axes of the slice: x: 4, y: 4, z: 8, core: 2. Of those that a mesh axis runs over, the one named last changes fastest.
Arguments:
- template: bfloat16 [2048, 128, 128], P('det'), may hold values from -4 to 4
- template_var: bfloat16 [2048, 128, 128], P('det'), may hold values from 2 to 32
- science: bfloat16 [4, 16384, 1024], P('exp', 'det'), may hold values from -10 to 10
- science_var: bfloat16 [4, 16384, 1024], P('exp', 'det'), may hold values from 0.5 to 2
- routes_src: int32 [4, 1024], P('exp', 'det'), may hold values from 0 to 63, as said below
- routes_blk: int32 [4, 1024], P('exp', 'det'), may hold values from 0 to 31
- stamp_rows: int32 [4, 256], P('exp', 'det'), may hold values from 0 to 128
- stamp_cols: int32 [4, 256], P('exp', 'det'), may hold values from 0 to 896
- basis_col: bfloat16 [40, 21], replicated, may hold values from -1.25 to 1.25
- basis_row: bfloat16 [40, 21], replicated, may hold values from -1.25 to 1.25
- psf_col: float32 [4, 21], P('exp'), may hold values from 0.05 to 0.5
- psf_row: float32 [4, 21], P('exp'), may hold values from 0.05 to 0.5
Outputs:
- significance: float32 [2048, 128, 128], P('det')
- psf_score: float32 [4, 16384, 1024], P('exp', 'det')
- coefficients: float32 [4, 2624], P('exp', 'det')
The draws below stay inside these ranges and needn't reach their ends.
Inputs may be any that keep to these rules, and one draw needn't show every extreme that they name: `routes_src`: within the 16 blocks of one device, at most 2 take their template from one owner, and on every device some owner supplies exactly 2 of them.
All inputs are finite; a program needn't handle non-finite values.
Results may differ from the reference program's by a relative error of at most 0.0085.
Values may be sent and summed in bfloat16 or wider, within the bound.
A program may use at most 128 MiB of HBM per device.

```python
import math
import jax
import jax.numpy as jnp
from jax import lax

PIX = 128
KW = 21
NBASIS = 40
BY = 2
BX = 8
TB = 32
NS = 4
EXPOSURES = 4
DETECTORS = 64
CAP = 2


def routes_of(key):
    base = jax.random.fold_in(key, 11)
    key_hot, key_forced, key_score, key_order, key_block = jax.random.split(base, 5)
    blocks_dev = BY * BX
    devices_all = EXPOSURES * DETECTORS
    slot_total = DETECTORS * CAP
    popular = (jax.random.permutation(key_hot, DETECTORS) < max(1, DETECTORS // 8)).astype(jnp.int32)
    slot_owner = jnp.arange(slot_total, dtype=jnp.int32) // CAP
    forced = jax.random.randint(key_forced, (devices_all, 1), 0, DETECTORS)
    noise_score = jax.random.randint(key_score, (devices_all, slot_total), 0, 2 ** 12)
    priority = noise_score + popular[slot_owner][None, :] * 2 ** 13 + (slot_owner[None, :] == forced).astype(jnp.int32) * 2 ** 14
    distinct = priority * slot_total + jnp.arange(slot_total, dtype=jnp.int32)[None, :]
    picked = lax.top_k(distinct, blocks_dev)[1]
    shuffle_key = jax.random.randint(key_order, (devices_all, blocks_dev), 0, 2 ** 12) * blocks_dev + jnp.arange(blocks_dev, dtype=jnp.int32)[None, :]
    ordering = jnp.argsort(shuffle_key, axis=1, stable=True)
    placed = jnp.take_along_axis(picked, ordering, axis=1)
    sources = (placed // CAP).reshape(EXPOSURES, DETECTORS * blocks_dev).astype(jnp.int32)
    indices = jax.random.randint(key_block, (EXPOSURES, DETECTORS * blocks_dev), 0, TB).astype(jnp.int32)
    return (sources, indices)


def template_of(key):
    base = jax.random.fold_in(key, 23)
    key_value = jax.random.fold_in(base, 0)
    return jnp.clip(jax.random.normal(key_value, (DETECTORS * TB, PIX, PIX)), -4.0, 4.0)


def draw_template(key, part):
    return template_of(key).astype(jnp.bfloat16)


def draw_routes_src(key, part):
    return routes_of(key)[0]


def draw_routes_blk(key, part):
    return routes_of(key)[1]


def draw_science(key, part):
    frames = template_of(key).astype(jnp.bfloat16).astype(jnp.float32)
    sources, indices = routes_of(key)
    picked = frames[(sources * TB + indices).reshape(-1)]
    base = jax.random.fold_in(key, 37)
    key_gain, key_offset, key_noise = jax.random.split(base, 3)
    blocks_all = EXPOSURES * DETECTORS * BY * BX
    gains = jax.random.uniform(key_gain, (blocks_all, 1, 1), minval=0.5, maxval=1.5)
    offsets = jax.random.uniform(key_offset, (EXPOSURES * DETECTORS, 1, 1, 1), minval=-1.0, maxval=1.0)
    noise = 0.5 * jnp.clip(jax.random.normal(key_noise, (blocks_all, PIX, PIX)), -4.0, 4.0)
    picture = (gains * picked + noise).reshape(EXPOSURES * DETECTORS, BY * BX, PIX, PIX) + offsets
    shaped = picture.reshape(EXPOSURES, DETECTORS, BY, BX, PIX, PIX).transpose(0, 1, 2, 4, 3, 5)
    return shaped.reshape(EXPOSURES, DETECTORS * BY * PIX, BX * PIX).astype(jnp.bfloat16)


def place_ends(values, rng, smallest, high):
    place = [jax.random.randint(jax.random.fold_in(rng, axis), (), 0, length) for axis, length in enumerate(values.shape)]
    widest = values.shape.index(max(values.shape))
    next_to = place[:widest] + [(place[widest] + 1) % values.shape[widest]] + place[widest + 1:]
    return values.at[tuple(place)].set(smallest).at[tuple(next_to)].set(high)


def shard_levels(stream_key, dims, shards, least, top_value):
    gain = 1.0
    for axis_at, parts in shards:
        heights = jax.random.uniform(jax.random.fold_in(jax.random.fold_in(stream_key, 6), axis_at), (parts,), jnp.float32, least / len(shards), top_value / len(shards))
        gain = gain * jnp.repeat(jnp.exp(heights), dims[axis_at] // parts).reshape((-1,) + (1,) * (len(dims) - 1 - axis_at))
    return gain


def normal_values(own_key, dims, spread, most, kind=jnp.bfloat16):
    result = spread * jax.random.normal(own_key, dims, jnp.float32)
    return jnp.clip(result, min=-most, max=most).astype(kind)


def setup_inputs(seed: int = 0) -> dict:
    seeds = jax.random.split(jax.random.key(seed), 13)
    template = draw_template(jax.random.fold_in(seeds[12], 71), 0)
    template_var = jnp.clip(jnp.exp(math.log(32.0) - 2.7725887 * jax.random.uniform(seeds[1], (DETECTORS * TB, PIX, PIX), jnp.float32) ** shard_levels(seeds[1], (DETECTORS * TB, PIX, PIX), ((0, 64),), -0.2, 0.2)), 2.0, 32.0).astype(jnp.bfloat16)
    science = draw_science(jax.random.fold_in(seeds[12], 71), 0)
    science_var = jnp.clip(jnp.exp(math.log(2.0) - 1.3862944 * jax.random.uniform(seeds[3], (EXPOSURES, DETECTORS * BY * PIX, BX * PIX), jnp.float32) ** shard_levels(seeds[3], (EXPOSURES, DETECTORS * BY * PIX, BX * PIX), ((0, 4), (1, 64)), -0.2, 0.2)), 0.5, 2.0).astype(jnp.bfloat16)
    routes_src = draw_routes_src(jax.random.fold_in(seeds[12], 71), 0)
    routes_blk = draw_routes_blk(jax.random.fold_in(seeds[12], 71), 0)
    stamp_rows = place_ends(jax.random.randint(seeds[6], (EXPOSURES, DETECTORS * NS), 0, (BY - 1) * PIX + 1), jax.random.fold_in(seeds[6], 1), 0, (BY - 1) * PIX).astype(jnp.int32)
    stamp_cols = place_ends(jax.random.randint(seeds[7], (EXPOSURES, DETECTORS * NS), 0, (BX - 1) * PIX + 1), jax.random.fold_in(seeds[7], 1), 0, (BX - 1) * PIX).astype(jnp.int32)
    basis_col = normal_values(seeds[8], (NBASIS, KW), KW ** -0.5, 1.25)
    basis_row = normal_values(seeds[9], (NBASIS, KW), KW ** -0.5, 1.25)
    psf_col = jnp.clip(jnp.exp(math.log(0.5) - 2.3025851 * jax.random.uniform(seeds[10], (EXPOSURES, KW), jnp.float32) ** shard_levels(seeds[10], (EXPOSURES, KW), ((0, 4),), -0.2, 0.2)), 0.05, 0.5)
    psf_row = jnp.clip(jnp.exp(math.log(0.5) - 2.3025851 * jax.random.uniform(seeds[11], (EXPOSURES, KW), jnp.float32) ** shard_levels(seeds[11], (EXPOSURES, KW), ((0, 4),), -0.2, 0.2)), 0.05, 0.5)
    return dict(template=template, template_var=template_var, science=science, science_var=science_var, routes_src=routes_src, routes_blk=routes_blk, stamp_rows=stamp_rows, stamp_cols=stamp_cols, basis_col=basis_col, basis_row=basis_row, psf_col=psf_col, psf_row=psf_row)


precise_mode = lax.Precision.HIGHEST
ridge_term = 0.01

def band_stack(filters, block_side):
    kernel_taps = filters.shape[1]
    inputs = jnp.arange(block_side + kernel_taps - 1)[:, None, None]
    outputs = jnp.arange(block_side)[None, :, None]
    offsets = jnp.arange(kernel_taps)[None, None, :]
    select = (inputs - outputs == offsets).astype(jnp.float32)
    return jnp.einsum('ni,rvi->nrv', filters.astype(jnp.float32), select, precision=precise_mode)

def column_windows(padded, block_side, kernel_taps):
    height_all, padded_span = padded.shape
    count_blocks = (padded_span - kernel_taps + 1) // block_side
    extended = jnp.pad(padded, ((0, 0), (0, (count_blocks + 1) * block_side - padded_span)))
    tiled_rows = extended.reshape(height_all, count_blocks + 1, block_side)
    return jnp.concatenate([tiled_rows[:, :count_blocks], tiled_rows[:, 1:, :kernel_taps - 1]], axis=2)

def row_windows(padded, block_side, kernel_taps):
    padded_span, across = padded.shape
    count_blocks = (padded_span - kernel_taps + 1) // block_side
    extended = jnp.pad(padded, ((0, (count_blocks + 1) * block_side - padded_span), (0, 0)))
    tiled_rows = extended.reshape(count_blocks + 1, block_side, across)
    return jnp.concatenate([tiled_rows[:count_blocks], tiled_rows[1:, :kernel_taps - 1]], axis=1)

def to_image(blocks, block_rows, block_cols):
    block_side = blocks.shape[-1]
    shaped = blocks.reshape(block_rows, block_cols, block_side, block_side).transpose(0, 2, 1, 3)
    return shaped.reshape(block_rows * block_side, block_cols * block_side)

def to_blocks(picture, block_side):
    height_all, across = picture.shape
    shaped = picture.reshape(height_all // block_side, block_side, across // block_side, block_side)
    return shaped.transpose(0, 2, 1, 3).reshape(-1, block_side, block_side)

def fit_kernel(frame_img, science_img, variance_img, rows_at, cols_at, basis_col, basis_row, block_side):
    kernel_taps = basis_col.shape[1]
    margin = kernel_taps // 2
    padded = jnp.pad(frame_img, margin)
    stamp_side = block_side + kernel_taps - 1

    def cut_stamp(top_row, left_col):
        return (lax.dynamic_slice(padded, (top_row, left_col), (stamp_side, stamp_side)), lax.dynamic_slice(science_img, (top_row, left_col), (block_side, block_side)), lax.dynamic_slice(variance_img, (top_row, left_col), (block_side, block_side)))
    stamps, science_cut, variance_cut = jax.vmap(cut_stamp)(rows_at, cols_at)
    col_bands = band_stack(basis_col, block_side).astype(jnp.bfloat16).astype(jnp.float32)
    row_bands = band_stack(basis_row, block_side).astype(jnp.bfloat16).astype(jnp.float32)
    vertical = jnp.einsum('kru,srx->skux', col_bands, stamps.astype(jnp.float32), precision=precise_mode).astype(jnp.bfloat16)
    design = jnp.einsum('skux,kxv->skuv', vertical.astype(jnp.float32), row_bands, precision=precise_mode)
    weight = 1.0 / variance_cut.astype(jnp.float32)
    science_f = science_cut.astype(jnp.float32)
    weighted = design * weight[:, None]
    pixel_count = rows_at.shape[0] * block_side * block_side
    gram_matrix = jnp.einsum('skuv,sluv->kl', weighted, design, precision=precise_mode)
    cross_terms = lax.optimization_barrier(jnp.sum(weighted, axis=(0, 2, 3)))
    weight_total = jnp.sum(weight)
    right_basis = jnp.einsum('skuv,suv->k', weighted, science_f, precision=precise_mode)
    right_back = jnp.sum(weight * science_f)
    upper = jnp.concatenate([gram_matrix, cross_terms[:, None]], axis=1)
    lower = jnp.concatenate([cross_terms, weight_total[None]])[None, :]
    normal = jnp.concatenate([upper, lower], axis=0) / pixel_count
    normal = normal + ridge_term * jnp.eye(normal.shape[0], dtype=jnp.float32)
    right_side = jnp.concatenate([right_basis, right_back[None]]) / pixel_count
    factor = jnp.linalg.cholesky(normal)
    return jax.scipy.linalg.cho_solve((factor, True), right_side)

def apply_kernel(frame_img, kernel_bf, block_side):
    kernel_taps = kernel_bf.shape[0]
    height_all = frame_img.shape[0]
    padded = jnp.pad(frame_img, kernel_taps // 2)
    windows = column_windows(padded, block_side, kernel_taps).astype(jnp.float32)
    kernel_bands = band_stack(kernel_bf, block_side)

    def add_row(offset, running):
        row_slab = lax.dynamic_slice_in_dim(windows, offset, height_all, 0)
        return running + jnp.einsum('ycr,rv->ycv', row_slab, kernel_bands[offset], precision=precise_mode)
    start = jnp.zeros((height_all, windows.shape[1], block_side), jnp.float32)
    return lax.fori_loop(0, kernel_taps, add_row, start).reshape(height_all, -1)

def correlate_psf(difference, psf_down, psf_across, block_side):
    kernel_taps = psf_down.shape[0]
    margin = kernel_taps // 2
    height_all, across = difference.shape
    data = difference.astype(jnp.float32)
    across_band = band_stack(psf_across[None, :], block_side)[0]
    windows = column_windows(jnp.pad(data, ((0, 0), (margin, margin))), block_side, kernel_taps)
    sideways = jnp.einsum('ycr,rv->ycv', windows, across_band, precision=precise_mode).reshape(height_all, across)
    down_band = band_stack(psf_down[None, :], block_side)[0]
    stacked = row_windows(jnp.pad(sideways, ((margin, margin), (0, 0))), block_side, kernel_taps)
    return jnp.einsum('brw,ru->buw', stacked, down_band, precision=precise_mode).reshape(height_all, across)

def reference(template, template_var, science, science_var, routes_src, routes_blk, stamp_rows, stamp_cols, basis_col, basis_row, psf_col, psf_row):
    blocks_dev = BY * BX
    height_all = BY * PIX
    across = BX * PIX
    source_ids = (routes_src * TB + routes_blk).reshape(-1).astype(jnp.int32)
    frames = template[source_ids].reshape(EXPOSURES * DETECTORS, blocks_dev, PIX, PIX)
    frame_vars = template_var[source_ids].reshape(EXPOSURES * DETECTORS, blocks_dev, PIX, PIX)
    science_all = science.reshape(EXPOSURES * DETECTORS, height_all, across)
    variance_all = science_var.reshape(EXPOSURES * DETECTORS, height_all, across)
    rows_all = stamp_rows.reshape(EXPOSURES * DETECTORS, NS)
    cols_all = stamp_cols.reshape(EXPOSURES * DETECTORS, NS)
    psf_downs = jnp.repeat(psf_col, DETECTORS, axis=0)
    psf_acrosses = jnp.repeat(psf_row, DETECTORS, axis=0)

    def process_detector(inputs):
        frame_blocks, tvar_blocks, science_img, variance_img, rows_at, cols_at, psf_down, psf_across = inputs
        frame_img = to_image(frame_blocks, BY, BX)
        fitted = fit_kernel(frame_img, science_img, variance_img, rows_at, cols_at, basis_col, basis_row, PIX)
        kernel = jnp.einsum('k,ki,kj->ij', fitted[:NBASIS], basis_col.astype(jnp.float32), basis_row.astype(jnp.float32), precision=precise_mode)
        kernel_sum = jnp.sum(kernel)
        matched = apply_kernel(frame_img, kernel.astype(jnp.bfloat16), PIX)
        difference = (science_img.astype(jnp.float32) - matched - fitted[NBASIS]).astype(jnp.bfloat16)
        scored = correlate_psf(difference, psf_down, psf_across, PIX)
        diff_blocks = to_blocks(difference, PIX)
        var_blocks = to_blocks(variance_img, PIX).astype(jnp.float32) + kernel_sum * kernel_sum * tvar_blocks.astype(jnp.float32)
        return (fitted, diff_blocks, var_blocks, scored)
    fitted_all, diff_all, var_all, scored_all = lax.map(process_detector, (frames, frame_vars, science_all, variance_all, rows_all, cols_all, psf_downs, psf_acrosses))
    diff_total = jax.ops.segment_sum(diff_all.reshape(-1, PIX, PIX).astype(jnp.float32), source_ids, num_segments=DETECTORS * TB)
    var_total = jax.ops.segment_sum(var_all.reshape(-1, PIX, PIX), source_ids, num_segments=DETECTORS * TB)
    significance = diff_total / jnp.sqrt(jnp.maximum(var_total, 1.0))
    return (significance, scored_all.reshape(EXPOSURES, DETECTORS * height_all, across), fitted_all.reshape(EXPOSURES, DETECTORS * (NBASIS + 1)))
```

```python
import jax, jax.numpy as jnp
from jax import lax
from jax.experimental import pallas as pl
from jax.experimental.pallas import tpu as pltpu

from jax.sharding import PartitionSpec as P

HI = lax.Precision.HIGHEST
precise_mode = HI
RS = 520

def fit_body(rows_s, cols_s, fp_ref, sci_ref, var_ref, colb_ref, rowb_ref, bc_ref, br_ref,
             coef_ref, diff_ref, ks_ref,
             sci32, var32, stk, dsg, sst, wst, wb, fs, conv, f128):
    f32, bf16 = jnp.float32, jnp.bfloat16
    sci32[:256, :1024] = sci_ref[...].astype(f32)
    var32[:256, :1024] = var_ref[...].astype(f32)
    for s in range(4):
        y0 = rows_s[s]
        x0 = cols_s[s]
        xa = pl.multiple_of((x0 // 128) * 128, 128)
        rem = x0 - xa
        ya = pl.multiple_of((y0 // 8) * 8, 8)
        ry = y0 - ya
        t = pltpu.roll(fp_ref[pl.ds(ya, 168), pl.ds(xa, 384)], 168 - ry, 0)[:160]
        t = pltpu.roll(t, 384 - rem, 1)[:, :256]
        stk[:, s * 256:(s + 1) * 256] = t.astype(bf16)
        c = pltpu.roll(sci32[pl.ds(ya, 136), pl.ds(xa, 256)], 136 - ry, 0)[:128]
        sst[s * 128:(s + 1) * 128, :] = pltpu.roll(c, 256 - rem, 1)[:, :128]
        v = pltpu.roll(var32[pl.ds(ya, 136), pl.ds(xa, 256)], 136 - ry, 0)[:128]
        wst[s * 128:(s + 1) * 128, :] = 1.0 / pltpu.roll(v, 256 - rem, 1)[:, :128]

    def per_basis(k, _):
        a = jnp.dot(colb_ref[k], stk[...], preferred_element_type=f32).astype(bf16)
        rb = rowb_ref[k]
        for s in range(4):
            d = jnp.dot(a[:, s * 256:(s + 1) * 256], rb, preferred_element_type=f32)
            dsg[pl.ds(pl.multiple_of(k * RS + s * 128, 8), 128), :] = d
        return 0
    lax.fori_loop(0, 40, per_basis, 0)

    sub = lax.broadcasted_iota(jnp.int32, (8, 128), 0)

    def per_rows(g, acc):
        xs, ys = [], []
        for q in range(8):
            r = g * 8 + q
            x = dsg[pl.ds(r, 40, stride=RS), :]
            srow = jnp.broadcast_to(sst[pl.ds(r, 1), :], (8, 128))
            extra = jnp.where(sub == 0, 1.0, jnp.where(sub == 1, srow, 0.0))
            x = jnp.concatenate([x, extra], axis=0)
            w = jnp.broadcast_to(wst[pl.ds(r, 1), :], (48, 128))
            xs.append(x)
            ys.append(x * w)
        x = jnp.concatenate(xs, axis=1)
        y = jnp.concatenate(ys, axis=1)
        xh = x.astype(bf16)
        xl = (x - xh.astype(f32)).astype(bf16)
        yh = y.astype(bf16)
        yl = (y - yh.astype(f32)).astype(bf16)
        nt = (((1,), (1,)), ((), ()))
        lhs = jnp.concatenate([yh, yh, yl], axis=1)
        rhs = jnp.concatenate([xh, xl, xh], axis=1)
        return acc + lax.dot_general(lhs, rhs, nt, preferred_element_type=f32)
    gram = lax.fori_loop(0, 64, per_rows, jnp.zeros((48, 48), f32))

    ri = lax.broadcasted_iota(jnp.int32, (48, 48), 0)
    ci = lax.broadcasted_iota(jnp.int32, (48, 48), 1)
    m = gram * (1.0 / 65536.0) + jnp.where((ri == ci) & (ri < 41), 0.01, 0.0)
    for n in range(41):
        prow = m[n:n + 1, :]
        pcol = m[:, n:n + 1]
        new = prow / m[n:n + 1, n:n + 1]
        m = jnp.where(ri == n, jnp.broadcast_to(new, (48, 48)), m - pcol * new)
    rcol = lax.broadcasted_iota(jnp.int32, (48, 1), 0)
    col = m[:, 41:42]
    row = jnp.sum(jnp.where(ri == ci, jnp.broadcast_to(col, (48, 48)), 0.0), axis=0, keepdims=True)
    coef_ref[...] = jnp.broadcast_to(jnp.pad(row, ((0, 0), (0, 80))), (8, 128))
    bg = m[40:41, 41:42]
    ccol = jnp.where(rcol < 40, col, 0.0)
    tn = (((0,), (0,)), ((), ()))
    ker = lax.dot_general(bc_ref[...] * ccol, br_ref[...], tn, precision=HI, preferred_element_type=f32)
    ker = ker[:24, :]
    ks = jnp.sum(ker, keepdims=True)
    ks_ref[...] = jnp.broadcast_to(ks * ks, (8, 128))
    wb[0, :, 128:] = jnp.zeros((256, 128), bf16)
    wb[21, :, :128] = jnp.zeros((256, 128), bf16)
    for dy in range(21):
        base = jnp.broadcast_to(ker[dy:dy + 1, :], (256, 256))
        band = pltpu.roll(base, 0, 1, stride=1, stride_axis=0)[:, :128].astype(bf16)
        wb[dy, :, :128] = band
        wb[dy + 1, :, 128:] = band
    for cc in range(9):
        sl = slice(cc * 128, (cc + 1) * 128)
        f128[cc] = fp_ref[:280, sl]
    for cc in range(9):
        sl = slice(cc * 128, (cc + 1) * 128)
        for dy in range(22):
            fs[dy, :, sl] = f128[cc, pl.ds(dy, 128, stride=2), :].astype(bf16)

    def per_col(c, _):
        c0 = pl.multiple_of(c * 128, 128)
        acc = jnp.zeros((128, 256), f32)
        for dy in range(22):
            acc = acc + jnp.dot(fs[dy, :, pl.ds(c0, 256)], wb[dy], preferred_element_type=f32)
        conv[pl.ds(0, 128, stride=2), :] = acc[:, :128]
        conv[pl.ds(1, 128, stride=2), :] = acc[:, 128:]
        for i in range(2):
            d = sci32[i * 128:(i + 1) * 128, pl.ds(c0, 128)] - conv[i * 128:(i + 1) * 128, :] - bg
            diff_ref[c + 8 * i] = d.astype(bf16)
        return 0
    lax.fori_loop(0, 8, per_col, 0)

def fit_call(rows, cols, fp, sci, var, colb, rowb, bc, br):
    f32, bf16 = jnp.float32, jnp.bfloat16
    sm = pl.BlockSpec(memory_space=pltpu.SMEM)
    vm = pl.BlockSpec(memory_space=pltpu.VMEM)
    return pl.pallas_call(
        fit_body,
        out_shape=(jax.ShapeDtypeStruct((8, 128), f32), jax.ShapeDtypeStruct((16, 128, 128), bf16),
                   jax.ShapeDtypeStruct((8, 128), f32)),
        in_specs=[sm, sm] + [vm] * 7,
        out_specs=(vm, vm, vm),
        scratch_shapes=[
            pltpu.VMEM((264, 1152), f32), pltpu.VMEM((264, 1152), f32),
            pltpu.VMEM((160, 1024), bf16), pltpu.VMEM((40 * RS, 128), f32),
            pltpu.VMEM((512, 128), f32), pltpu.VMEM((512, 128), f32),
            pltpu.VMEM((22, 256, 256), bf16), pltpu.VMEM((22, 128, 1152), bf16),
            pltpu.VMEM((256, 128), f32), pltpu.VMEM((9, 280, 128), f32)],
        compiler_params=pltpu.CompilerParams(vmem_limit_bytes=60 * 1024 * 1024),
        name="fit",
    )(rows, cols, fp, sci, var, colb, rowb, bc, br)

def toeplitz(basis, select):
    return jnp.einsum("ni,rvi->nrv", basis, select, preferred_element_type=jnp.bfloat16)


def bands(basis_col, basis_row):
    bf16 = jnp.bfloat16
    taps = jnp.arange(21)[None, None, :]
    tall = jnp.arange(256)[:, None, None]
    flat = jnp.arange(128)[None, :, None]
    colb = toeplitz(basis_col, (jnp.arange(160)[None, :, None] - jnp.arange(128)[:, None, None] == taps).astype(bf16))
    rowb = toeplitz(basis_row, (tall - flat == taps).astype(bf16))
    bc = jnp.pad(basis_col.astype(jnp.float32), ((0, 8), (0, 107)))
    br = jnp.pad(basis_row.astype(jnp.float32), ((0, 8), (0, 0)))
    rev = jnp.concatenate([br[:, :1], jnp.zeros((48, 235), jnp.float32), br[:, :0:-1]], axis=1)
    return colb, rowb, bc, rev


def band_stack(filters, block_side):
    kernel_taps = filters.shape[1]
    inputs = jnp.arange(block_side + kernel_taps - 1)[:, None, None]
    outputs = jnp.arange(block_side)[None, :, None]
    offsets = jnp.arange(kernel_taps)[None, None, :]
    select = (inputs - outputs == offsets).astype(jnp.float32)
    return jnp.einsum("ni,rvi->nrv", filters.astype(jnp.float32), select, precision=precise_mode)


def column_windows(padded, block_side, kernel_taps):
    height_all, padded_span = padded.shape
    count_blocks = (padded_span - kernel_taps + 1) // block_side
    extended = jnp.pad(padded, ((0, 0), (0, (count_blocks + 1) * block_side - padded_span)))
    tiled_rows = extended.reshape(height_all, count_blocks + 1, block_side)
    return jnp.concatenate(
        [tiled_rows[:, :count_blocks], tiled_rows[:, 1:, : kernel_taps - 1]], axis=2
    )


def row_windows(padded, block_side, kernel_taps):
    padded_span, across = padded.shape
    count_blocks = (padded_span - kernel_taps + 1) // block_side
    extended = jnp.pad(padded, ((0, (count_blocks + 1) * block_side - padded_span), (0, 0)))
    tiled_rows = extended.reshape(count_blocks + 1, block_side, across)
    return jnp.concatenate([tiled_rows[:count_blocks], tiled_rows[1:, : kernel_taps - 1]], axis=1)


def to_image(blocks, block_rows, block_cols):
    block_side = blocks.shape[-1]
    shaped = blocks.reshape(block_rows, block_cols, block_side, block_side).transpose(0, 2, 1, 3)
    return shaped.reshape(block_rows * block_side, block_cols * block_side)


def to_blocks(picture, block_side):
    height_all, across = picture.shape
    shaped = picture.reshape(height_all // block_side, block_side, across // block_side, block_side)
    return shaped.transpose(0, 2, 1, 3).reshape(-1, block_side, block_side)


def correlate_psf(difference, psf_down, psf_across, block_side):
    kernel_taps = psf_down.shape[0]
    margin = kernel_taps // 2
    height_all, across = difference.shape
    data = difference.astype(jnp.float32)
    across_band = band_stack(psf_across[None, :], block_side)[0]
    windows = column_windows(jnp.pad(data, ((0, 0), (margin, margin))), block_side, kernel_taps)
    sideways = jnp.einsum("ycr,rv->ycv", windows, across_band, precision=precise_mode).reshape(
        height_all, across
    )
    down_band = band_stack(psf_down[None, :], block_side)[0]
    stacked = row_windows(jnp.pad(sideways, ((margin, margin), (0, 0))), block_side, kernel_taps)
    return jnp.einsum("brw,ru->buw", stacked, down_band, precision=precise_mode).reshape(
        height_all, across
    )


def local(
    template,
    template_var,
    science,
    science_var,
    routes_src,
    routes_blk,
    stamp_rows,
    stamp_cols,
    basis_col,
    basis_row,
    psf_col,
    psf_row,
):
    peer_count = lax.axis_size("det")
    block_side = template.shape[1]
    tract_blocks = template.shape[0]
    science_img = science[0]
    variance_img = science_var[0]
    block_rows = science_img.shape[0] // block_side
    block_cols = science_img.shape[1] // block_side
    blocks_dev = block_rows * block_cols
    basis_count = basis_col.shape[0]
    capacity = max(2, (blocks_dev + peer_count - 1) // peer_count)
    slot_count = peer_count * capacity
    owner_of = routes_src[0]
    wanted = routes_blk[0]
    owner_hot = (owner_of[:, None] == jnp.arange(peer_count, dtype=jnp.int32)[None, :]).astype(
        jnp.int32
    )
    earlier = jnp.cumsum(owner_hot, axis=0) - owner_hot
    slot_of = owner_of * capacity + jnp.sum(earlier * owner_hot, axis=1)
    slot_hot = (slot_of[:, None] == jnp.arange(slot_count, dtype=jnp.int32)[None, :]).astype(
        jnp.int32
    )
    request = jnp.sum(slot_hot * (wanted[:, None] + 1), axis=0).reshape(peer_count, capacity)
    incoming = lax.all_to_all(request, "det", split_axis=0, concat_axis=0, tiled=True).reshape(
        slot_count
    )
    chosen = jnp.maximum(incoming - 1, 0)
    arrived = lax.all_to_all(template[chosen], "det", split_axis=0, concat_axis=0, tiled=True)
    sender = jnp.sum(slot_hot * jnp.arange(blocks_dev, dtype=jnp.int32)[:, None], axis=0)
    svar_blocks = to_blocks(variance_img, block_side)
    back_var = lax.all_to_all(svar_blocks[sender], "det", split_axis=0, concat_axis=0, tiled=True)
    frame_img = to_image(arrived[slot_of], block_rows, block_cols)
    fp = jnp.pad(frame_img.astype(jnp.float32), ((10, 30), (10, 246)))
    coef, diff_blocks, ks2 = fit_call(
        stamp_rows[0], stamp_cols[0], fp, science_img, variance_img, *bands(basis_col, basis_row)
    )
    fitted = coef[0, : basis_count + 1]
    squares = lax.all_gather(ks2[0, :1], "det", tiled=True)
    back_diff = lax.all_to_all(diff_blocks[sender], "det", split_axis=0, concat_axis=0, tiled=True)
    scored = correlate_psf(
        to_image(diff_blocks, block_rows, block_cols), psf_col[0], psf_row[0], block_side
    )
    tract_hot = incoming[None, :] - 1 == jnp.arange(tract_blocks, dtype=jnp.int32)[:, None]
    hot = tract_hot.astype(jnp.bfloat16)
    tract_float = tract_hot.astype(jnp.float32)
    var_part = jnp.einsum("mq,qpv->mpv", hot, back_var, preferred_element_type=jnp.float32)
    square_sum = jnp.sum(tract_float * jnp.repeat(squares, capacity)[None, :], axis=1)
    var_total = var_part + square_sum[:, None, None] * template_var.astype(jnp.float32)
    diff_total = jnp.einsum("mq,qpv->mpv", hot, back_diff, preferred_element_type=jnp.float32)
    summed_diff, summed_var = (
        lax.psum(diff_total.astype(jnp.bfloat16), "exp").astype(jnp.float32),
        lax.psum(var_total.astype(jnp.bfloat16), "exp").astype(jnp.float32),
    )
    significance = summed_diff / jnp.sqrt(jnp.maximum(summed_var, 1.0))
    return (significance, scored[None], fitted[None])


def solution(mesh):
    placed = (
        P("det", None, None),
        P("det", None, None),
        P("exp", "det", None),
        P("exp", "det", None),
        P("exp", "det"),
        P("exp", "det"),
        P("exp", "det"),
        P("exp", "det"),
        P(),
        P(),
        P("exp", None),
        P("exp", None),
    )
    return jax.shard_map(
        local,
        mesh=mesh,
        in_specs=placed,
        out_specs=(P("det", None, None), P("exp", "det", None), P("exp", "det")),
        check_vma=False,
    )
```

```python
import jax, jax.numpy as jnp
from jax import lax
from jax.experimental import pallas as pl
from jax.experimental.pallas import tpu as pltpu

from jax.sharding import Mesh, PartitionSpec as P

HI = lax.Precision.HIGHEST
precise_mode = HI
RS = 520

def fit_body(rows_s, cols_s, fp_ref, sci_ref, var_ref, colb_ref, rowb_ref, bc_ref, br_ref,
             coef_ref, diff_ref, ks_ref,
             sci32, var32, stk, dsg, sst, wst, wb, fs, conv, f128):
    f32, bf16 = jnp.float32, jnp.bfloat16
    sci32[:256, :1024] = sci_ref[...].astype(f32)
    var32[:256, :1024] = var_ref[...].astype(f32)
    for s in range(4):
        y0 = rows_s[s]
        x0 = cols_s[s]
        xa = pl.multiple_of((x0 // 128) * 128, 128)
        rem = x0 - xa
        ya = pl.multiple_of((y0 // 8) * 8, 8)
        ry = y0 - ya
        t = pltpu.roll(fp_ref[pl.ds(ya, 168), pl.ds(xa, 384)], 168 - ry, 0)[:160]
        t = pltpu.roll(t, 384 - rem, 1)[:, :256]
        stk[:, s * 256:(s + 1) * 256] = t.astype(bf16)
        c = pltpu.roll(sci32[pl.ds(ya, 136), pl.ds(xa, 256)], 136 - ry, 0)[:128]
        sst[s * 128:(s + 1) * 128, :] = pltpu.roll(c, 256 - rem, 1)[:, :128]
        v = pltpu.roll(var32[pl.ds(ya, 136), pl.ds(xa, 256)], 136 - ry, 0)[:128]
        wst[s * 128:(s + 1) * 128, :] = 1.0 / pltpu.roll(v, 256 - rem, 1)[:, :128]

    def per_basis(k, _):
        a = jnp.dot(colb_ref[k], stk[...], preferred_element_type=f32).astype(bf16)
        rb = rowb_ref[k]
        for s in range(4):
            d = jnp.dot(a[:, s * 256:(s + 1) * 256], rb, preferred_element_type=f32)
            dsg[pl.ds(pl.multiple_of(k * RS + s * 128, 8), 128), :] = d
        return 0
    lax.fori_loop(0, 40, per_basis, 0)

    sub = lax.broadcasted_iota(jnp.int32, (8, 128), 0)

    def per_rows(g, acc):
        xs, ys = [], []
        for q in range(8):
            r = g * 8 + q
            x = dsg[pl.ds(r, 40, stride=RS), :]
            srow = jnp.broadcast_to(sst[pl.ds(r, 1), :], (8, 128))
            extra = jnp.where(sub == 0, 1.0, jnp.where(sub == 1, srow, 0.0))
            x = jnp.concatenate([x, extra], axis=0)
            w = jnp.broadcast_to(wst[pl.ds(r, 1), :], (48, 128))
            xs.append(x)
            ys.append(x * w)
        x = jnp.concatenate(xs, axis=1)
        y = jnp.concatenate(ys, axis=1)
        xh = x.astype(bf16)
        xl = (x - xh.astype(f32)).astype(bf16)
        yh = y.astype(bf16)
        yl = (y - yh.astype(f32)).astype(bf16)
        nt = (((1,), (1,)), ((), ()))
        lhs = jnp.concatenate([yh, yh, yl], axis=1)
        rhs = jnp.concatenate([xh, xl, xh], axis=1)
        return acc + lax.dot_general(lhs, rhs, nt, preferred_element_type=f32)
    gram = lax.fori_loop(0, 64, per_rows, jnp.zeros((48, 48), f32))

    ri = lax.broadcasted_iota(jnp.int32, (48, 48), 0)
    ci = lax.broadcasted_iota(jnp.int32, (48, 48), 1)
    m = gram * (1.0 / 65536.0) + jnp.where((ri == ci) & (ri < 41), 0.01, 0.0)
    for n in range(41):
        prow = m[n:n + 1, :]
        pcol = m[:, n:n + 1]
        new = prow / m[n:n + 1, n:n + 1]
        m = jnp.where(ri == n, jnp.broadcast_to(new, (48, 48)), m - pcol * new)
    rcol = lax.broadcasted_iota(jnp.int32, (48, 1), 0)
    col = m[:, 41:42]
    row = jnp.sum(jnp.where(ri == ci, jnp.broadcast_to(col, (48, 48)), 0.0), axis=0, keepdims=True)
    coef_ref[...] = jnp.broadcast_to(jnp.pad(row, ((0, 0), (0, 80))), (8, 128))
    bg = m[40:41, 41:42]
    ccol = jnp.where(rcol < 40, col, 0.0)
    tn = (((0,), (0,)), ((), ()))
    ker = lax.dot_general(bc_ref[...] * ccol, br_ref[...], tn, precision=HI, preferred_element_type=f32)
    ker = ker[:24, :]
    ks = jnp.sum(ker, keepdims=True)
    ks_ref[...] = jnp.broadcast_to(ks * ks, (8, 128))
    wb[0, :, 128:] = jnp.zeros((256, 128), bf16)
    wb[21, :, :128] = jnp.zeros((256, 128), bf16)
    for dy in range(21):
        base = jnp.broadcast_to(ker[dy:dy + 1, :], (256, 256))
        band = pltpu.roll(base, 0, 1, stride=1, stride_axis=0)[:, :128].astype(bf16)
        wb[dy, :, :128] = band
        wb[dy + 1, :, 128:] = band
    for cc in range(9):
        sl = slice(cc * 128, (cc + 1) * 128)
        f128[cc] = fp_ref[:280, sl]
    for cc in range(9):
        sl = slice(cc * 128, (cc + 1) * 128)
        for dy in range(22):
            fs[dy, :, sl] = f128[cc, pl.ds(dy, 128, stride=2), :].astype(bf16)

    def per_col(c, _):
        c0 = pl.multiple_of(c * 128, 128)
        acc = jnp.zeros((128, 256), f32)
        for dy in range(22):
            acc = acc + jnp.dot(fs[dy, :, pl.ds(c0, 256)], wb[dy], preferred_element_type=f32)
        conv[pl.ds(0, 128, stride=2), :] = acc[:, :128]
        conv[pl.ds(1, 128, stride=2), :] = acc[:, 128:]
        for i in range(2):
            d = sci32[i * 128:(i + 1) * 128, pl.ds(c0, 128)] - conv[i * 128:(i + 1) * 128, :] - bg
            diff_ref[c + 8 * i] = d.astype(bf16)
        return 0
    lax.fori_loop(0, 8, per_col, 0)

def fit_call(rows, cols, fp, sci, var, colb, rowb, bc, br):
    f32, bf16 = jnp.float32, jnp.bfloat16
    sm = pl.BlockSpec(memory_space=pltpu.SMEM)
    vm = pl.BlockSpec(memory_space=pltpu.VMEM)
    return pl.pallas_call(
        fit_body,
        out_shape=(jax.ShapeDtypeStruct((8, 128), f32), jax.ShapeDtypeStruct((16, 128, 128), bf16),
                   jax.ShapeDtypeStruct((8, 128), f32)),
        in_specs=[sm, sm] + [vm] * 7,
        out_specs=(vm, vm, vm),
        scratch_shapes=[
            pltpu.VMEM((264, 1152), f32), pltpu.VMEM((264, 1152), f32),
            pltpu.VMEM((160, 1024), bf16), pltpu.VMEM((40 * RS, 128), f32),
            pltpu.VMEM((512, 128), f32), pltpu.VMEM((512, 128), f32),
            pltpu.VMEM((22, 256, 256), bf16), pltpu.VMEM((22, 128, 1152), bf16),
            pltpu.VMEM((256, 128), f32), pltpu.VMEM((9, 280, 128), f32)],
        compiler_params=pltpu.CompilerParams(vmem_limit_bytes=60 * 1024 * 1024),
        name="fit",
    )(rows, cols, fp, sci, var, colb, rowb, bc, br)

def toeplitz(basis, select):
    return jnp.einsum("ni,rvi->nrv", basis, select, preferred_element_type=jnp.bfloat16)


def bands(basis_col, basis_row):
    bf16 = jnp.bfloat16
    taps = jnp.arange(21)[None, None, :]
    tall = jnp.arange(256)[:, None, None]
    flat = jnp.arange(128)[None, :, None]
    colb = toeplitz(basis_col, (jnp.arange(160)[None, :, None] - jnp.arange(128)[:, None, None] == taps).astype(bf16))
    rowb = toeplitz(basis_row, (tall - flat == taps).astype(bf16))
    bc = jnp.pad(basis_col.astype(jnp.float32), ((0, 8), (0, 107)))
    br = jnp.pad(basis_row.astype(jnp.float32), ((0, 8), (0, 0)))
    rev = jnp.concatenate([br[:, :1], jnp.zeros((48, 235), jnp.float32), br[:, :0:-1]], axis=1)
    return colb, rowb, bc, rev


def band_stack(filters, block_side):
    kernel_taps = filters.shape[1]
    inputs = jnp.arange(block_side + kernel_taps - 1)[:, None, None]
    outputs = jnp.arange(block_side)[None, :, None]
    offsets = jnp.arange(kernel_taps)[None, None, :]
    select = (inputs - outputs == offsets).astype(jnp.float32)
    return jnp.einsum("ni,rvi->nrv", filters.astype(jnp.float32), select, precision=precise_mode)


def column_windows(padded, block_side, kernel_taps):
    height_all, padded_span = padded.shape
    count_blocks = (padded_span - kernel_taps + 1) // block_side
    extended = jnp.pad(padded, ((0, 0), (0, (count_blocks + 1) * block_side - padded_span)))
    tiled_rows = extended.reshape(height_all, count_blocks + 1, block_side)
    return jnp.concatenate(
        [tiled_rows[:, :count_blocks], tiled_rows[:, 1:, : kernel_taps - 1]], axis=2
    )


def row_windows(padded, block_side, kernel_taps):
    padded_span, across = padded.shape
    count_blocks = (padded_span - kernel_taps + 1) // block_side
    extended = jnp.pad(padded, ((0, (count_blocks + 1) * block_side - padded_span), (0, 0)))
    tiled_rows = extended.reshape(count_blocks + 1, block_side, across)
    return jnp.concatenate([tiled_rows[:count_blocks], tiled_rows[1:, : kernel_taps - 1]], axis=1)


def to_image(blocks, block_rows, block_cols):
    block_side = blocks.shape[-1]
    shaped = blocks.reshape(block_rows, block_cols, block_side, block_side).transpose(0, 2, 1, 3)
    return shaped.reshape(block_rows * block_side, block_cols * block_side)


def to_blocks(picture, block_side):
    height_all, across = picture.shape
    shaped = picture.reshape(height_all // block_side, block_side, across // block_side, block_side)
    return shaped.transpose(0, 2, 1, 3).reshape(-1, block_side, block_side)


def correlate_psf(difference, psf_down, psf_across, block_side):
    kernel_taps = psf_down.shape[0]
    margin = kernel_taps // 2
    height_all, across = difference.shape
    data = difference.astype(jnp.float32)
    across_band = band_stack(psf_across[None, :], block_side)[0]
    windows = column_windows(jnp.pad(data, ((0, 0), (margin, margin))), block_side, kernel_taps)
    sideways = jnp.einsum("ycr,rv->ycv", windows, across_band, precision=precise_mode).reshape(
        height_all, across
    )
    down_band = band_stack(psf_down[None, :], block_side)[0]
    stacked = row_windows(jnp.pad(sideways, ((margin, margin), (0, 0))), block_side, kernel_taps)
    return jnp.einsum("brw,ru->buw", stacked, down_band, precision=precise_mode).reshape(
        height_all, across
    )


MESH_ID = pl.DeviceIdType.MESH
SIDE = 128


class Net:
    def __init__(self, ssem, rsem):
        self.ssem, self.rsem, self.sent = ssem, rsem, []
        self.z, self.x, self.c, self.y = (lax.axis_index(a) for a in ("z", "x", "core", "y"))

    def at(self, dz=0, dx=0, dy=0, flip=False):
        c = 1 - self.c if flip else self.c
        return ((self.z + dz + 8) % 8, (self.x + dx + 4) % 4, c, (self.y + dy + 4) % 4)

    def meet(self, peers):
        barrier = pltpu.get_barrier_semaphore()
        for peer in peers:
            pl.semaphore_signal(barrier, inc=1, device_id=peer, device_id_type=MESH_ID)
        pl.semaphore_wait(barrier, len(peers))

    def send(self, src, dst, peer):
        i = len(self.sent)
        copy = pltpu.make_async_remote_copy(
            src_ref=src, dst_ref=dst, send_sem=self.ssem.at[i], recv_sem=self.rsem.at[i],
            device_id=peer, device_id_type=MESH_ID,
        )
        copy.start()
        self.sent.append(copy)
        return copy

    def drain(self):
        for copy in self.sent:
            copy.wait_send()


class ZRing:
    def __init__(self, net, own, out, pieces, arrive):
        self.net, self.out, self.pieces, self.arrive = net, out, pieces, arrive
        self.got = {}
        for p, (start, size) in enumerate(pieces):
            for d in (1, -1):
                self.got[d, 1, p] = net.send(
                    own.at[pl.ds(start, size)], out.at[net.z, net.c, pl.ds(start, size)], net.at(dz=d)
                )

    def part(self, p, d, s):
        start, size = self.pieces[p]
        if s < 4:
            return pl.ds(start, size)
        return pl.ds(start + (0 if d == 1 else size // 2), size // 2)

    def step(self, s):
        net = self.net
        for p in range(len(self.pieces)):
            for d in (1, -1):
                self.got[d, s, p].wait_recv()
                zs = (net.z - d * s + 8) % 8
                if s < 4:
                    ref = self.out.at[zs, net.c, self.part(p, d, s + 1)]
                    self.got[d, s + 1, p] = net.send(ref, ref, net.at(dz=d))
                self.arrive(p, d, s, zs, self.part(p, d, s))


class SmallRing:
    def __init__(self, net, own, out):
        self.net, self.out = net, out
        out[net.c, net.z] = own[...]
        self.got = {(d, 1): net.send(own, out.at[net.c, net.z], net.at(dz=d)) for d in (1, -1)}

    def step(self, s):
        net = self.net
        for d in (1, -1):
            if (d, s) not in self.got:
                continue
            self.got[d, s].wait_recv()
            zs = (net.z - d * s + 8) % 8
            if s + 1 <= (4 if d == 1 else 3):
                ref = self.out.at[net.c, zs]
                self.got[d, s + 1] = net.send(ref, ref, net.at(dz=d))

    def pair(self):
        ref = self.out.at[self.net.c]
        return self.net.send(ref, ref, self.net.at(flip=True))


class Ring4:
    def __init__(self, net, axis, src, dst, relay):
        self.net, self.dst, self.relay = net, dst, relay
        self.up = net.at(**{axis: 1})
        self.down = net.at(**{axis: -1})
        self.fa = net.send(src(2, 0), relay(0), self.up)
        self.fb = net.send(src(2, 1), relay(1), self.down)
        self.na = net.send(src(1, None), dst(0, None), self.up)
        self.nb = net.send(src(-1, None), dst(1, None), self.down)

    def pass_on(self):
        self.fa.wait_recv()
        self.ra = self.net.send(self.relay(0), self.dst(2, 0), self.up)
        self.fb.wait_recv()
        self.rb = self.net.send(self.relay(1), self.dst(2, 1), self.down)

    def finish(self):
        for copy in (self.na, self.nb, self.ra, self.rb):
            copy.wait_recv()


def comm_call(body, outs, spaces, scratch, copies, ident, name, in_spaces, side_bytes):
    def spec(space):
        return pl.BlockSpec(memory_space=pltpu.VMEM if space == "v" else pl.ANY)

    return pl.pallas_call(
        body,
        out_shape=tuple(jax.ShapeDtypeStruct(s, d) for s, d in outs),
        in_specs=[spec(s) for s in in_spaces],
        out_specs=tuple(spec(s) for s in spaces),
        scratch_shapes=list(scratch)
        + [pltpu.SemaphoreType.DMA((copies,)), pltpu.SemaphoreType.DMA((copies,)), pltpu.SemaphoreType.DMA((2,))],
        compiler_params=pltpu.CompilerParams(
            collective_id=ident, has_side_effects=True, vmem_limit_bytes=side_bytes << 20
        ),
        name=name,
    )


def spread_body(t_ref, r_ref, gt, rz, rx, ssem, rsem, lsem):
    net = Net(ssem, rsem)
    z, x, c, y = net.z, net.x, net.c, net.y
    net.meet([net.at(dz=1), net.at(dz=-1), net.at(dy=1), net.at(dy=-1),
              net.at(dx=1), net.at(dx=-1), net.at(dx=2), net.at(flip=True)])
    own = pltpu.make_async_copy(t_ref, gt.at[z, c], lsem.at[0])
    small = SmallRing(net, r_ref, rz)
    rx[x] = r_ref[...]
    row = [net.send(r_ref, rx.at[x], net.at(dx=k)) for k in (1, -1, 2)]
    q0 = y * 8
    q1 = ((y + 1) % 4) * 8
    up = {}

    def arrive(p, d, s, zs, part):
        ref = gt.at[zs, c, part]
        up[p, d, s] = net.send(ref, ref, net.at(dy=1 if p == 0 else -1))

    ring = ZRing(net, t_ref, gt, [(q0, 8), (q1, 8)], arrive)
    own.start()
    ref = gt.at[z, c]
    pair = [net.send(t_ref, ref, net.at(flip=True))]

    def hand_over(s):
        for d in (1, -1):
            for p in (0, 1):
                up[p, d, s].wait_recv()
            if s < 4:
                ref = gt.at[(z - d * s + 8) % 8, c]
                pair.append(net.send(ref, ref, net.at(flip=True)))
        if s == 4:
            ref = gt.at[(z + 4) % 8, c]
            pair.append(net.send(ref, ref, net.at(flip=True)))

    for s in range(1, 5):
        ring.step(s)
        small.step(s)
        if s > 1:
            hand_over(s - 1)
    for copy in row:
        copy.wait_recv()
    small_pair = small.pair()
    hand_over(4)
    for copy in pair:
        copy.wait_recv()
    small_pair.wait_recv()
    own.wait()
    net.drain()


def spread(template, route):
    return comm_call(
        spread_body,
        [((8, 2, 32, SIDE, SIDE), jnp.bfloat16), ((2, 8, 8, 128), jnp.int32), ((4, 8, 128), jnp.int32)],
        "avv", [], 56, 1, "spread", "vv", 16,
    )(template, route)


def gather_column(net, own_ref, out, own_copy):
    ref = out.at[net.z, net.c]
    pair = [net.send(own_ref, ref, net.at(flip=True))]
    size = own_ref.shape[0] // 2

    def arrive(p, d, s, zs, part):
        if s == 4:
            return
        ref = out.at[zs, net.c, part]
        pair.append(net.send(ref, ref, net.at(flip=True)))

    ring = ZRing(net, own_ref, out, [(0, size), (size, size)], arrive)
    own_copy.start()

    def last():
        ref = out.at[(net.z + 4) % 8, net.c]
        pair.append(net.send(ref, ref, net.at(flip=True)))
        for copy in pair:
            copy.wait_recv()
        own_copy.wait()

    return ring, last


def fetch_body(sel, v_ref, xf, gv, relay, ssem, rsem, lsem):
    net = Net(ssem, rsem)
    net.meet([net.at(dz=1), net.at(dz=-1), net.at(dx=1), net.at(dx=-1), net.at(flip=True)])

    def src(k, half):
        part = pl.ds(0, 16) if half is None else pl.ds(8 * half, 8)
        return sel.at[(net.x + k + 4) % 4, part]

    def dst(slot, half):
        return xf.at[slot] if half is None else xf.at[slot, pl.ds(8 * half, 8)]

    side = Ring4(net, "dx", src, dst, lambda i: relay.at[i])
    own = pltpu.make_async_copy(v_ref, gv.at[net.z, net.c], lsem.at[0])
    ring, last = gather_column(net, v_ref, gv, own)
    side.pass_on()
    for s in range(1, 5):
        ring.step(s)
    side.finish()
    last()
    net.drain()


def fetch(sel, svar):
    return comm_call(
        fetch_body,
        [((3, 16, SIDE, SIDE), jnp.bfloat16), ((8, 2, 16, SIDE, SIDE), jnp.bfloat16)],
        "aa", [pltpu.VMEM((2, 8, SIDE, SIDE), jnp.bfloat16)], 40, 2, "fetch", "vv", 16,
    )(sel, svar)


def reduce_scratch():
    def buf(*shape):
        return pltpu.VMEM(shape + (SIDE, SIDE), jnp.bfloat16)

    return [buf(3, 16), buf(3, 4, 4), buf(2, 8), buf(2, 2, 4), buf(16), buf(4, 4),
            buf(3, 4), buf(3, 4), buf(2, 2), buf(2, 2)]


class Reduce:
    def __init__(self, net, part, bufs):
        (self.a0, self.b0, ra, rb, self.ha, self.hb, self.a1, self.b1, self.ra1, self.rb1) = bufs
        self.net, self.part = net, part
        x, y = net.x, net.y

        def src_a(k, half):
            return part.at[(x + k + 4) % 4, pl.ds(0, 16) if half is None else pl.ds(8 * half, 8)]

        def dst_a(slot, half):
            return self.a0.at[slot] if half is None else self.a0.at[slot, pl.ds(8 * half, 8)]

        def src_b(k, half):
            rows = pl.ds(16 + 4 * ((y + k + 4) % 4), 4)
            return part.at[pl.ds(0, 4) if half is None else pl.ds(2 * half, 2), rows]

        def dst_b(slot, half):
            return self.b0.at[slot] if half is None else self.b0.at[slot, pl.ds(2 * half, 2)]

        self.one = [Ring4(net, "dx", src_a, dst_a, lambda i: ra.at[i]),
                    Ring4(net, "dy", src_b, dst_b, lambda i: rb.at[i])]

    def pass_one(self):
        for ring in self.one:
            ring.pass_on()

    def stage_two(self):
        net = self.net
        x, y = net.x, net.y
        for ring in self.one:
            ring.finish()
        f32 = jnp.float32

        def add_a(i, _):
            total = self.part[x, i].astype(f32)
            for slot in range(3):
                total = total + self.a0[slot, i].astype(f32)
            self.ha[i] = total.astype(jnp.bfloat16)
            return 0

        def add_b(i, _):
            p, q = i // 4, i % 4
            total = self.part[p, 16 + 4 * y + q].astype(f32)
            for slot in range(3):
                total = total + self.b0[slot, p, q].astype(f32)
            self.hb[p, q] = total.astype(jnp.bfloat16)
            return 0

        lax.fori_loop(0, 16, add_a, 0)
        lax.fori_loop(0, 16, add_b, 0)

        def src_a(k, half):
            base = 4 * ((y + k + 4) % 4)
            return self.ha.at[pl.ds(base, 4) if half is None else pl.ds(base + 2 * half, 2)]

        def dst_a(slot, half):
            return self.a1.at[slot] if half is None else self.a1.at[slot, pl.ds(2 * half, 2)]

        def src_b(k, half):
            return self.hb.at[(x + k + 4) % 4, pl.ds(0, 4) if half is None else pl.ds(2 * half, 2)]

        def dst_b(slot, half):
            return self.b1.at[slot] if half is None else self.b1.at[slot, pl.ds(2 * half, 2)]

        self.two = [Ring4(net, "dy", src_a, dst_a, lambda i: self.ra1.at[i]),
                    Ring4(net, "dx", src_b, dst_b, lambda i: self.rb1.at[i])]

    def pass_two(self):
        for ring in self.two:
            ring.pass_on()

    def finish(self):
        for ring in self.two:
            ring.finish()

    def total(self, h, i):
        f32 = jnp.float32
        net = self.net
        if h == 0:
            own, got = self.ha[4 * net.y + i], self.a1
        else:
            own, got = self.hb[net.x, i], self.b1
        total = own.astype(f32)
        for slot in range(3):
            total = total + got[slot, i].astype(f32)
        return total


def mid_body(d_ref, k_ref, part, gd, gk, vsum, *rest):
    bufs, (ssem, rsem, lsem) = rest[:10], rest[10:]
    net = Net(ssem, rsem)
    net.meet([net.at(dz=1), net.at(dz=-1), net.at(dx=1), net.at(dx=-1),
              net.at(dy=1), net.at(dy=-1), net.at(flip=True)])
    small = SmallRing(net, k_ref, gk)
    own = pltpu.make_async_copy(d_ref, gd.at[net.z, net.c], lsem.at[0])
    ring, last = gather_column(net, d_ref, gd, own)
    red = Reduce(net, part, bufs)
    red.pass_one()
    ring.step(1)
    small.step(1)
    ring.step(2)
    small.step(2)
    red.stage_two()
    red.pass_two()
    ring.step(3)
    small.step(3)
    red.finish()

    def put(i, _):
        for h in range(2):
            vsum[4 * h + i] = red.total(h, i)
        return 0

    lax.fori_loop(0, 4, put, 0)
    ring.step(4)
    small.step(4)
    pair = small.pair()
    last()
    pair.wait_recv()
    net.drain()


def mid(diff, squares, part):
    return comm_call(
        mid_body,
        [((8, 2, 16, SIDE, SIDE), jnp.bfloat16), ((2, 8, 8, 128), jnp.float32), ((8, SIDE, SIDE), jnp.float32)],
        "avv", reduce_scratch(), 72, 3, "mid", "vvv", 32,
    )(diff, squares, part)


def end_body(part, kpart, vsum, tvar, gs, kx, ky, kown, *rest):
    bufs, (ssem, rsem, lsem) = rest[:10], rest[10:]
    net = Net(ssem, rsem)
    x, y = net.x, net.y
    f32 = jnp.float32
    net.meet([net.at(dx=1), net.at(dx=-1), net.at(dx=2), net.at(dy=1), net.at(dy=-1), net.at(dy=2)])
    kxs = [net.send(kpart.at[(x + k + 4) % 4], kx.at[i], net.at(dx=k)) for i, k in enumerate((1, -1, 2))]
    red = Reduce(net, part, bufs)
    red.pass_one()
    for copy in kxs:
        copy.wait_recv()
    kown[...] = kpart[x] + kx[0] + kx[1] + kx[2]
    kys = [net.send(kown, ky.at[i], net.at(dy=k)) for i, k in enumerate((1, -1, 2))]
    red.stage_two()
    red.pass_two()
    for copy in kys:
        copy.wait_recv()
    ksum = kown[0:1, :] + ky[0, 0:1, :] + ky[1, 0:1, :] + ky[2, 0:1, :]
    red.finish()
    lane = lax.broadcasted_iota(jnp.int32, (1, 128), 1)

    def put(i, _):
        for h in range(2):
            ks = jnp.sum(jnp.where(lane == 16 * h + 4 * y + i, ksum, 0.0), axis=1, keepdims=True)
            var = vsum[4 * h + i] + ks * tvar[4 * h + i].astype(f32)
            sig = red.total(h, i) / jnp.sqrt(jnp.maximum(var, 1.0))
            gs[y, 4 * h + i] = sig.astype(jnp.bfloat16)
        return 0

    lax.fori_loop(0, 4, put, 0)
    mine = gs.at[y]
    up, down = net.at(dy=1), net.at(dy=-1)
    a = net.send(mine, mine, up)
    b = net.send(mine, mine, down)
    a.wait_recv()
    ref = gs.at[(y + 3) % 4, pl.ds(0, 4)]
    a2 = net.send(ref, ref, up)
    b.wait_recv()
    ref = gs.at[(y + 1) % 4, pl.ds(4, 4)]
    b2 = net.send(ref, ref, down)
    a2.wait_recv()
    b2.wait_recv()
    net.drain()


def end(part, kpart, vsum, tvar):
    tile = pltpu.VMEM((3, 8, 128), jnp.float32)
    return comm_call(
        end_body,
        [((4, 8, SIDE, SIDE), jnp.bfloat16)],
        "v", [tile, tile, pltpu.VMEM((8, 128), jnp.float32)] + reduce_scratch(), 40, 4, "end", "vvvv", 32,
    )(part, kpart, vsum, tvar)[0]


def segment_body(target, raw, out, acc):
    g = pl.program_id(0)

    @pl.when(g == 0)
    def _():
        def clear(i, _):
            acc[i] = jnp.zeros((SIDE, SIDE), jnp.float32)
            return 0
        lax.fori_loop(0, 128, clear, 0)

    def add(i, _):
        t = target[g * 16 + i]

        @pl.when(t >= 0)
        def _():
            acc[t] = acc[t] + raw[i].astype(jnp.float32)
        return 0

    lax.fori_loop(0, 16, add, 0)

    @pl.when(g == 15)
    def _():
        def put(i, _):
            out[i] = acc[i].astype(jnp.bfloat16)
            return 0
        lax.fori_loop(0, 128, put, 0)


def segment(target, raw):
    return pl.pallas_call(
        segment_body,
        out_shape=jax.ShapeDtypeStruct((128, SIDE, SIDE), jnp.bfloat16),
        grid_spec=pltpu.PrefetchScalarGridSpec(
            num_scalar_prefetch=1, grid=(16,),
            in_specs=[pl.BlockSpec((16, SIDE, SIDE), lambda g, t: (g, 0, 0))],
            out_specs=pl.BlockSpec((128, SIDE, SIDE), lambda g, t: (0, 0, 0)),
            scratch_shapes=[pltpu.VMEM((128, SIDE, SIDE), jnp.float32)]),
        compiler_params=pltpu.CompilerParams(vmem_limit_bytes=40 << 20),
        name="segment",
    )(target, raw.reshape(256, SIDE, SIDE))


def local(
    template,
    template_var,
    science,
    science_var,
    routes_src,
    routes_blk,
    stamp_rows,
    stamp_cols,
    basis_col,
    basis_row,
    psf_col,
    psf_row,
):
    bf16, f32 = jnp.bfloat16, jnp.float32
    z, x, c, y = (lax.axis_index(a) for a in ("z", "x", "core", "y"))
    route = routes_src[0] * 32 + routes_blk[0]
    route = jnp.broadcast_to(jnp.pad(route, (0, 112))[None], (8, 128))
    gt, rz, rx = spread(template, route)
    wants = rx[:, 0, :16].reshape(64)
    owner = wants // 32
    here = (owner // 2) % 4 == x
    slot = (owner // 8) * 64 + (owner % 2) * 32 + wants % 32
    sel = gt.reshape(512, SIDE, SIDE)[jnp.where(here, slot, 0)]
    sel = jnp.where(here[:, None, None], sel, jnp.zeros((), bf16)).reshape(4, 16, SIDE, SIDE)
    xf, gv = fetch(sel, to_blocks(science_var[0], SIDE))
    frame = lax.dynamic_index_in_dim(sel, x, 0, keepdims=False) + xf[0] + xf[1] + xf[2]
    fp = jnp.pad(to_image(frame, 2, 8).astype(f32), ((10, 30), (10, 246)))
    coef, diff, ks2 = fit_call(
        stamp_rows[0], stamp_cols[0], fp, science[0], science_var[0], *bands(basis_col, basis_row)
    )
    goes = rz[:, :, 0, :16].transpose(1, 0, 2).reshape(256)
    owner = goes // 32
    ours = (owner // 8 == z) & (owner % 2 == c)
    target = jnp.where(ours, ((owner // 2) % 4) * 32 + goes % 32, -1)
    gd, gk, vsum = mid(diff, ks2, segment(target, gv).reshape(4, 32, SIDE, SIDE))
    part = segment(target, gd).reshape(4, 32, SIDE, SIDE)
    squares = jnp.repeat(gk[:, :, 0, 0].T.reshape(16), 16)
    kpart = jnp.sum(jnp.where(target[None, :] == jnp.arange(128)[:, None], squares[None, :], 0.0), axis=1)
    kpart = jnp.broadcast_to(jnp.pad(kpart.reshape(4, 1, 32), ((0, 0), (0, 0), (0, 96))), (4, 8, 128))
    tvar = jnp.concatenate(
        [lax.dynamic_slice_in_dim(template_var, 16 * h + 4 * y, 4, 0) for h in range(2)]
    )
    gs = end(part, kpart, vsum, tvar)
    scored = correlate_psf(to_image(diff, 2, 8), psf_col[0], psf_row[0], SIDE)
    significance = gs.reshape(4, 2, 4, SIDE, SIDE).transpose(1, 0, 2, 3, 4).reshape(32, SIDE, SIDE)
    return (significance.astype(f32), scored[None], coef[:1, :41])


def solution(mesh):
    fine = Mesh(mesh.devices.reshape(8, 4, 2, 4), ("z", "x", "core", "y"))
    det = ("z", "x", "core")
    placed = (
        P(det, None, None),
        P(det, None, None),
        P("y", det, None),
        P("y", det, None),
        P("y", det),
        P("y", det),
        P("y", det),
        P("y", det),
        P(),
        P(),
        P("y", None),
        P("y", None),
    )
    return jax.shard_map(
        local,
        mesh=fine,
        in_specs=placed,
        out_specs=(P(det, None, None), P("y", det, None), P("y", det)),
        check_vma=False,
    )
```

```python
import jax, jax.numpy as jnp
from jax import lax
from jax.experimental import pallas as pl
from jax.experimental.pallas import tpu as pltpu

from jax.sharding import Mesh, PartitionSpec as P

HI = lax.Precision.HIGHEST
precise_mode = HI
RS = 520

def fit_body(rows_s, cols_s, fp_ref, sci_ref, var_ref, cb_ref, rb_ref, bc_ref, br_ref,
             coef_ref, diff_ref, img_ref, ks_ref,
             sci32, var32, stk, dsg, sst, wst, wb, fs, conv, f128, rows32):
    f32, bf16 = jnp.float32, jnp.bfloat16
    sci32[:256, :1024] = sci_ref[...].astype(f32)
    var32[:256, :1024] = var_ref[...].astype(f32)
    for s in range(4):
        y0 = rows_s[s]
        x0 = cols_s[s]
        xa = pl.multiple_of((x0 // 128) * 128, 128)
        rem = x0 - xa
        ya = pl.multiple_of((y0 // 8) * 8, 8)
        ry = y0 - ya
        t = pltpu.roll(fp_ref[pl.ds(ya, 168), pl.ds(xa, 384)], 168 - ry, 0)[:160]
        t = pltpu.roll(t, 384 - rem, 1)[:, :256]
        stk[:, s * 256:(s + 1) * 256] = t.astype(bf16)
        c = pltpu.roll(sci32[pl.ds(ya, 136), pl.ds(xa, 256)], 136 - ry, 0)[:128]
        sst[s * 128:(s + 1) * 128, :] = pltpu.roll(c, 256 - rem, 1)[:, :128]
        v = pltpu.roll(var32[pl.ds(ya, 136), pl.ds(xa, 256)], 136 - ry, 0)[:128]
        wst[s * 128:(s + 1) * 128, :] = 1.0 / pltpu.roll(v, 256 - rem, 1)[:, :128]

    def per_basis(k, _):
        cb = jnp.broadcast_to(cb_ref[k][0:1], (128, 256))
        cb = pltpu.roll(cb, 0, 1, stride=1, stride_axis=0)[:, :160].astype(bf16)
        rb = jnp.broadcast_to(rb_ref[k][0:1], (256, 256))
        rb = pltpu.roll(rb, 0, 1, stride=1, stride_axis=0)[:, :128].astype(bf16)
        a = jnp.dot(cb, stk[...], preferred_element_type=f32).astype(bf16)
        for s in range(4):
            d = jnp.dot(a[:, s * 256:(s + 1) * 256], rb, preferred_element_type=f32)
            dsg[pl.ds(pl.multiple_of(k * RS + s * 128, 8), 128), :] = d
        return 0
    lax.fori_loop(0, 40, per_basis, 0)

    sub = lax.broadcasted_iota(jnp.int32, (8, 128), 0)

    def per_rows(g, acc):
        xs, ys = [], []
        for q in range(8):
            r = g * 8 + q
            x = dsg[pl.ds(r, 40, stride=RS), :]
            srow = jnp.broadcast_to(sst[pl.ds(r, 1), :], (8, 128))
            extra = jnp.where(sub == 0, 1.0, jnp.where(sub == 1, srow, 0.0))
            x = jnp.concatenate([x, extra], axis=0)
            w = jnp.broadcast_to(wst[pl.ds(r, 1), :], (48, 128))
            xs.append(x)
            ys.append(x * w)
        x = jnp.concatenate(xs, axis=1)
        y = jnp.concatenate(ys, axis=1)
        xh = x.astype(bf16)
        xl = (x - xh.astype(f32)).astype(bf16)
        yh = y.astype(bf16)
        yl = (y - yh.astype(f32)).astype(bf16)
        nt = (((1,), (1,)), ((), ()))
        lhs = jnp.concatenate([yh, yh, yl], axis=1)
        rhs = jnp.concatenate([xh, xl, xh], axis=1)
        return acc + lax.dot_general(lhs, rhs, nt, preferred_element_type=f32)
    gram = lax.fori_loop(0, 64, per_rows, jnp.zeros((48, 48), f32))

    ri = lax.broadcasted_iota(jnp.int32, (48, 48), 0)
    ci = lax.broadcasted_iota(jnp.int32, (48, 48), 1)
    m = gram * (1.0 / 65536.0) + jnp.where((ri == ci) & (ri < 41), 0.01, 0.0)
    for n in range(41):
        prow = m[n:n + 1, :]
        pcol = m[:, n:n + 1]
        new = prow / m[n:n + 1, n:n + 1]
        m = jnp.where(ri == n, jnp.broadcast_to(new, (48, 48)), m - pcol * new)
    rcol = lax.broadcasted_iota(jnp.int32, (48, 1), 0)
    col = m[:, 41:42]
    row = jnp.sum(jnp.where(ri == ci, jnp.broadcast_to(col, (48, 48)), 0.0), axis=0, keepdims=True)
    coef_ref[...] = jnp.broadcast_to(jnp.pad(row, ((0, 0), (0, 80))), (8, 128))
    bg = m[40:41, 41:42]
    ccol = jnp.where(rcol < 40, col, 0.0)
    tn = (((0,), (0,)), ((), ()))
    ker = lax.dot_general(bc_ref[...] * ccol, br_ref[...], tn, precision=HI, preferred_element_type=f32)
    ker = ker[:24, :]
    ks = jnp.sum(ker, keepdims=True)
    ks_ref[...] = jnp.broadcast_to(ks * ks, (8, 128))
    wb[0, :, 128:] = jnp.zeros((256, 128), bf16)
    wb[21, :, :128] = jnp.zeros((256, 128), bf16)
    for dy in range(21):
        base = jnp.broadcast_to(ker[dy:dy + 1, :], (256, 256))
        band = pltpu.roll(base, 0, 1, stride=1, stride_axis=0)[:, :128].astype(bf16)
        wb[dy, :, :128] = band
        wb[dy + 1, :, 128:] = band
    for cc in range(9):
        sl = slice(cc * 128, (cc + 1) * 128)
        f128[cc] = fp_ref[:280, sl]
    for cc in range(9):
        sl = slice(cc * 128, (cc + 1) * 128)
        for dy in range(22):
            fs[dy, :, sl] = f128[cc, pl.ds(dy, 128, stride=2), :].astype(bf16)

    def per_col(c, _):
        c0 = pl.multiple_of(c * 128, 128)
        acc = jnp.zeros((128, 256), f32)
        for dy in range(22):
            acc = acc + jnp.dot(fs[dy, :, pl.ds(c0, 256)], wb[dy], preferred_element_type=f32)
        conv[pl.ds(0, 128, stride=2), :] = acc[:, :128]
        conv[pl.ds(1, 128, stride=2), :] = acc[:, 128:]
        for i in range(2):
            d = sci32[i * 128:(i + 1) * 128, pl.ds(c0, 128)] - conv[i * 128:(i + 1) * 128, :] - bg
            rows32[pl.ds(c + 8 * i, 128, stride=16), :] = d
            img_ref[i * 128:(i + 1) * 128, pl.ds(c0, 128)] = d.astype(bf16)
        return 0
    lax.fori_loop(0, 8, per_col, 0)
    diff_ref[...] = rows32[...].reshape(128, 16, 128).astype(bf16)

def fit_call(rows, cols, fp, sci, var, cb, rb, bc, br):
    f32, bf16 = jnp.float32, jnp.bfloat16
    sm = pl.BlockSpec(memory_space=pltpu.SMEM)
    vm = pl.BlockSpec(memory_space=pltpu.VMEM)
    return pl.pallas_call(
        fit_body,
        out_shape=(jax.ShapeDtypeStruct((8, 128), f32), jax.ShapeDtypeStruct((128, 16, 128), bf16),
                   jax.ShapeDtypeStruct((256, 1024), bf16),
                   jax.ShapeDtypeStruct((8, 128), f32)),
        in_specs=[sm, sm] + [vm] * 7,
        out_specs=(vm, vm, vm, vm),
        scratch_shapes=[
            pltpu.VMEM((264, 1152), f32), pltpu.VMEM((264, 1152), f32),
            pltpu.VMEM((160, 1024), bf16), pltpu.VMEM((40 * RS, 128), f32),
            pltpu.VMEM((512, 128), f32), pltpu.VMEM((512, 128), f32),
            pltpu.VMEM((22, 256, 256), bf16), pltpu.VMEM((22, 128, 1152), bf16),
            pltpu.VMEM((256, 128), f32), pltpu.VMEM((9, 280, 128), f32),
            pltpu.VMEM((2048, 128), f32)],
        compiler_params=pltpu.CompilerParams(vmem_limit_bytes=60 * 1024 * 1024),
        name="fit",
    )(rows, cols, fp, sci, var, cb, rb, bc, br)

def bands(basis_col, basis_row):
    col = jnp.pad(basis_col.astype(jnp.float32), ((0, 8), (0, 235)))
    row = jnp.pad(basis_row.astype(jnp.float32), ((0, 8), (0, 0)))
    rev = jnp.concatenate([row[:, :1], jnp.zeros((48, 235), jnp.float32), row[:, :0:-1]], axis=1)
    cb = jnp.broadcast_to(col[:40, None, :], (40, 8, 256))
    rb = jnp.broadcast_to(rev[:40, None, :], (40, 8, 256))
    return cb, rb, col[:, :128], rev


def pick_body(where_s, gt, out, sems):
    def copy(i):
        return pltpu.make_async_copy(gt.at[where_s[i]], out.at[i], sems.at[i])

    def begin(i, _):
        @pl.when(where_s[i] >= 0)
        def _():
            copy(i).start()

        @pl.when(where_s[i] < 0)
        def _():
            out[i] = jnp.zeros((128, 128), jnp.bfloat16)
        return 0

    def done(i, _):
        @pl.when(where_s[i] >= 0)
        def _():
            copy(i).wait()
        return 0

    lax.fori_loop(0, 64, begin, 0)
    lax.fori_loop(0, 64, done, 0)


def pick(where_at, gt):
    return pl.pallas_call(
        pick_body,
        out_shape=jax.ShapeDtypeStruct((64, 128, 128), jnp.bfloat16),
        in_specs=[pl.BlockSpec(memory_space=pltpu.SMEM), pl.BlockSpec(memory_space=pl.ANY)],
        out_specs=pl.BlockSpec(memory_space=pltpu.VMEM),
        scratch_shapes=[pltpu.SemaphoreType.DMA((64,))],
        compiler_params=pltpu.CompilerParams(vmem_limit_bytes=8 << 20),
        name="pick",
    )(where_at, gt)


def band_stack(filters, block_side):
    kernel_taps = filters.shape[1]
    inputs = jnp.arange(block_side + kernel_taps - 1)[:, None, None]
    outputs = jnp.arange(block_side)[None, :, None]
    offsets = jnp.arange(kernel_taps)[None, None, :]
    select = (inputs - outputs == offsets).astype(jnp.float32)
    return jnp.einsum("ni,rvi->nrv", filters.astype(jnp.float32), select, precision=precise_mode)


def column_windows(padded, block_side, kernel_taps):
    height_all, padded_span = padded.shape
    count_blocks = (padded_span - kernel_taps + 1) // block_side
    extended = jnp.pad(padded, ((0, 0), (0, (count_blocks + 1) * block_side - padded_span)))
    tiled_rows = extended.reshape(height_all, count_blocks + 1, block_side)
    return jnp.concatenate(
        [tiled_rows[:, :count_blocks], tiled_rows[:, 1:, : kernel_taps - 1]], axis=2
    )


def row_windows(padded, block_side, kernel_taps):
    padded_span, across = padded.shape
    count_blocks = (padded_span - kernel_taps + 1) // block_side
    extended = jnp.pad(padded, ((0, (count_blocks + 1) * block_side - padded_span), (0, 0)))
    tiled_rows = extended.reshape(count_blocks + 1, block_side, across)
    return jnp.concatenate([tiled_rows[:count_blocks], tiled_rows[1:, : kernel_taps - 1]], axis=1)


def to_image(blocks, block_rows, block_cols):
    block_side = blocks.shape[-1]
    shaped = blocks.reshape(block_rows, block_cols, block_side, block_side).transpose(0, 2, 1, 3)
    return shaped.reshape(block_rows * block_side, block_cols * block_side)


def to_blocks(picture, block_side):
    height_all, across = picture.shape
    shaped = picture.reshape(height_all // block_side, block_side, across // block_side, block_side)
    return shaped.transpose(0, 2, 1, 3).reshape(-1, block_side, block_side)


def correlate_psf(difference, psf_down, psf_across, block_side):
    kernel_taps = psf_down.shape[0]
    margin = kernel_taps // 2
    height_all, across = difference.shape
    data = difference.astype(jnp.float32)
    across_band = band_stack(psf_across[None, :], block_side)[0]
    windows = column_windows(jnp.pad(data, ((0, 0), (margin, margin))), block_side, kernel_taps)
    sideways = jnp.einsum("ycr,rv->ycv", windows, across_band, precision=precise_mode).reshape(
        height_all, across
    )
    down_band = band_stack(psf_down[None, :], block_side)[0]
    stacked = row_windows(jnp.pad(sideways, ((margin, margin), (0, 0))), block_side, kernel_taps)
    return jnp.einsum("brw,ru->buw", stacked, down_band, precision=precise_mode).reshape(
        height_all, across
    )


MESH_ID = pl.DeviceIdType.MESH
SIDE = 128


class Net:
    def __init__(self, ssem, rsem):
        self.ssem, self.rsem, self.sent = ssem, rsem, []
        self.z, self.x, self.c, self.y = (lax.axis_index(a) for a in ("z", "x", "core", "y"))

    def at(self, dz=0, dx=0, dy=0, flip=False):
        c = 1 - self.c if flip else self.c
        return ((self.z + dz + 8) % 8, (self.x + dx + 4) % 4, c, (self.y + dy + 4) % 4)

    def meet(self, peers):
        barrier = pltpu.get_barrier_semaphore()
        for peer in peers:
            pl.semaphore_signal(barrier, inc=1, device_id=peer, device_id_type=MESH_ID)
        pl.semaphore_wait(barrier, len(peers))

    def send(self, src, dst, peer):
        i = len(self.sent)
        copy = pltpu.make_async_remote_copy(
            src_ref=src, dst_ref=dst, send_sem=self.ssem.at[i], recv_sem=self.rsem.at[i],
            device_id=peer, device_id_type=MESH_ID,
        )
        copy.start()
        self.sent.append(copy)
        return copy

    def drain(self):
        for copy in self.sent:
            copy.wait_send()


class ZRing:
    def __init__(self, net, own, out, pieces, arrive):
        self.net, self.out, self.pieces, self.arrive = net, out, pieces, arrive
        self.got = {}
        for p, (start, size) in enumerate(pieces):
            for d in (1, -1):
                self.got[d, 1, p] = net.send(
                    own.at[pl.ds(start, size)], out.at[net.z, net.c, pl.ds(start, size)], net.at(dz=d)
                )

    def part(self, p, d, s):
        start, size = self.pieces[p]
        if s < 4:
            return pl.ds(start, size)
        return pl.ds(start + (0 if d == 1 else size // 2), size // 2)

    def step(self, s):
        net = self.net
        for p in range(len(self.pieces)):
            for d in (1, -1):
                self.got[d, s, p].wait_recv()
                zs = (net.z - d * s + 8) % 8
                if s < 4:
                    ref = self.out.at[zs, net.c, self.part(p, d, s + 1)]
                    self.got[d, s + 1, p] = net.send(ref, ref, net.at(dz=d))
                self.arrive(p, d, s, zs, self.part(p, d, s))


class SmallRing:
    def __init__(self, net, own, out):
        self.net, self.out = net, out
        out[net.c, net.z] = own[...]
        self.got = {(d, 1): net.send(own, out.at[net.c, net.z], net.at(dz=d)) for d in (1, -1)}

    def step(self, s):
        net = self.net
        for d in (1, -1):
            if (d, s) not in self.got:
                continue
            self.got[d, s].wait_recv()
            zs = (net.z - d * s + 8) % 8
            if s + 1 <= (4 if d == 1 else 3):
                ref = self.out.at[net.c, zs]
                self.got[d, s + 1] = net.send(ref, ref, net.at(dz=d))

    def pair(self):
        ref = self.out.at[self.net.c]
        return self.net.send(ref, ref, self.net.at(flip=True))


class Ring4:
    def __init__(self, net, axis, src, dst, relay):
        self.net, self.dst, self.relay = net, dst, relay
        self.up = net.at(**{axis: 1})
        self.down = net.at(**{axis: -1})
        self.fa = net.send(src(2, 0), relay(0), self.up)
        self.fb = net.send(src(2, 1), relay(1), self.down)
        self.na = net.send(src(1, None), dst(0, None), self.up)
        self.nb = net.send(src(-1, None), dst(1, None), self.down)

    def pass_on(self):
        self.fa.wait_recv()
        self.ra = self.net.send(self.relay(0), self.dst(2, 0), self.up)
        self.fb.wait_recv()
        self.rb = self.net.send(self.relay(1), self.dst(2, 1), self.down)

    def finish(self):
        for copy in (self.na, self.nb, self.ra, self.rb):
            copy.wait_recv()


def comm_call(body, outs, spaces, scratch, copies, ident, name, in_spaces, side_bytes):
    def spec(space):
        return pl.BlockSpec(memory_space=pltpu.VMEM if space == "v" else pl.ANY)

    return pl.pallas_call(
        body,
        out_shape=tuple(jax.ShapeDtypeStruct(s, d) for s, d in outs),
        in_specs=[spec(s) for s in in_spaces],
        out_specs=tuple(spec(s) for s in spaces),
        scratch_shapes=list(scratch)
        + [pltpu.SemaphoreType.DMA((copies,)), pltpu.SemaphoreType.DMA((copies,)), pltpu.SemaphoreType.DMA((2,))],
        compiler_params=pltpu.CompilerParams(
            collective_id=ident, has_side_effects=True, vmem_limit_bytes=side_bytes << 20
        ),
        name=name,
    )


def spread_body(t_ref, r_ref, gt, rz, rx, ssem, rsem, lsem):
    net = Net(ssem, rsem)
    z, x, c, y = net.z, net.x, net.c, net.y
    net.meet([net.at(dz=1), net.at(dz=-1), net.at(dy=1), net.at(dy=-1),
              net.at(dx=1), net.at(dx=-1), net.at(dx=2), net.at(flip=True)])
    own = pltpu.make_async_copy(t_ref, gt.at[z, c], lsem.at[0])
    small = SmallRing(net, r_ref, rz)
    rx[x] = r_ref[...]
    row = [net.send(r_ref, rx.at[x], net.at(dx=k)) for k in (1, -1, 2)]
    q0 = y * 8
    q1 = ((y + 1) % 4) * 8
    up = {}

    def arrive(p, d, s, zs, part):
        ref = gt.at[zs, c, part]
        up[p, d, s] = net.send(ref, ref, net.at(dy=1 if p == 0 else -1))

    ring = ZRing(net, t_ref, gt, [(q0, 8), (q1, 8)], arrive)
    own.start()
    ref = gt.at[z, c]
    pair = [net.send(t_ref, ref, net.at(flip=True))]

    def hand_over(s):
        for d in (1, -1):
            for p in (0, 1):
                up[p, d, s].wait_recv()
            if s < 4:
                ref = gt.at[(z - d * s + 8) % 8, c]
                pair.append(net.send(ref, ref, net.at(flip=True)))
        if s == 4:
            ref = gt.at[(z + 4) % 8, c]
            pair.append(net.send(ref, ref, net.at(flip=True)))

    for s in range(1, 5):
        ring.step(s)
        small.step(s)
        if s > 1:
            hand_over(s - 1)
    for copy in row:
        copy.wait_recv()
    small_pair = small.pair()
    hand_over(4)
    for copy in pair:
        copy.wait_recv()
    small_pair.wait_recv()
    own.wait()
    net.drain()


def spread(template, route):
    return comm_call(
        spread_body,
        [((8, 2, 32, SIDE, SIDE), jnp.bfloat16), ((2, 8, 8, 128), jnp.int32), ((4, 8, 128), jnp.int32)],
        "avv", [], 56, 1, "spread", "vv", 16,
    )(template, route)


class Column:
    def __init__(self, net, own, out, base, size, pieces):
        self.net, self.out, self.base, self.size = net, out, base, size
        rows = pl.ds(base, size)
        self.pair = [net.send(own.at[rows], out.at[net.z, net.c, rows], net.at(flip=True))]
        cut = size // pieces
        self.ring = ZRing(net, own, out, [(base + i * cut, cut) for i in range(pieces)], self.arrive)
        self.step = self.ring.step

    def arrive(self, p, d, s, zs, part):
        if s < 4:
            ref = self.out.at[zs, self.net.c, part]
            self.pair.append(self.net.send(ref, ref, self.net.at(flip=True)))

    def last(self):
        ref = self.out.at[(self.net.z + 4) % 8, self.net.c, pl.ds(self.base, self.size)]
        self.pair.append(self.net.send(ref, ref, self.net.at(flip=True)))
        for copy in self.pair:
            copy.wait_recv()


def fetch_body(sel, v_ref, xf, gv, relay, ssem, rsem, lsem):
    net = Net(ssem, rsem)
    net.meet([net.at(dz=1), net.at(dz=-1), net.at(dx=1), net.at(dx=-1), net.at(flip=True)])

    def src(k, half):
        part = pl.ds(0, 16) if half is None else pl.ds(8 * half, 8)
        return sel.at[(net.x + k + 4) % 4, part]

    def dst(slot, half):
        return xf.at[slot] if half is None else xf.at[slot, pl.ds(8 * half, 8)]

    side = Ring4(net, "dx", src, dst, lambda i: relay.at[i])
    own = pltpu.make_async_copy(v_ref, gv.at[net.z, net.c], lsem.at[0])
    ring = Column(net, v_ref, gv, 0, 128, 2)
    own.start()
    side.pass_on()
    for s in range(1, 5):
        ring.step(s)
    side.finish()
    ring.last()
    own.wait()
    net.drain()


def fetch(sel, svar):
    return comm_call(
        fetch_body,
        [((3, 16, SIDE, SIDE), jnp.bfloat16), ((8, 2, SIDE, 16, SIDE), jnp.bfloat16)],
        "aa", [pltpu.VMEM((2, 8, SIDE, SIDE), jnp.bfloat16)], 40, 2, "fetch", "vv", 16,
    )(sel, svar)


def reduce_scratch():
    def buf(*shape):
        return pltpu.VMEM((4,) + shape + (32, SIDE), jnp.bfloat16)

    return [buf(3, 32), buf(3, 8, 4), buf(2, 16), buf(2, 4, 4), buf(32), buf(8, 4),
            buf(3, 8), buf(3, 8), buf(2, 4), buf(2, 4)]


class Reduce:
    def __init__(self, net, part, base, bufs):
        (self.a0, self.b0, ra, rb, self.ha, self.hb, self.a1, self.b1, self.ra1, self.rb1) = bufs
        self.net, self.part, self.base = net, part, base
        x, y = net.x, net.y

        def src_a(k, half):
            rows = pl.ds(base, 32) if half is None else pl.ds(base + 16 * half, 16)
            return part.at[rows, (x + k + 4) % 4]

        def dst_a(slot, half):
            return self.a0.at[slot] if half is None else self.a0.at[slot, pl.ds(16 * half, 16)]

        def src_b(k, half):
            first = base + 32 + 8 * ((y + k + 4) % 4)
            return part.at[pl.ds(first, 8) if half is None else pl.ds(first + 4 * half, 4)]

        def dst_b(slot, half):
            return self.b0.at[slot] if half is None else self.b0.at[slot, pl.ds(4 * half, 4)]

        self.one = [Ring4(net, "dx", src_a, dst_a, lambda i: ra.at[i]),
                    Ring4(net, "dy", src_b, dst_b, lambda i: rb.at[i])]

    def pass_one(self):
        for ring in self.one:
            ring.pass_on()

    def stage_two(self):
        net = self.net
        x, y = net.x, net.y
        for ring in self.one:
            ring.finish()
        f32 = jnp.float32

        def add_a(i, _):
            total = self.part[self.base + i, x].astype(f32)
            for slot in range(3):
                total = total + self.a0[slot, i].astype(f32)
            self.ha[i] = total.astype(jnp.bfloat16)
            return 0

        def add_b(i, _):
            total = self.part[self.base + 32 + 8 * y + i].astype(f32)
            for slot in range(3):
                total = total + self.b0[slot, i].astype(f32)
            self.hb[i] = total.astype(jnp.bfloat16)
            return 0

        lax.fori_loop(0, 32, add_a, 0)
        lax.fori_loop(0, 8, add_b, 0)

        def src_a(k, half):
            first = 8 * ((y + k + 4) % 4)
            return self.ha.at[pl.ds(first, 8) if half is None else pl.ds(first + 4 * half, 4)]

        def dst_a(slot, half):
            return self.a1.at[slot] if half is None else self.a1.at[slot, pl.ds(4 * half, 4)]

        def src_b(k, half):
            return self.hb.at[pl.ds(0, 8) if half is None else pl.ds(4 * half, 4), (x + k + 4) % 4]

        def dst_b(slot, half):
            return self.b1.at[slot] if half is None else self.b1.at[slot, pl.ds(4 * half, 4)]

        self.two = [Ring4(net, "dy", src_a, dst_a, lambda i: self.ra1.at[i]),
                    Ring4(net, "dx", src_b, dst_b, lambda i: self.rb1.at[i])]

    def pass_two(self):
        for ring in self.two:
            ring.pass_on()

    def finish(self):
        for ring in self.two:
            ring.finish()

    def total(self, h, i):
        f32 = jnp.float32
        if h == 0:
            own, got = self.ha[8 * self.net.y + i], self.a1
        else:
            own, got = self.hb[i, self.net.x], self.b1
        total = own.astype(f32)
        for slot in range(3):
            total = total + got[slot, i].astype(f32)
        return total


def tail_body(dp, ks, hot, count, tq, gv, gs, gd, gk, vv, vpart, dpart, kx, ky, kown, kall, *rest):
    bufs, (ssem, rsem, lsem) = rest[:10], rest[10:]
    net = Net(ssem, rsem)
    x, y = net.x, net.y
    f32, bf16 = jnp.float32, jnp.bfloat16
    fetch_v = pltpu.make_async_copy(gv, vv, lsem.at[0])
    fetch_v.start()
    net.meet([net.at(dz=1), net.at(dz=-1), net.at(dx=1), net.at(dx=-1), net.at(dx=2),
              net.at(dy=1), net.at(dy=-1), net.at(dy=2), net.at(flip=True)])
    own = pltpu.make_async_copy(dp, gd.at[net.z, net.c], lsem.at[1])
    first = Column(net, dp, gd, 0, 64, 2)
    own.start()
    small = SmallRing(net, ks, gk)
    fetch_v.wait()

    def sums(column, part, base):
        def one(i, _):
            for u in range(2):
                p = base + 2 * i + u
                got = jnp.dot(hot[...], column[:, :, p].reshape(256, SIDE), preferred_element_type=f32)
                part[p] = got.astype(bf16).reshape(4, 32, SIDE)
            return 0

        lax.fori_loop(0, 32, one, 0)

    def reduce(part, base, g):
        return Reduce(net, part, base, [b.at[g] for b in bufs])

    sums(vv, vpart, 0)
    v0 = reduce(vpart, 0, 0)
    sums(vv, vpart, 64)
    v1 = reduce(vpart, 64, 1)
    first.step(1)
    small.step(1)
    first.step(2)
    small.step(2)
    v0.pass_one()
    v1.pass_one()
    second = Column(net, dp, gd, 64, 64, 2)
    first.step(3)
    small.step(3)
    first.step(4)
    small.step(4)
    pair = small.pair()
    own.wait()
    first.last()
    v0.stage_two()
    v1.stage_two()
    sums(gd, dpart, 0)
    d0 = reduce(dpart, 0, 2)
    second.step(1)
    v0.pass_two()
    v1.pass_two()
    pair.wait_recv()
    total = gk[0, 0] * count[0]
    for i in range(1, 16):
        total = total + gk[i % 2, i // 2] * count[i]
    kown[...] = total
    kxs = [net.send(kown, kx.at[i], net.at(dx=k)) for i, k in enumerate((1, -1, 2))]
    second.step(2)
    d0.pass_one()
    for copy in kxs:
        copy.wait_recv()
    kall[...] = kown[...] + kx[0] + kx[1] + kx[2]
    kys = [net.send(kall, ky.at[i], net.at(dy=k)) for i, k in enumerate((1, -1, 2))]
    second.step(3)
    second.step(4)
    second.last()
    sums(gd, dpart, 64)
    d1 = reduce(dpart, 64, 3)
    d0.stage_two()
    for copy in kys:
        copy.wait_recv()
    ksum = kall[0:1, :] + ky[0, 0:1, :] + ky[1, 0:1, :] + ky[2, 0:1, :]
    lane = lax.broadcasted_iota(jnp.int32, (32, SIDE), 1)
    line = lax.broadcasted_iota(jnp.int32, (32, SIDE), 0)
    kcol = jnp.sum(jnp.where(lane == x * 32 + line, jnp.broadcast_to(ksum, (32, SIDE)), 0.0), axis=1, keepdims=True)
    up, down = net.at(dy=1), net.at(dy=-1)
    v0.finish()
    v1.finish()
    d1.pass_one()
    d0.pass_two()

    def settle(diff, var, g):
        def put(i, _):
            for h in range(2):
                v = var.total(h, i) + kcol * tq[g, h, i].astype(f32)
                gs[g, y, h, i] = (diff.total(h, i) / jnp.sqrt(jnp.maximum(v, 1.0))).astype(bf16)
            return 0

        lax.fori_loop(0, 8, put, 0)
        mine = gs.at[g, y]
        return net.send(mine, mine, up), net.send(mine, mine, down)

    def relay(pair_of, g):
        a, b = pair_of
        a.wait_recv()
        ref = gs.at[g, (y + 3) % 4, 0]
        a2 = net.send(ref, ref, up)
        b.wait_recv()
        ref = gs.at[g, (y + 1) % 4, 1]
        return a2, net.send(ref, ref, down)

    d0.finish()
    out0 = settle(d0, v0, 0)
    d1.stage_two()
    d1.pass_two()
    far0 = relay(out0, 0)
    d1.finish()
    out1 = settle(d1, v1, 1)
    far1 = relay(out1, 1)
    for copy in far0 + far1:
        copy.wait_recv()
    net.drain()


def tail(diff, squares, hot, count, tq, gv):
    f32, bf16 = jnp.float32, jnp.bfloat16
    tile = pltpu.VMEM((3, 8, 128), f32)
    return comm_call(
        tail_body,
        [((2, 4, 2, 8, 32, SIDE), bf16)],
        "v",
        [pltpu.VMEM((8, 2, SIDE, 16, SIDE), bf16), pltpu.VMEM((2, 8, 8, SIDE), f32),
         pltpu.VMEM((8, 2, SIDE, 16, SIDE), bf16), pltpu.VMEM((SIDE, 4, 32, SIDE), bf16),
         pltpu.VMEM((SIDE, 4, 32, SIDE), bf16), tile, tile, pltpu.VMEM((8, 128), f32), pltpu.VMEM((8, 128), f32)]
        + reduce_scratch(),
        184, 3, "tail", "vvvvva", 52,
    )(diff, squares, hot, count, tq, gv)[0]


def local(
    template,
    template_var,
    science,
    science_var,
    routes_src,
    routes_blk,
    stamp_rows,
    stamp_cols,
    basis_col,
    basis_row,
    psf_col,
    psf_row,
):
    bf16, f32 = jnp.bfloat16, jnp.float32
    z, x, c, y = (lax.axis_index(a) for a in ("z", "x", "core", "y"))
    route = routes_src[0] * 32 + routes_blk[0]
    route = jnp.broadcast_to(jnp.pad(route, (0, 112))[None], (8, 128))
    gt, rz, rx = spread(template, route)
    wants = rx[:, 0, :16].reshape(64)
    owner = wants // 32
    here = (owner // 2) % 4 == x
    slot = (owner // 8) * 64 + (owner % 2) * 32 + wants % 32
    sel = pick(jnp.where(here, slot, -1), gt.reshape(512, SIDE, SIDE)).reshape(4, 16, SIDE, SIDE)
    svar = science_var[0].reshape(2, SIDE, 8, SIDE).transpose(1, 0, 2, 3).reshape(SIDE, 16, SIDE)
    xf, gv = fetch(sel, svar)
    frame = lax.dynamic_index_in_dim(sel, x, 0, keepdims=False) + xf[0] + xf[1] + xf[2]
    fp = jnp.pad(to_image(frame, 2, 8).astype(f32), ((10, 30), (10, 246)))
    coef, diff, image, ks2 = fit_call(
        stamp_rows[0], stamp_cols[0], fp, science[0], science_var[0], *bands(basis_col, basis_row)
    )
    goes = rz[:, :, 0, :16].transpose(1, 0, 2).reshape(256)
    owner = goes // 32
    ours = (owner // 8 == z) & (owner % 2 == c)
    target = jnp.where(ours, ((owner // 2) % 4) * 32 + goes % 32, -1)
    hot = target[None, :] == jnp.arange(SIDE)[:, None]
    count = jnp.sum(hot.reshape(SIDE, 16, 16).astype(f32), axis=2).T
    count = jnp.broadcast_to(count[:, None, :], (16, 8, SIDE))
    tq = lax.dynamic_index_in_dim(template_var.reshape(32, 2, 2, 4, 8, SIDE), y, 3, keepdims=False)
    gs = tail(diff, ks2, hot.astype(bf16), count, tq.transpose(1, 2, 3, 0, 4), gv)
    scored = correlate_psf(image, psf_col[0], psf_row[0], SIDE)
    significance = gs.transpose(4, 0, 2, 1, 3, 5).reshape(32, SIDE, SIDE)
    return (significance.astype(f32), scored[None], coef[:1, :41])


def solution(mesh):
    fine = Mesh(mesh.devices.reshape(8, 4, 2, 4), ("z", "x", "core", "y"))
    det = ("z", "x", "core")
    placed = (
        P(det, None, None),
        P(det, None, None),
        P("y", det, None),
        P("y", det, None),
        P("y", det),
        P("y", det),
        P("y", det),
        P("y", det),
        P(),
        P(),
        P("y", None),
        P("y", None),
    )
    return jax.shard_map(
        local,
        mesh=fine,
        in_specs=placed,
        out_specs=(P(det, None, None), P("y", det, None), P("y", det)),
        check_vma=False,
    )
```

```python
import jax, jax.numpy as jnp
from jax import lax
from jax.experimental import pallas as pl
from jax.experimental.pallas import tpu as pltpu

from jax.sharding import Mesh, PartitionSpec as P

HI = lax.Precision.HIGHEST
precise_mode = HI
RS = 520

def fit_body(rows_s, cols_s, fp_ref, sci_ref, var_ref, cb_ref, rb_ref, bc_ref, br_ref, ps_ref,
             coef_ref, diff_ref, img_ref, ks_ref, hb_ref, vb_ref,
             sci32, var32, stk, dsg, sst, wst, wb, fs, conv, f128, rows32):
    f32, bf16 = jnp.float32, jnp.bfloat16
    sci32[:256, :1024] = sci_ref[...].astype(f32)
    var32[:256, :1024] = var_ref[...].astype(f32)
    for s in range(4):
        y0 = rows_s[s]
        x0 = cols_s[s]
        xa = pl.multiple_of((x0 // 128) * 128, 128)
        rem = x0 - xa
        ya = pl.multiple_of((y0 // 8) * 8, 8)
        ry = y0 - ya
        t = pltpu.roll(fp_ref[pl.ds(ya, 168), pl.ds(xa, 384)], 168 - ry, 0)[:160]
        t = pltpu.roll(t, 384 - rem, 1)[:, :256]
        stk[s * 160:(s + 1) * 160, :] = t.astype(bf16)
        c = pltpu.roll(sci32[pl.ds(ya, 136), pl.ds(xa, 256)], 136 - ry, 0)[:128]
        sst[s * 128:(s + 1) * 128, :] = pltpu.roll(c, 256 - rem, 1)[:, :128]
        v = pltpu.roll(var32[pl.ds(ya, 136), pl.ds(xa, 256)], 136 - ry, 0)[:128]
        wst[s * 128:(s + 1) * 128, :] = jnp.sqrt(1.0 / pltpu.roll(v, 256 - rem, 1)[:, :128])

    def split(band):
        high = band.astype(bf16)
        return high, (band - high.astype(f32)).astype(bf16)

    h0, h1 = split(pltpu.roll(jnp.broadcast_to(ps_ref[0:1, :], (384, 512)), 0, 1, stride=1, stride_axis=0)[:, :128])
    hb_ref[:, :128] = h0
    hb_ref[:, 128:] = h1
    h0, h1 = split(pltpu.roll(jnp.broadcast_to(ps_ref[8:9, :], (256, 512)), 0, 1, stride=1, stride_axis=0)[:, :256])
    vb_ref[:, :256] = h0
    vb_ref[:, 256:512] = h1
    vb_ref[:, 512:] = h0

    def per_basis(k, _):
        cb = jnp.broadcast_to(cb_ref[k][0:1], (128, 256))
        cb = pltpu.roll(cb, 0, 1, stride=1, stride_axis=0)[:, :160].astype(bf16)
        rb = jnp.broadcast_to(rb_ref[k][0:1], (256, 256))
        rb = pltpu.roll(rb, 0, 1, stride=1, stride_axis=0)[:, :128].astype(bf16)
        a = jnp.dot(stk[...], rb, preferred_element_type=f32).astype(bf16)
        a = jnp.concatenate([a[i * 160:(i + 1) * 160] for i in range(4)], axis=1)
        d = jnp.dot(cb, a, preferred_element_type=f32)
        for s in range(4):
            dsg[pl.ds(pl.multiple_of(k * RS + s * 128, 8), 128), :] = d[:, s * 128:(s + 1) * 128]
        return 0
    lax.fori_loop(0, 40, per_basis, 0)

    sub = lax.broadcasted_iota(jnp.int32, (8, 128), 0)

    def per_rows(g, acc):
        xs = []
        for q in range(8):
            r = g * 8 + q
            x = dsg[pl.ds(r, 40, stride=RS), :]
            srow = jnp.broadcast_to(sst[pl.ds(r, 1), :], (8, 128))
            extra = jnp.where(sub == 0, 1.0, jnp.where(sub == 1, srow, 0.0))
            x = jnp.concatenate([x, extra], axis=0)
            xs.append(x * jnp.broadcast_to(wst[pl.ds(r, 1), :], (48, 128)))
        x = jnp.concatenate(xs, axis=1)
        xh = x.astype(bf16)
        xl = (x - xh.astype(f32)).astype(bf16)
        nt = (((1,), (1,)), ((), ()))
        both = lax.dot_general(xh, jnp.concatenate([xh, xl], axis=0), nt, preferred_element_type=f32)
        return acc + both
    both = lax.fori_loop(0, 64, per_rows, jnp.zeros((48, 96), f32))
    both = jnp.concatenate([both, jnp.zeros((48, 32), f32)], axis=1)
    cross = pltpu.roll(both, 80, 1)[:, :48]
    eye = (lax.broadcasted_iota(jnp.int32, (48, 48), 0) == lax.broadcasted_iota(jnp.int32, (48, 48), 1)).astype(f32)
    flip = lax.dot_general(cross, eye, (((0,), (0,)), ((), ())), precision=HI, preferred_element_type=f32)
    gram = both[:, :48] + cross + flip

    ri = lax.broadcasted_iota(jnp.int32, (48, 48), 0)
    ci = lax.broadcasted_iota(jnp.int32, (48, 48), 1)
    m = gram * (1.0 / 65536.0) + jnp.where((ri == ci) & (ri < 41), 0.01, 0.0)
    for n in range(41):
        prow = m[n:n + 1, :]
        pcol = m[:, n:n + 1]
        new = prow / m[n:n + 1, n:n + 1]
        m = jnp.where(ri == n, jnp.broadcast_to(new, (48, 48)), m - pcol * new)
    rcol = lax.broadcasted_iota(jnp.int32, (48, 1), 0)
    col = m[:, 41:42]
    row = jnp.sum(jnp.where(ri == ci, jnp.broadcast_to(col, (48, 48)), 0.0), axis=0, keepdims=True)
    coef_ref[...] = jnp.broadcast_to(jnp.pad(row, ((0, 0), (0, 80))), (8, 128))
    bg = m[40:41, 41:42]
    ccol = jnp.where(rcol < 40, col, 0.0)
    tn = (((0,), (0,)), ((), ()))
    ker = lax.dot_general(bc_ref[...] * ccol, br_ref[...], tn, precision=HI, preferred_element_type=f32)
    ker = ker[:24, :]
    ks = jnp.sum(ker, keepdims=True)
    ks_ref[...] = jnp.broadcast_to(ks * ks, (8, 128))
    wb[0, :, 128:] = jnp.zeros((256, 128), bf16)
    wb[21, :, :128] = jnp.zeros((256, 128), bf16)
    for dy in range(21):
        base = jnp.broadcast_to(ker[dy:dy + 1, :], (256, 256))
        band = pltpu.roll(base, 0, 1, stride=1, stride_axis=0)[:, :128].astype(bf16)
        wb[dy, :, :128] = band
        wb[dy + 1, :, 128:] = band
    for cc in range(9):
        sl = slice(cc * 128, (cc + 1) * 128)
        f128[cc] = fp_ref[:280, sl]
    for cc in range(9):
        sl = slice(cc * 128, (cc + 1) * 128)
        for dy in range(22):
            fs[dy, :, sl] = f128[cc, pl.ds(dy, 128, stride=2), :].astype(bf16)

    def per_col(c, _):
        c0 = pl.multiple_of(c * 128, 128)
        acc = jnp.zeros((128, 256), f32)
        for dy in range(22):
            acc = acc + jnp.dot(fs[dy, :, pl.ds(c0, 256)], wb[dy], preferred_element_type=f32)
        conv[pl.ds(0, 128, stride=2), :] = acc[:, :128]
        conv[pl.ds(1, 128, stride=2), :] = acc[:, 128:]
        for i in range(2):
            d = sci32[i * 128:(i + 1) * 128, pl.ds(c0, 128)] - conv[i * 128:(i + 1) * 128, :] - bg
            rows32[pl.ds(c + 8 * i, 128, stride=16), :] = d
            img_ref[i * 128:(i + 1) * 128, pl.ds(c0, 128)] = d.astype(bf16)
        return 0
    lax.fori_loop(0, 8, per_col, 0)
    diff_ref[...] = rows32[...].reshape(128, 16, 128).astype(bf16)

def fit_call(rows, cols, fp, sci, var, cb, rb, bc, br, ps):
    f32, bf16 = jnp.float32, jnp.bfloat16
    sm = pl.BlockSpec(memory_space=pltpu.SMEM)
    vm = pl.BlockSpec(memory_space=pltpu.VMEM)
    return pl.pallas_call(
        fit_body,
        out_shape=(jax.ShapeDtypeStruct((8, 128), f32), jax.ShapeDtypeStruct((128, 16, 128), bf16),
                   jax.ShapeDtypeStruct((256, 1024), bf16),
                   jax.ShapeDtypeStruct((8, 128), f32), jax.ShapeDtypeStruct((384, 256), bf16),
                   jax.ShapeDtypeStruct((256, 768), bf16)),
        in_specs=[sm, sm] + [vm] * 8,
        out_specs=(vm,) * 6,
        scratch_shapes=[
            pltpu.VMEM((264, 1152), f32), pltpu.VMEM((264, 1152), f32),
            pltpu.VMEM((640, 256), bf16), pltpu.VMEM((40 * RS, 128), f32),
            pltpu.VMEM((512, 128), f32), pltpu.VMEM((512, 128), f32),
            pltpu.VMEM((22, 256, 256), bf16), pltpu.VMEM((22, 128, 1152), bf16),
            pltpu.VMEM((256, 128), f32), pltpu.VMEM((9, 280, 128), f32),
            pltpu.VMEM((2048, 128), f32)],
        compiler_params=pltpu.CompilerParams(vmem_limit_bytes=60 * 1024 * 1024),
        name="fit",
    )(rows, cols, fp, sci, var, cb, rb, bc, br, ps)

def bands(basis_col, basis_row):
    col = jnp.pad(basis_col.astype(jnp.float32), ((0, 8), (0, 235)))
    row = jnp.pad(basis_row.astype(jnp.float32), ((0, 8), (0, 0)))
    rev = jnp.concatenate([row[:, :1], jnp.zeros((48, 235), jnp.float32), row[:, :0:-1]], axis=1)
    cb = jnp.broadcast_to(col[:40, None, :], (40, 8, 256))
    rb = jnp.broadcast_to(rev[:40, None, :], (40, 8, 256))
    return cb, rb, col[:, :128], rev


def score_rows(psf_down, psf_across):
    flat = jnp.concatenate([jnp.zeros((374,), jnp.float32), psf_across[::-1], jnp.zeros((117,), jnp.float32)])
    tall = jnp.concatenate([psf_down[10:], jnp.zeros((491,), jnp.float32), psf_down[:10]])
    return jnp.concatenate([jnp.broadcast_to(flat[None], (8, 512)), jnp.broadcast_to(tall[None], (8, 512))])


def pick_body(where_s, gt, out, sems):
    def copy(i):
        return pltpu.make_async_copy(gt.at[where_s[i]], out.at[i], sems.at[i])

    def begin(i, _):
        @pl.when(where_s[i] >= 0)
        def _():
            copy(i).start()

        @pl.when(where_s[i] < 0)
        def _():
            out[i] = jnp.zeros((128, 128), jnp.bfloat16)
        return 0

    def done(i, _):
        @pl.when(where_s[i] >= 0)
        def _():
            copy(i).wait()
        return 0

    lax.fori_loop(0, 64, begin, 0)
    lax.fori_loop(0, 64, done, 0)


def pick(where_at, gt):
    return pl.pallas_call(
        pick_body,
        out_shape=jax.ShapeDtypeStruct((64, 128, 128), jnp.bfloat16),
        in_specs=[pl.BlockSpec(memory_space=pltpu.SMEM), pl.BlockSpec(memory_space=pltpu.HBM)],
        out_specs=pl.BlockSpec(memory_space=pltpu.VMEM),
        scratch_shapes=[pltpu.SemaphoreType.DMA((64,))],
        compiler_params=pltpu.CompilerParams(vmem_limit_bytes=8 << 20),
        name="pick",
    )(where_at, gt)


def to_image(blocks, block_rows, block_cols):
    block_side = blocks.shape[-1]
    shaped = blocks.reshape(block_rows, block_cols, block_side, block_side).transpose(0, 2, 1, 3)
    return shaped.reshape(block_rows * block_side, block_cols * block_side)


MESH_ID = pl.DeviceIdType.MESH
SIDE = 128


class Net:
    def __init__(self, ssem, rsem):
        self.ssem, self.rsem, self.sent = ssem, rsem, []
        self.z, self.x, self.c, self.y = (lax.axis_index(a) for a in ("z", "x", "core", "y"))

    def at(self, dz=0, dx=0, dy=0, flip=False):
        c = 1 - self.c if flip else self.c
        return ((self.z + dz + 8) % 8, (self.x + dx + 4) % 4, c, (self.y + dy + 4) % 4)

    def meet(self, peers):
        barrier = pltpu.get_barrier_semaphore()
        for peer in peers:
            pl.semaphore_signal(barrier, inc=1, device_id=peer, device_id_type=MESH_ID)
        pl.semaphore_wait(barrier, len(peers))

    def send(self, src, dst, peer):
        i = len(self.sent)
        copy = pltpu.make_async_remote_copy(
            src_ref=src, dst_ref=dst, send_sem=self.ssem.at[i], recv_sem=self.rsem.at[i],
            device_id=peer, device_id_type=MESH_ID,
        )
        copy.start()
        self.sent.append(copy)
        return copy

    def drain(self):
        for copy in self.sent:
            copy.wait_send()


class ZRing:
    def __init__(self, net, own, out, pieces, arrive):
        self.net, self.out, self.pieces, self.arrive = net, out, pieces, arrive
        self.got = {}
        for p, (start, size) in enumerate(pieces):
            for d in (1, -1):
                self.got[d, 1, p] = net.send(
                    own.at[pl.ds(start, size)], out.at[net.z, net.c, pl.ds(start, size)], net.at(dz=d)
                )

    def part(self, p, d, s):
        start, size = self.pieces[p]
        if s < 4:
            return pl.ds(start, size)
        return pl.ds(start + (0 if d == 1 else size // 2), size // 2)

    def step(self, s):
        net = self.net
        for p in range(len(self.pieces)):
            for d in (1, -1):
                self.got[d, s, p].wait_recv()
                zs = (net.z - d * s + 8) % 8
                if s < 4:
                    ref = self.out.at[zs, net.c, self.part(p, d, s + 1)]
                    self.got[d, s + 1, p] = net.send(ref, ref, net.at(dz=d))
                self.arrive(p, d, s, zs, self.part(p, d, s))


class SmallRing:
    def __init__(self, net, own, out):
        self.net, self.out = net, out
        out[net.c, net.z] = own[...]
        self.got = {(d, 1): net.send(own, out.at[net.c, net.z], net.at(dz=d)) for d in (1, -1)}

    def step(self, s):
        net = self.net
        for d in (1, -1):
            if (d, s) not in self.got:
                continue
            self.got[d, s].wait_recv()
            zs = (net.z - d * s + 8) % 8
            if s + 1 <= (4 if d == 1 else 3):
                ref = self.out.at[net.c, zs]
                self.got[d, s + 1] = net.send(ref, ref, net.at(dz=d))

    def pair(self):
        ref = self.out.at[self.net.c]
        return self.net.send(ref, ref, self.net.at(flip=True))


class Ring4:
    def __init__(self, net, axis, src, dst, relay):
        self.net, self.dst, self.relay = net, dst, relay
        self.up = net.at(**{axis: 1})
        self.down = net.at(**{axis: -1})
        self.fa = net.send(src(2, 0), relay(0), self.up)
        self.fb = net.send(src(2, 1), relay(1), self.down)
        self.na = net.send(src(1, None), dst(0, None), self.up)
        self.nb = net.send(src(-1, None), dst(1, None), self.down)

    def pass_on(self):
        self.fa.wait_recv()
        self.ra = self.net.send(self.relay(0), self.dst(2, 0), self.up)
        self.fb.wait_recv()
        self.rb = self.net.send(self.relay(1), self.dst(2, 1), self.down)

    def finish(self):
        for copy in (self.na, self.nb, self.ra, self.rb):
            copy.wait_recv()


def comm_call(body, outs, spaces, scratch, copies, ident, name, in_spaces, side_bytes):
    def spec(space):
        return pl.BlockSpec(memory_space={"v": pltpu.VMEM, "a": pl.ANY, "h": pltpu.HBM}[space])

    return pl.pallas_call(
        body,
        out_shape=tuple(jax.ShapeDtypeStruct(s, d) for s, d in outs),
        in_specs=[spec(s) for s in in_spaces],
        out_specs=tuple(spec(s) for s in spaces),
        scratch_shapes=list(scratch)
        + [pltpu.SemaphoreType.DMA((copies,)), pltpu.SemaphoreType.DMA((copies,)), pltpu.SemaphoreType.DMA((2,))],
        compiler_params=pltpu.CompilerParams(
            collective_id=ident, has_side_effects=True, vmem_limit_bytes=side_bytes << 20
        ),
        name=name,
    )


def spread_body(t_ref, r_ref, gt, rz, rx, ssem, rsem, lsem):
    net = Net(ssem, rsem)
    z, x, c, y = net.z, net.x, net.c, net.y
    net.meet([net.at(dz=1), net.at(dz=-1), net.at(dy=1), net.at(dy=-1),
              net.at(dx=1), net.at(dx=-1), net.at(dx=2), net.at(flip=True)])
    own = pltpu.make_async_copy(t_ref, gt.at[z, c], lsem.at[0])
    small = SmallRing(net, r_ref, rz)
    rx[x] = r_ref[...]
    row = [net.send(r_ref, rx.at[x], net.at(dx=k)) for k in (1, -1, 2)]
    q0 = y * 8
    q1 = ((y + 1) % 4) * 8
    up = {}

    def arrive(p, d, s, zs, part):
        ref = gt.at[zs, c, part]
        up[p, d, s] = net.send(ref, ref, net.at(dy=1 if p == 0 else -1))

    ring = ZRing(net, t_ref, gt, [(q0, 8), (q1, 8)], arrive)
    own.start()
    ref = gt.at[z, c]
    pair = [net.send(t_ref, ref, net.at(flip=True))]

    def hand_over(s):
        for d in (1, -1):
            for p in (0, 1):
                up[p, d, s].wait_recv()
            if s < 4:
                ref = gt.at[(z - d * s + 8) % 8, c]
                pair.append(net.send(ref, ref, net.at(flip=True)))
        if s == 4:
            ref = gt.at[(z + 4) % 8, c]
            pair.append(net.send(ref, ref, net.at(flip=True)))

    for s in range(1, 5):
        ring.step(s)
        small.step(s)
        if s > 1:
            hand_over(s - 1)
    for copy in row:
        copy.wait_recv()
    small_pair = small.pair()
    hand_over(4)
    for copy in pair:
        copy.wait_recv()
    small_pair.wait_recv()
    own.wait()
    net.drain()


def spread(template, route):
    return comm_call(
        spread_body,
        [((8, 2, 32, SIDE, SIDE), jnp.bfloat16), ((2, 8, 8, 128), jnp.int32), ((4, 8, 128), jnp.int32)],
        "hvv", [], 56, 1, "spread", "vv", 16,
    )(template, route)


class Column:
    def __init__(self, net, own, out, base, size, pieces):
        self.net, self.out, self.base, self.size = net, out, base, size
        rows = pl.ds(base, size)
        self.pair = [net.send(own.at[rows], out.at[net.z, net.c, rows], net.at(flip=True))]
        cut = size // pieces
        self.ring = ZRing(net, own, out, [(base + i * cut, cut) for i in range(pieces)], self.arrive)
        self.step = self.ring.step

    def arrive(self, p, d, s, zs, part):
        if s < 4:
            ref = self.out.at[zs, self.net.c, part]
            self.pair.append(self.net.send(ref, ref, self.net.at(flip=True)))

    def last(self):
        ref = self.out.at[(self.net.z + 4) % 8, self.net.c, pl.ds(self.base, self.size)]
        self.pair.append(self.net.send(ref, ref, self.net.at(flip=True)))
        for copy in self.pair:
            copy.wait_recv()


def fetch_body(sel, v_ref, xf, gv, relay, ssem, rsem, lsem):
    net = Net(ssem, rsem)
    net.meet([net.at(dz=1), net.at(dz=-1), net.at(dx=1), net.at(dx=-1), net.at(flip=True)])

    def src(k, half):
        part = pl.ds(0, 16) if half is None else pl.ds(8 * half, 8)
        return sel.at[(net.x + k + 4) % 4, part]

    def dst(slot, half):
        return xf.at[slot] if half is None else xf.at[slot, pl.ds(8 * half, 8)]

    side = Ring4(net, "dx", src, dst, lambda i: relay.at[i])
    own = pltpu.make_async_copy(v_ref, gv.at[net.z, net.c], lsem.at[0])
    ring = Column(net, v_ref, gv, 0, 128, 2)
    own.start()
    side.pass_on()
    for s in range(1, 5):
        ring.step(s)
    side.finish()
    ring.last()
    own.wait()
    net.drain()


def fetch(sel, svar):
    return comm_call(
        fetch_body,
        [((3, 16, SIDE, SIDE), jnp.bfloat16), ((8, 2, SIDE, 16, SIDE), jnp.bfloat16)],
        "ah", [pltpu.VMEM((2, 8, SIDE, SIDE), jnp.bfloat16)], 40, 2, "fetch", "vv", 16,
    )(sel, svar)


def reduce_scratch():
    def buf(*shape):
        return pltpu.VMEM((4,) + shape + (32, SIDE), jnp.bfloat16)

    return [buf(3, 32), buf(3, 8, 4), buf(2, 16), buf(2, 4, 4), buf(32), buf(8, 4),
            buf(3, 8), buf(3, 8), buf(2, 4), buf(2, 4)]


class Reduce:
    def __init__(self, net, part, base, bufs):
        (self.a0, self.b0, ra, rb, self.ha, self.hb, self.a1, self.b1, self.ra1, self.rb1) = bufs
        self.net, self.part, self.base = net, part, base
        x, y = net.x, net.y

        def src_a(k, half):
            rows = pl.ds(base, 32) if half is None else pl.ds(base + 16 * half, 16)
            return part.at[rows, (x + k + 4) % 4]

        def dst_a(slot, half):
            return self.a0.at[slot] if half is None else self.a0.at[slot, pl.ds(16 * half, 16)]

        def src_b(k, half):
            first = base + 32 + 8 * ((y + k + 4) % 4)
            return part.at[pl.ds(first, 8) if half is None else pl.ds(first + 4 * half, 4)]

        def dst_b(slot, half):
            return self.b0.at[slot] if half is None else self.b0.at[slot, pl.ds(4 * half, 4)]

        self.one = [Ring4(net, "dx", src_a, dst_a, lambda i: ra.at[i]),
                    Ring4(net, "dy", src_b, dst_b, lambda i: rb.at[i])]

    def pass_one(self):
        for ring in self.one:
            ring.pass_on()

    def stage_two(self):
        net = self.net
        x, y = net.x, net.y
        for ring in self.one:
            ring.finish()
        f32 = jnp.float32

        def add_a(i, _):
            total = self.part[self.base + i, x].astype(f32)
            for slot in range(3):
                total = total + self.a0[slot, i].astype(f32)
            self.ha[i] = total.astype(jnp.bfloat16)
            return 0

        def add_b(i, _):
            total = self.part[self.base + 32 + 8 * y + i].astype(f32)
            for slot in range(3):
                total = total + self.b0[slot, i].astype(f32)
            self.hb[i] = total.astype(jnp.bfloat16)
            return 0

        lax.fori_loop(0, 32, add_a, 0)
        lax.fori_loop(0, 8, add_b, 0)

        def src_a(k, half):
            first = 8 * ((y + k + 4) % 4)
            return self.ha.at[pl.ds(first, 8) if half is None else pl.ds(first + 4 * half, 4)]

        def dst_a(slot, half):
            return self.a1.at[slot] if half is None else self.a1.at[slot, pl.ds(4 * half, 4)]

        def src_b(k, half):
            return self.hb.at[pl.ds(0, 8) if half is None else pl.ds(4 * half, 4), (x + k + 4) % 4]

        def dst_b(slot, half):
            return self.b1.at[slot] if half is None else self.b1.at[slot, pl.ds(4 * half, 4)]

        self.two = [Ring4(net, "dy", src_a, dst_a, lambda i: self.ra1.at[i]),
                    Ring4(net, "dx", src_b, dst_b, lambda i: self.rb1.at[i])]

    def pass_two(self):
        for ring in self.two:
            ring.pass_on()

    def finish(self):
        for ring in self.two:
            ring.finish()

    def total(self, h, i):
        f32 = jnp.float32
        if h == 0:
            own, got = self.ha[8 * self.net.y + i], self.a1
        else:
            own, got = self.hb[i, self.net.x], self.b1
        total = own.astype(f32)
        for slot in range(3):
            total = total + got[slot, i].astype(f32)
        return total


def tail_body(dp, ks, hot, count, tq, gv, img, hb, vb, gs, score, gd, gk, vv, vpart, dpart, kx, ky, kown, kall, *rest):
    bufs, (ssem, rsem, lsem) = rest[:10], rest[10:]
    net = Net(ssem, rsem)
    x, y = net.x, net.y
    f32, bf16 = jnp.float32, jnp.bfloat16
    fetch_v = pltpu.make_async_copy(gv, vv, lsem.at[0])
    fetch_v.start()
    net.meet([net.at(dz=1), net.at(dz=-1), net.at(dx=1), net.at(dx=-1), net.at(dx=2),
              net.at(dy=1), net.at(dy=-1), net.at(dy=2), net.at(flip=True)])
    own = pltpu.make_async_copy(dp, gd.at[net.z, net.c], lsem.at[1])
    first = Column(net, dp, gd, 0, 64, 2)
    own.start()
    small = SmallRing(net, ks, gk)
    fetch_v.wait()

    def sums(column, part, base):
        def one(i, _):
            for u in (0, 2):
                p = base + 4 * i + u
                rows = [column[:, :, p + v].reshape(256, SIDE) for v in range(2)]
                got = jnp.dot(hot[...], jnp.concatenate(rows, axis=1), preferred_element_type=f32).astype(bf16)
                for v in range(2):
                    part[p + v] = got[:, v * SIDE:(v + 1) * SIDE].reshape(4, 32, SIDE)
            return 0

        lax.fori_loop(0, 16, one, 0)

    def scores(first_block):
        for c in (first_block, first_block + 1):
            low, high = max(c - 1, 0), min(c + 2, 8)
            window = hb[(low - c + 1) * SIDE:(high - c + 1) * SIDE]
            side = jnp.dot(img[:, low * SIDE:high * SIDE], window, preferred_element_type=f32)
            side = side[:, :SIDE] + side[:, SIDE:]
            top = side.astype(bf16)
            rest_ = (side - top.astype(f32)).astype(bf16)
            stack = jnp.concatenate([top, top, rest_], axis=0)
            score[:, c * SIDE:(c + 1) * SIDE] = jnp.dot(vb[...], stack, preferred_element_type=f32)

    def reduce(part, base, g):
        return Reduce(net, part, base, [b.at[g] for b in bufs])

    sums(vv, vpart, 0)
    v0 = reduce(vpart, 0, 0)
    first.step(1)
    small.step(1)
    sums(vv, vpart, 64)
    v1 = reduce(vpart, 64, 1)
    first.step(2)
    small.step(2)
    second = Column(net, dp, gd, 64, 64, 2)
    v0.pass_one()
    scores(0)
    first.step(3)
    small.step(3)
    scores(2)
    first.step(4)
    small.step(4)
    pair = small.pair()
    v1.pass_one()
    own.wait()
    second.step(1)
    v0.stage_two()
    first.last()
    sums(gd, dpart, 0)
    d0 = reduce(dpart, 0, 2)
    v1.stage_two()
    second.step(2)
    v0.pass_two()
    v1.pass_two()
    pair.wait_recv()
    total = gk[0, 0] * count[0]
    for i in range(1, 16):
        total = total + gk[i % 2, i // 2] * count[i]
    kown[...] = total
    kxs = [net.send(kown, kx.at[i], net.at(dx=k)) for i, k in enumerate((1, -1, 2))]
    d0.pass_one()
    scores(4)
    second.step(3)
    for copy in kxs:
        copy.wait_recv()
    kall[...] = kown[...] + kx[0] + kx[1] + kx[2]
    kys = [net.send(kall, ky.at[i], net.at(dy=k)) for i, k in enumerate((1, -1, 2))]
    scores(6)
    second.step(4)
    second.last()
    sums(gd, dpart, 64)
    d1 = reduce(dpart, 64, 3)
    d0.stage_two()
    for copy in kys:
        copy.wait_recv()
    ksum = kall[0:1, :] + ky[0, 0:1, :] + ky[1, 0:1, :] + ky[2, 0:1, :]
    lane = lax.broadcasted_iota(jnp.int32, (32, SIDE), 1)
    line = lax.broadcasted_iota(jnp.int32, (32, SIDE), 0)
    kcol = jnp.sum(jnp.where(lane == x * 32 + line, jnp.broadcast_to(ksum, (32, SIDE)), 0.0), axis=1, keepdims=True)
    up, down = net.at(dy=1), net.at(dy=-1)
    v0.finish()
    v1.finish()
    d1.pass_one()
    d0.pass_two()

    def settle(diff, var, g):
        def put(i, _):
            for h in range(2):
                v = var.total(h, i) + kcol * tq[g, h, i].astype(f32)
                gs[g, y, h, i] = (diff.total(h, i) / jnp.sqrt(jnp.maximum(v, 1.0))).astype(bf16)
            return 0

        lax.fori_loop(0, 8, put, 0)
        mine = gs.at[g, y]
        return net.send(mine, mine, up), net.send(mine, mine, down)

    def relay(pair_of, g):
        a, b = pair_of
        a.wait_recv()
        ref = gs.at[g, (y + 3) % 4, 0]
        a2 = net.send(ref, ref, up)
        b.wait_recv()
        ref = gs.at[g, (y + 1) % 4, 1]
        return a2, net.send(ref, ref, down)

    d0.finish()
    out0 = settle(d0, v0, 0)
    d1.stage_two()
    d1.pass_two()
    far0 = relay(out0, 0)
    d1.finish()
    out1 = settle(d1, v1, 1)
    far1 = relay(out1, 1)
    for copy in far0 + far1:
        copy.wait_recv()
    net.drain()


def tail(diff, squares, hot, count, tq, gv, img, hb, vb):
    f32, bf16 = jnp.float32, jnp.bfloat16
    tile = pltpu.VMEM((3, 8, 128), f32)
    return comm_call(
        tail_body,
        [((2, 4, 2, 8, 32, SIDE), bf16), ((256, 1024), f32)],
        "vv",
        [pltpu.VMEM((8, 2, SIDE, 16, SIDE), bf16), pltpu.VMEM((2, 8, 8, SIDE), f32),
         pltpu.VMEM((8, 2, SIDE, 16, SIDE), bf16), pltpu.VMEM((SIDE, 4, 32, SIDE), bf16),
         pltpu.VMEM((SIDE, 4, 32, SIDE), bf16), tile, tile, pltpu.VMEM((8, 128), f32), pltpu.VMEM((8, 128), f32)]
        + reduce_scratch(),
        184, 3, "tail", "vvvvvhvvv", 58,
    )(diff, squares, hot, count, tq, gv, img, hb, vb)


def local(
    template,
    template_var,
    science,
    science_var,
    routes_src,
    routes_blk,
    stamp_rows,
    stamp_cols,
    basis_col,
    basis_row,
    psf_col,
    psf_row,
):
    bf16, f32 = jnp.bfloat16, jnp.float32
    z, x, c, y = (lax.axis_index(a) for a in ("z", "x", "core", "y"))
    route = routes_src[0] * 32 + routes_blk[0]
    route = jnp.broadcast_to(jnp.pad(route, (0, 112))[None], (8, 128))
    gt, rz, rx = spread(template, route)
    wants = rx[:, 0, :16].reshape(64)
    owner = wants // 32
    here = (owner // 2) % 4 == x
    slot = (owner // 8) * 64 + (owner % 2) * 32 + wants % 32
    sel = pick(jnp.where(here, slot, -1), gt.reshape(512, SIDE, SIDE)).reshape(4, 16, SIDE, SIDE)
    svar = science_var[0].reshape(2, SIDE, 8, SIDE).transpose(1, 0, 2, 3).reshape(SIDE, 16, SIDE)
    xf, gv = fetch(sel, svar)
    frame = lax.dynamic_index_in_dim(sel, x, 0, keepdims=False) + xf[0] + xf[1] + xf[2]
    fp = jnp.pad(to_image(frame, 2, 8).astype(f32), ((10, 30), (10, 246)))
    coef, diff, image, ks2, hb, vb = fit_call(
        stamp_rows[0], stamp_cols[0], fp, science[0], science_var[0], *bands(basis_col, basis_row),
        score_rows(psf_col[0], psf_row[0]),
    )
    goes = rz[:, :, 0, :16].transpose(1, 0, 2).reshape(256)
    owner = goes // 32
    ours = (owner // 8 == z) & (owner % 2 == c)
    target = jnp.where(ours, ((owner // 2) % 4) * 32 + goes % 32, -1)
    hot = target[None, :] == jnp.arange(SIDE)[:, None]
    count = jnp.sum(hot.reshape(SIDE, 16, 16).astype(f32), axis=2).T
    count = jnp.broadcast_to(count[:, None, :], (16, 8, SIDE))
    tq = lax.dynamic_index_in_dim(template_var.reshape(32, 2, 2, 4, 8, SIDE), y, 3, keepdims=False)
    gs, scored = tail(diff, ks2, hot.astype(bf16), count, tq.transpose(1, 2, 3, 0, 4), gv, image, hb, vb)
    significance = gs.transpose(4, 0, 2, 1, 3, 5).reshape(32, SIDE, SIDE)
    return (significance.astype(f32), scored[None], coef[:1, :41])


def solution(mesh):
    fine = Mesh(mesh.devices.reshape(8, 4, 2, 4), ("z", "x", "core", "y"))
    det = ("z", "x", "core")
    placed = (
        P(det, None, None),
        P(det, None, None),
        P("y", det, None),
        P("y", det, None),
        P("y", det),
        P("y", det),
        P("y", det),
        P("y", det),
        P(),
        P(),
        P("y", None),
        P("y", None),
    )
    return jax.shard_map(
        local,
        mesh=fine,
        in_specs=placed,
        out_specs=(P(det, None, None), P("y", det, None), P("y", det)),
        check_vma=False,
    )
```

```python
import jax, jax.numpy as jnp
from jax import lax
from jax.experimental import pallas as pl
from jax.experimental.pallas import tpu as pltpu

from jax.sharding import Mesh, PartitionSpec as P

HI = lax.Precision.HIGHEST
precise_mode = HI
RS = 520

def cut_body(rows_s, cols_s, fp_ref, sci_ref, var_ref, ps_ref, stk, sst, wst, hb_ref, vb_ref, sci32, var32):
    f32, bf16 = jnp.float32, jnp.bfloat16
    sci32[:256, :1024] = sci_ref[...].astype(f32)
    var32[:256, :1024] = var_ref[...].astype(f32)
    for s in range(4):
        y0 = rows_s[s]
        x0 = cols_s[s]
        xa = pl.multiple_of((x0 // 128) * 128, 128)
        rem = x0 - xa
        ya = pl.multiple_of((y0 // 8) * 8, 8)
        ry = y0 - ya
        t = pltpu.roll(fp_ref[pl.ds(ya, 168), pl.ds(xa, 384)], 168 - ry, 0)[:160]
        t = pltpu.roll(t, 384 - rem, 1)[:, :256]
        stk[s * 160:(s + 1) * 160, :] = t.astype(bf16)
        c = pltpu.roll(sci32[pl.ds(ya, 136), pl.ds(xa, 256)], 136 - ry, 0)[:128]
        sst[s * 128:(s + 1) * 128, :] = pltpu.roll(c, 256 - rem, 1)[:, :128]
        v = pltpu.roll(var32[pl.ds(ya, 136), pl.ds(xa, 256)], 136 - ry, 0)[:128]
        wst[s * 128:(s + 1) * 128, :] = jnp.sqrt(1.0 / pltpu.roll(v, 256 - rem, 1)[:, :128])

    def split(band):
        high = band.astype(bf16)
        return high, (band - high.astype(f32)).astype(bf16)

    h0, h1 = split(pltpu.roll(jnp.broadcast_to(ps_ref[0:1, :], (384, 512)), 0, 1, stride=1, stride_axis=0)[:, :128])
    hb_ref[:, :128] = h0
    hb_ref[:, 128:] = h1
    h0, h1 = split(pltpu.roll(jnp.broadcast_to(ps_ref[8:9, :], (256, 512)), 0, 1, stride=1, stride_axis=0)[:, :256])
    vb_ref[:, :256] = h0
    vb_ref[:, 256:512] = h1
    vb_ref[:, 512:] = h0


def cut_call(rows, cols, fp, sci, var, ps):
    f32, bf16 = jnp.float32, jnp.bfloat16
    sm = pl.BlockSpec(memory_space=pltpu.SMEM)
    vm = pl.BlockSpec(memory_space=pltpu.VMEM)
    return pl.pallas_call(
        cut_body,
        out_shape=(jax.ShapeDtypeStruct((640, 256), bf16), jax.ShapeDtypeStruct((512, 128), f32),
                   jax.ShapeDtypeStruct((512, 128), f32), jax.ShapeDtypeStruct((384, 256), bf16),
                   jax.ShapeDtypeStruct((256, 768), bf16)),
        in_specs=[sm, sm] + [vm] * 4,
        out_specs=(vm,) * 5,
        scratch_shapes=[pltpu.VMEM((264, 1152), f32), pltpu.VMEM((264, 1152), f32)],
        compiler_params=pltpu.CompilerParams(vmem_limit_bytes=24 << 20),
        name="cut",
    )(rows, cols, fp, sci, var, ps)


def fit_body(stk, sst, wst, fp_ref, sci_ref, cb_ref, rb_ref, bc_ref, br_ref, v_ref,
             coef_ref, diff_ref, img_ref, ks_ref, gv,
             sci32, dsg, wb, fs, conv, f128, rows32, ssem, rsem, lsem):
    f32, bf16 = jnp.float32, jnp.bfloat16
    net = Net(ssem, rsem)
    net.meet([net.at(dz=1), net.at(dz=-1), net.at(flip=True)])
    own = pltpu.make_async_copy(v_ref, gv.at[net.z, net.c], lsem.at[0])
    column = Column(net, v_ref, gv, 0, 128, 2)
    own.start()
    sci32[:256, :1024] = sci_ref[...].astype(f32)

    def per_basis(k, _):
        cb = jnp.broadcast_to(cb_ref[k][0:1], (128, 256))
        cb = pltpu.roll(cb, 0, 1, stride=1, stride_axis=0)[:, :160].astype(bf16)
        rb = jnp.broadcast_to(rb_ref[k][0:1], (256, 256))
        rb = pltpu.roll(rb, 0, 1, stride=1, stride_axis=0)[:, :128].astype(bf16)
        a = jnp.dot(stk[...], rb, preferred_element_type=f32).astype(bf16)
        a = jnp.concatenate([a[i * 160:(i + 1) * 160] for i in range(4)], axis=1)
        d = jnp.dot(cb, a, preferred_element_type=f32)
        for s in range(4):
            dsg[pl.ds(pl.multiple_of(k * RS + s * 128, 8), 128), :] = d[:, s * 128:(s + 1) * 128]
        return 0
    lax.fori_loop(0, 24, per_basis, 0)
    column.step(1)
    lax.fori_loop(24, 40, per_basis, 0)

    sub = lax.broadcasted_iota(jnp.int32, (8, 128), 0)

    def per_rows(g, acc):
        xs = []
        for q in range(8):
            r = g * 8 + q
            x = dsg[pl.ds(r, 40, stride=RS), :]
            srow = jnp.broadcast_to(sst[pl.ds(r, 1), :], (8, 128))
            extra = jnp.where(sub == 0, 1.0, jnp.where(sub == 1, srow, 0.0))
            x = jnp.concatenate([x, extra], axis=0)
            xs.append(x * jnp.broadcast_to(wst[pl.ds(r, 1), :], (48, 128)))
        x = jnp.concatenate(xs, axis=1)
        xh = x.astype(bf16)
        xl = (x - xh.astype(f32)).astype(bf16)
        nt = (((1,), (1,)), ((), ()))
        both = lax.dot_general(xh, jnp.concatenate([xh, xl], axis=0), nt, preferred_element_type=f32)
        return acc + both
    both = lax.fori_loop(0, 28, per_rows, jnp.zeros((48, 96), f32))
    column.step(2)
    both = lax.fori_loop(28, 64, per_rows, both)
    both = jnp.concatenate([both, jnp.zeros((48, 32), f32)], axis=1)
    cross = pltpu.roll(both, 80, 1)[:, :48]
    eye = (lax.broadcasted_iota(jnp.int32, (48, 48), 0) == lax.broadcasted_iota(jnp.int32, (48, 48), 1)).astype(f32)
    flip = lax.dot_general(cross, eye, (((0,), (0,)), ((), ())), precision=HI, preferred_element_type=f32)
    gram = both[:, :48] + cross + flip

    ri = lax.broadcasted_iota(jnp.int32, (48, 48), 0)
    ci = lax.broadcasted_iota(jnp.int32, (48, 48), 1)
    m = gram * (1.0 / 65536.0) + jnp.where((ri == ci) & (ri < 41), 0.01, 0.0)
    for n in range(41):
        prow = m[n:n + 1, :]
        pcol = m[:, n:n + 1]
        new = prow / m[n:n + 1, n:n + 1]
        m = jnp.where(ri == n, jnp.broadcast_to(new, (48, 48)), m - pcol * new)
    rcol = lax.broadcasted_iota(jnp.int32, (48, 1), 0)
    col = m[:, 41:42]
    row = jnp.sum(jnp.where(ri == ci, jnp.broadcast_to(col, (48, 48)), 0.0), axis=0, keepdims=True)
    coef_ref[...] = jnp.broadcast_to(jnp.pad(row, ((0, 0), (0, 80))), (8, 128))
    bg = m[40:41, 41:42]
    ccol = jnp.where(rcol < 40, col, 0.0)
    tn = (((0,), (0,)), ((), ()))
    ker = lax.dot_general(bc_ref[...] * ccol, br_ref[...], tn, precision=HI, preferred_element_type=f32)
    ker = ker[:24, :]
    ks = jnp.sum(ker, keepdims=True)
    ks_ref[...] = jnp.broadcast_to(ks * ks, (8, 128))
    wb[0, :, 128:] = jnp.zeros((256, 128), bf16)
    wb[21, :, :128] = jnp.zeros((256, 128), bf16)
    for dy in range(21):
        base = jnp.broadcast_to(ker[dy:dy + 1, :], (256, 256))
        band = pltpu.roll(base, 0, 1, stride=1, stride_axis=0)[:, :128].astype(bf16)
        wb[dy, :, :128] = band
        wb[dy + 1, :, 128:] = band
    for cc in range(9):
        sl = slice(cc * 128, (cc + 1) * 128)
        f128[cc] = fp_ref[:280, sl]
    for cc in range(9):
        sl = slice(cc * 128, (cc + 1) * 128)
        for dy in range(22):
            fs[dy, :, sl] = f128[cc, pl.ds(dy, 128, stride=2), :].astype(bf16)

    def per_col(c, _):
        c0 = pl.multiple_of(c * 128, 128)
        acc = jnp.zeros((128, 256), f32)
        for dy in range(22):
            acc = acc + jnp.dot(fs[dy, :, pl.ds(c0, 256)], wb[dy], preferred_element_type=f32)
        conv[pl.ds(0, 128, stride=2), :] = acc[:, :128]
        conv[pl.ds(1, 128, stride=2), :] = acc[:, 128:]
        for i in range(2):
            d = sci32[i * 128:(i + 1) * 128, pl.ds(c0, 128)] - conv[i * 128:(i + 1) * 128, :] - bg
            rows32[pl.ds(c + 8 * i, 128, stride=16), :] = d
            img_ref[i * 128:(i + 1) * 128, pl.ds(c0, 128)] = d.astype(bf16)
        return 0
    column.step(3)
    lax.fori_loop(0, 8, per_col, 0)
    diff_ref[...] = rows32[...].reshape(128, 16, 128).astype(bf16)
    column.step(4)
    column.last()
    own.wait()
    net.drain()

def fit_call(stk, sst, wst, fp, sci, cb, rb, bc, br, v):
    f32, bf16 = jnp.float32, jnp.bfloat16
    vm = pl.BlockSpec(memory_space=pltpu.VMEM)
    return pl.pallas_call(
        fit_body,
        out_shape=(jax.ShapeDtypeStruct((8, 128), f32), jax.ShapeDtypeStruct((128, 16, 128), bf16),
                   jax.ShapeDtypeStruct((256, 1024), bf16),
                   jax.ShapeDtypeStruct((8, 128), f32),
                   jax.ShapeDtypeStruct((8, 2, 128, 16, 128), bf16)),
        in_specs=[vm] * 10,
        out_specs=(vm,) * 4 + (pl.BlockSpec(memory_space=pltpu.HBM),),
        scratch_shapes=[
            pltpu.VMEM((264, 1152), f32), pltpu.VMEM((40 * RS, 128), f32),
            pltpu.VMEM((22, 256, 256), bf16), pltpu.VMEM((22, 128, 1152), bf16),
            pltpu.VMEM((256, 128), f32), pltpu.VMEM((9, 280, 128), f32),
            pltpu.VMEM((2048, 128), f32), pltpu.SemaphoreType.DMA((32,)), pltpu.SemaphoreType.DMA((32,)),
            pltpu.SemaphoreType.DMA((1,))],
        compiler_params=pltpu.CompilerParams(
            vmem_limit_bytes=60 * 1024 * 1024, collective_id=5, has_side_effects=True),
        name="fit",
    )(stk, sst, wst, fp, sci, cb, rb, bc, br, v)

def bands(basis_col, basis_row):
    col = jnp.pad(basis_col.astype(jnp.float32), ((0, 8), (0, 235)))
    row = jnp.pad(basis_row.astype(jnp.float32), ((0, 8), (0, 0)))
    rev = jnp.concatenate([row[:, :1], jnp.zeros((48, 235), jnp.float32), row[:, :0:-1]], axis=1)
    cb = jnp.broadcast_to(col[:40, None, :], (40, 8, 256))
    rb = jnp.broadcast_to(rev[:40, None, :], (40, 8, 256))
    return cb, rb, col[:, :128], rev


def score_rows(psf_down, psf_across):
    flat = jnp.concatenate([jnp.zeros((374,), jnp.float32), psf_across[::-1], jnp.zeros((117,), jnp.float32)])
    tall = jnp.concatenate([psf_down[10:], jnp.zeros((491,), jnp.float32), psf_down[:10]])
    return jnp.concatenate([jnp.broadcast_to(flat[None], (8, 512)), jnp.broadcast_to(tall[None], (8, 512))])


def pick_body(where_s, gt, out, sems):
    def copy(i):
        return pltpu.make_async_copy(gt.at[where_s[i]], out.at[i], sems.at[i])

    def begin(i, _):
        @pl.when(where_s[i] >= 0)
        def _():
            copy(i).start()

        @pl.when(where_s[i] < 0)
        def _():
            out[i] = jnp.zeros((128, 128), jnp.bfloat16)
        return 0

    def done(i, _):
        @pl.when(where_s[i] >= 0)
        def _():
            copy(i).wait()
        return 0

    lax.fori_loop(0, 64, begin, 0)
    lax.fori_loop(0, 64, done, 0)


def pick(where_at, gt):
    return pl.pallas_call(
        pick_body,
        out_shape=jax.ShapeDtypeStruct((64, 128, 128), jnp.bfloat16),
        in_specs=[pl.BlockSpec(memory_space=pltpu.SMEM), pl.BlockSpec(memory_space=pltpu.HBM)],
        out_specs=pl.BlockSpec(memory_space=pltpu.VMEM),
        scratch_shapes=[pltpu.SemaphoreType.DMA((64,))],
        compiler_params=pltpu.CompilerParams(vmem_limit_bytes=60 << 20),
        name="pick",
    )(where_at, gt)


def to_image(blocks, block_rows, block_cols):
    block_side = blocks.shape[-1]
    shaped = blocks.reshape(block_rows, block_cols, block_side, block_side).transpose(0, 2, 1, 3)
    return shaped.reshape(block_rows * block_side, block_cols * block_side)


MESH_ID = pl.DeviceIdType.MESH
SIDE = 128


class Net:
    def __init__(self, ssem, rsem):
        self.ssem, self.rsem, self.sent = ssem, rsem, []
        self.z, self.x, self.c, self.y = (lax.axis_index(a) for a in ("z", "x", "core", "y"))

    def at(self, dz=0, dx=0, dy=0, flip=False):
        c = 1 - self.c if flip else self.c
        return ((self.z + dz + 8) % 8, (self.x + dx + 4) % 4, c, (self.y + dy + 4) % 4)

    def meet(self, peers):
        barrier = pltpu.get_barrier_semaphore()
        for peer in peers:
            pl.semaphore_signal(barrier, inc=1, device_id=peer, device_id_type=MESH_ID)
        pl.semaphore_wait(barrier, len(peers))

    def send(self, src, dst, peer):
        i = len(self.sent)
        copy = pltpu.make_async_remote_copy(
            src_ref=src, dst_ref=dst, send_sem=self.ssem.at[i], recv_sem=self.rsem.at[i],
            device_id=peer, device_id_type=MESH_ID,
        )
        copy.start()
        self.sent.append(copy)
        return copy

    def drain(self):
        for copy in self.sent:
            copy.wait_send()


class ZRing:
    def __init__(self, net, own, out, pieces, arrive):
        self.net, self.out, self.pieces, self.arrive = net, out, pieces, arrive
        self.got = {}
        for p, (start, size) in enumerate(pieces):
            for d in (1, -1):
                self.got[d, 1, p] = net.send(
                    own.at[pl.ds(start, size)], out.at[net.z, net.c, pl.ds(start, size)], net.at(dz=d)
                )

    def part(self, p, d, s):
        start, size = self.pieces[p]
        if s < 4:
            return pl.ds(start, size)
        return pl.ds(start + (0 if d == 1 else size // 2), size // 2)

    def step(self, s):
        net = self.net
        for p in range(len(self.pieces)):
            for d in (1, -1):
                self.got[d, s, p].wait_recv()
                zs = (net.z - d * s + 8) % 8
                if s < 4:
                    ref = self.out.at[zs, net.c, self.part(p, d, s + 1)]
                    self.got[d, s + 1, p] = net.send(ref, ref, net.at(dz=d))
                self.arrive(p, d, s, zs, self.part(p, d, s))


class SmallRing:
    def __init__(self, net, own, out):
        self.net, self.out = net, out
        out[net.c, net.z] = own[...]
        self.got = {(d, 1): net.send(own, out.at[net.c, net.z], net.at(dz=d)) for d in (1, -1)}

    def step(self, s):
        net = self.net
        for d in (1, -1):
            if (d, s) not in self.got:
                continue
            self.got[d, s].wait_recv()
            zs = (net.z - d * s + 8) % 8
            if s + 1 <= (4 if d == 1 else 3):
                ref = self.out.at[net.c, zs]
                self.got[d, s + 1] = net.send(ref, ref, net.at(dz=d))

    def pair(self):
        ref = self.out.at[self.net.c]
        return self.net.send(ref, ref, self.net.at(flip=True))


class Ring4:
    def __init__(self, net, axis, src, dst, relay):
        self.net, self.dst, self.relay = net, dst, relay
        self.up = net.at(**{axis: 1})
        self.down = net.at(**{axis: -1})
        self.fa = net.send(src(2, 0), relay(0), self.up)
        self.fb = net.send(src(2, 1), relay(1), self.down)
        self.na = net.send(src(1, None), dst(0, None), self.up)
        self.nb = net.send(src(-1, None), dst(1, None), self.down)

    def pass_on(self):
        self.fa.wait_recv()
        self.ra = self.net.send(self.relay(0), self.dst(2, 0), self.up)
        self.fb.wait_recv()
        self.rb = self.net.send(self.relay(1), self.dst(2, 1), self.down)

    def finish(self):
        for copy in (self.na, self.nb, self.ra, self.rb):
            copy.wait_recv()


def comm_call(body, outs, spaces, scratch, copies, ident, name, in_spaces, side_bytes):
    def spec(space):
        return pl.BlockSpec(memory_space={"v": pltpu.VMEM, "a": pl.ANY, "h": pltpu.HBM}[space])

    return pl.pallas_call(
        body,
        out_shape=tuple(jax.ShapeDtypeStruct(s, d) for s, d in outs),
        in_specs=[spec(s) for s in in_spaces],
        out_specs=tuple(spec(s) for s in spaces),
        scratch_shapes=list(scratch)
        + [pltpu.SemaphoreType.DMA((copies,)), pltpu.SemaphoreType.DMA((copies,)), pltpu.SemaphoreType.DMA((2,))],
        compiler_params=pltpu.CompilerParams(
            collective_id=ident, has_side_effects=True, vmem_limit_bytes=side_bytes << 20
        ),
        name=name,
    )


def spread_body(t_ref, r_ref, gt, rz, rx, ssem, rsem, lsem):
    net = Net(ssem, rsem)
    z, x, c, y = net.z, net.x, net.c, net.y
    net.meet([net.at(dz=1), net.at(dz=-1), net.at(dy=1), net.at(dy=-1),
              net.at(dx=1), net.at(dx=-1), net.at(dx=2), net.at(flip=True)])
    own = pltpu.make_async_copy(t_ref, gt.at[z, c], lsem.at[0])
    small = SmallRing(net, r_ref, rz)
    rx[x] = r_ref[...]
    row = [net.send(r_ref, rx.at[x], net.at(dx=k)) for k in (1, -1, 2)]
    q0 = y * 8
    q1 = ((y + 1) % 4) * 8
    up = {}

    def arrive(p, d, s, zs, part):
        ref = gt.at[zs, c, part]
        up[p, d, s] = net.send(ref, ref, net.at(dy=1 if p % 2 == 0 else -1))

    ring = ZRing(net, t_ref, gt, [(q0, 4), (q1, 4), (q0 + 4, 4), (q1 + 4, 4)], arrive)
    own.start()
    ref = gt.at[z, c]
    pair = [net.send(t_ref, ref, net.at(flip=True))]

    def hand_over(s):
        for d in (1, -1):
            for p in range(4):
                up[p, d, s].wait_recv()
            if s < 4:
                ref = gt.at[(z - d * s + 8) % 8, c]
                pair.append(net.send(ref, ref, net.at(flip=True)))
        if s == 4:
            ref = gt.at[(z + 4) % 8, c]
            pair.append(net.send(ref, ref, net.at(flip=True)))

    for s in range(1, 5):
        ring.step(s)
        small.step(s)
        if s > 1:
            hand_over(s - 1)
    for copy in row:
        copy.wait_recv()
    small_pair = small.pair()
    hand_over(4)
    for copy in pair:
        copy.wait_recv()
    small_pair.wait_recv()
    own.wait()
    net.drain()


def spread(template, route):
    return comm_call(
        spread_body,
        [((8, 2, 32, SIDE, SIDE), jnp.bfloat16), ((2, 8, 8, 128), jnp.int32), ((4, 8, 128), jnp.int32)],
        "hvv", [], 84, 1, "spread", "vv", 60,
    )(template, route)


class Column:
    def __init__(self, net, own, out, base, size, pieces):
        self.net, self.out, self.base, self.size = net, out, base, size
        rows = pl.ds(base, size)
        self.pair = [net.send(own.at[rows], out.at[net.z, net.c, rows], net.at(flip=True))]
        cut = size // pieces
        self.ring = ZRing(net, own, out, [(base + i * cut, cut) for i in range(pieces)], self.arrive)
        self.step = self.ring.step

    def arrive(self, p, d, s, zs, part):
        if s < 4:
            ref = self.out.at[zs, self.net.c, part]
            self.pair.append(self.net.send(ref, ref, self.net.at(flip=True)))

    def last(self):
        ref = self.out.at[(self.net.z + 4) % 8, self.net.c, pl.ds(self.base, self.size)]
        self.pair.append(self.net.send(ref, ref, self.net.at(flip=True)))
        for copy in self.pair:
            copy.wait_recv()


def fetch_body(sel, xf, relay, ssem, rsem, lsem):
    net = Net(ssem, rsem)
    net.meet([net.at(dx=1), net.at(dx=-1)])

    def src(k, half):
        part = pl.ds(0, 16) if half is None else pl.ds(8 * half, 8)
        return sel.at[(net.x + k + 4) % 4, part]

    def dst(slot, half):
        return xf.at[slot] if half is None else xf.at[slot, pl.ds(8 * half, 8)]

    side = Ring4(net, "dx", src, dst, lambda i: relay.at[i])
    side.pass_on()
    side.finish()
    net.drain()


def fetch(sel):
    return comm_call(
        fetch_body,
        [((3, 16, SIDE, SIDE), jnp.bfloat16)],
        "v", [pltpu.VMEM((2, 8, SIDE, SIDE), jnp.bfloat16)], 8, 2, "fetch", "v", 60,
    )(sel)[0]


def reduce_scratch():
    def buf(*shape):
        return pltpu.VMEM((4,) + shape + (32, SIDE), jnp.bfloat16)

    return [buf(3, 32), buf(3, 8, 4), buf(2, 16), buf(2, 4, 4), buf(32), buf(8, 4),
            buf(3, 8), buf(3, 8), buf(2, 4), buf(2, 4)]


class Reduce:
    def __init__(self, net, part, base, bufs):
        (self.a0, self.b0, ra, rb, self.ha, self.hb, self.a1, self.b1, self.ra1, self.rb1) = bufs
        self.net, self.part, self.base = net, part, base
        x, y = net.x, net.y

        def src_a(k, half):
            rows = pl.ds(base, 32) if half is None else pl.ds(base + 16 * half, 16)
            return part.at[rows, (x + k + 4) % 4]

        def dst_a(slot, half):
            return self.a0.at[slot] if half is None else self.a0.at[slot, pl.ds(16 * half, 16)]

        def src_b(k, half):
            first = base + 32 + 8 * ((y + k + 4) % 4)
            return part.at[pl.ds(first, 8) if half is None else pl.ds(first + 4 * half, 4)]

        def dst_b(slot, half):
            return self.b0.at[slot] if half is None else self.b0.at[slot, pl.ds(4 * half, 4)]

        self.one = [Ring4(net, "dx", src_a, dst_a, lambda i: ra.at[i]),
                    Ring4(net, "dy", src_b, dst_b, lambda i: rb.at[i])]

    def pass_one(self):
        for ring in self.one:
            ring.pass_on()

    def stage_two(self):
        net = self.net
        x, y = net.x, net.y
        for ring in self.one:
            ring.finish()
        f32 = jnp.float32

        def add_a(i, _):
            total = self.part[self.base + i, x].astype(f32)
            for slot in range(3):
                total = total + self.a0[slot, i].astype(f32)
            self.ha[i] = total.astype(jnp.bfloat16)
            return 0

        def add_b(i, _):
            total = self.part[self.base + 32 + 8 * y + i].astype(f32)
            for slot in range(3):
                total = total + self.b0[slot, i].astype(f32)
            self.hb[i] = total.astype(jnp.bfloat16)
            return 0

        lax.fori_loop(0, 32, add_a, 0)
        lax.fori_loop(0, 8, add_b, 0)

        def src_a(k, half):
            first = 8 * ((y + k + 4) % 4)
            return self.ha.at[pl.ds(first, 8) if half is None else pl.ds(first + 4 * half, 4)]

        def dst_a(slot, half):
            return self.a1.at[slot] if half is None else self.a1.at[slot, pl.ds(4 * half, 4)]

        def src_b(k, half):
            return self.hb.at[pl.ds(0, 8) if half is None else pl.ds(4 * half, 4), (x + k + 4) % 4]

        def dst_b(slot, half):
            return self.b1.at[slot] if half is None else self.b1.at[slot, pl.ds(4 * half, 4)]

        self.two = [Ring4(net, "dy", src_a, dst_a, lambda i: self.ra1.at[i]),
                    Ring4(net, "dx", src_b, dst_b, lambda i: self.rb1.at[i])]

    def pass_two(self):
        for ring in self.two:
            ring.pass_on()

    def finish(self):
        for ring in self.two:
            ring.finish()

    def total(self, h, i):
        f32 = jnp.float32
        if h == 0:
            own, got = self.ha[8 * self.net.y + i], self.a1
        else:
            own, got = self.hb[i, self.net.x], self.b1
        total = own.astype(f32)
        for slot in range(3):
            total = total + got[slot, i].astype(f32)
        return total


def tail_body(dp, ks, hot, count, tq, gv, img, hb, vb, gs, score, gd, gk, vv, vpart, dpart, kx, ky, kown, kall, *rest):
    bufs, (ssem, rsem, lsem) = rest[:10], rest[10:]
    net = Net(ssem, rsem)
    x, y = net.x, net.y
    f32, bf16 = jnp.float32, jnp.bfloat16
    fetch_v = pltpu.make_async_copy(gv, vv, lsem.at[0])
    fetch_v.start()
    net.meet([net.at(dz=1), net.at(dz=-1), net.at(dx=1), net.at(dx=-1), net.at(dx=2),
              net.at(dy=1), net.at(dy=-1), net.at(dy=2), net.at(flip=True)])
    own = pltpu.make_async_copy(dp, gd.at[net.z, net.c], lsem.at[1])
    first = Column(net, dp, gd, 0, 64, 2)
    own.start()
    small = SmallRing(net, ks, gk)
    fetch_v.wait()

    def sums(column, part, base):
        def one(i, _):
            for u in (0, 2):
                p = base + 4 * i + u
                rows = [column[:, :, p + v].reshape(256, SIDE) for v in range(2)]
                got = jnp.dot(hot[...], jnp.concatenate(rows, axis=1), preferred_element_type=f32).astype(bf16)
                for v in range(2):
                    part[p + v] = got[:, v * SIDE:(v + 1) * SIDE].reshape(4, 32, SIDE)
            return 0

        lax.fori_loop(0, 16, one, 0)

    def scores(first_block):
        for c in (first_block, first_block + 1):
            low, high = max(c - 1, 0), min(c + 2, 8)
            window = hb[(low - c + 1) * SIDE:(high - c + 1) * SIDE]
            side = jnp.dot(img[:, low * SIDE:high * SIDE], window, preferred_element_type=f32)
            side = side[:, :SIDE] + side[:, SIDE:]
            top = side.astype(bf16)
            rest_ = (side - top.astype(f32)).astype(bf16)
            stack = jnp.concatenate([top, top, rest_], axis=0)
            score[:, c * SIDE:(c + 1) * SIDE] = jnp.dot(vb[...], stack, preferred_element_type=f32)

    def reduce(part, base, g):
        return Reduce(net, part, base, [b.at[g] for b in bufs])

    sums(vv, vpart, 0)
    v0 = reduce(vpart, 0, 0)
    first.step(1)
    small.step(1)
    sums(vv, vpart, 64)
    v1 = reduce(vpart, 64, 1)
    first.step(2)
    small.step(2)
    second = Column(net, dp, gd, 64, 64, 2)
    v0.pass_one()
    scores(0)
    first.step(3)
    small.step(3)
    scores(2)
    first.step(4)
    small.step(4)
    pair = small.pair()
    v1.pass_one()
    own.wait()
    second.step(1)
    v0.stage_two()
    first.last()
    sums(gd, dpart, 0)
    d0 = reduce(dpart, 0, 2)
    v1.stage_two()
    second.step(2)
    v0.pass_two()
    v1.pass_two()
    pair.wait_recv()
    total = gk[0, 0] * count[0]
    for i in range(1, 16):
        total = total + gk[i % 2, i // 2] * count[i]
    kown[...] = total
    kxs = [net.send(kown, kx.at[i], net.at(dx=k)) for i, k in enumerate((1, -1, 2))]
    d0.pass_one()
    scores(4)
    second.step(3)
    for copy in kxs:
        copy.wait_recv()
    kall[...] = kown[...] + kx[0] + kx[1] + kx[2]
    kys = [net.send(kall, ky.at[i], net.at(dy=k)) for i, k in enumerate((1, -1, 2))]
    scores(6)
    second.step(4)
    second.last()
    sums(gd, dpart, 64)
    d1 = reduce(dpart, 64, 3)
    d0.stage_two()
    for copy in kys:
        copy.wait_recv()
    ksum = kall[0:1, :] + ky[0, 0:1, :] + ky[1, 0:1, :] + ky[2, 0:1, :]
    lane = lax.broadcasted_iota(jnp.int32, (32, SIDE), 1)
    line = lax.broadcasted_iota(jnp.int32, (32, SIDE), 0)
    kcol = jnp.sum(jnp.where(lane == x * 32 + line, jnp.broadcast_to(ksum, (32, SIDE)), 0.0), axis=1, keepdims=True)
    up, down = net.at(dy=1), net.at(dy=-1)
    v0.finish()
    v1.finish()
    d1.pass_one()
    d0.pass_two()

    def settle(diff, var, g):
        def put(i, _):
            for h in range(2):
                v = var.total(h, i) + kcol * tq[g, h, i].astype(f32)
                gs[g, y, h, i] = (diff.total(h, i) / jnp.sqrt(jnp.maximum(v, 1.0))).astype(bf16)
            return 0

        lax.fori_loop(0, 8, put, 0)
        mine = gs.at[g, y]
        return net.send(mine, mine, up), net.send(mine, mine, down)

    def relay(pair_of, g):
        a, b = pair_of
        a.wait_recv()
        ref = gs.at[g, (y + 3) % 4, 0]
        a2 = net.send(ref, ref, up)
        b.wait_recv()
        ref = gs.at[g, (y + 1) % 4, 1]
        return a2, net.send(ref, ref, down)

    d0.finish()
    out0 = settle(d0, v0, 0)
    d1.stage_two()
    d1.pass_two()
    far0 = relay(out0, 0)
    d1.finish()
    out1 = settle(d1, v1, 1)
    far1 = relay(out1, 1)
    for copy in far0 + far1:
        copy.wait_recv()
    net.drain()


def tail(diff, squares, hot, count, tq, gv, img, hb, vb):
    f32, bf16 = jnp.float32, jnp.bfloat16
    tile = pltpu.VMEM((3, 8, 128), f32)
    return comm_call(
        tail_body,
        [((2, 4, 2, 8, 32, SIDE), bf16), ((256, 1024), f32)],
        "vv",
        [pltpu.VMEM((8, 2, SIDE, 16, SIDE), bf16), pltpu.VMEM((2, 8, 8, SIDE), f32),
         pltpu.VMEM((8, 2, SIDE, 16, SIDE), bf16), pltpu.VMEM((SIDE, 4, 32, SIDE), bf16),
         pltpu.VMEM((SIDE, 4, 32, SIDE), bf16), tile, tile, pltpu.VMEM((8, 128), f32), pltpu.VMEM((8, 128), f32)]
        + reduce_scratch(),
        184, 3, "tail", "vvvvvhvvv", 60,
    )(diff, squares, hot, count, tq, gv, img, hb, vb)


def local(
    template,
    template_var,
    science,
    science_var,
    routes_src,
    routes_blk,
    stamp_rows,
    stamp_cols,
    basis_col,
    basis_row,
    psf_col,
    psf_row,
):
    bf16, f32 = jnp.bfloat16, jnp.float32
    z, x, c, y = (lax.axis_index(a) for a in ("z", "x", "core", "y"))
    route = routes_src[0] * 32 + routes_blk[0]
    route = jnp.broadcast_to(jnp.pad(route, (0, 112))[None], (8, 128))
    gt, rz, rx = spread(template, route)
    wants = rx[:, 0, :16].reshape(64)
    owner = wants // 32
    here = (owner // 2) % 4 == x
    slot = (owner // 8) * 64 + (owner % 2) * 32 + wants % 32
    sel = pick(jnp.where(here, slot, -1), gt.reshape(512, SIDE, SIDE)).reshape(4, 16, SIDE, SIDE)
    svar = science_var[0].reshape(2, SIDE, 8, SIDE).transpose(1, 0, 2, 3).reshape(SIDE, 16, SIDE)
    xf = fetch(sel)
    frame = lax.dynamic_index_in_dim(sel, x, 0, keepdims=False) + xf[0] + xf[1] + xf[2]
    fp = jnp.pad(to_image(frame, 2, 8).astype(f32), ((10, 30), (10, 246)))
    stk, sst, wst, hb, vb = cut_call(
        stamp_rows[0], stamp_cols[0], fp, science[0], science_var[0], score_rows(psf_col[0], psf_row[0])
    )
    coef, diff, image, ks2, gv = fit_call(stk, sst, wst, fp, science[0], *bands(basis_col, basis_row), svar)
    goes = rz[:, :, 0, :16].transpose(1, 0, 2).reshape(256)
    owner = goes // 32
    ours = (owner // 8 == z) & (owner % 2 == c)
    target = jnp.where(ours, ((owner // 2) % 4) * 32 + goes % 32, -1)
    hot = target[None, :] == jnp.arange(SIDE)[:, None]
    count = jnp.sum(hot.reshape(SIDE, 16, 16).astype(f32), axis=2).T
    count = jnp.broadcast_to(count[:, None, :], (16, 8, SIDE))
    tq = lax.dynamic_index_in_dim(template_var.reshape(32, 2, 2, 4, 8, SIDE), y, 3, keepdims=False)
    gs, scored = tail(diff, ks2, hot.astype(bf16), count, tq.transpose(1, 2, 3, 0, 4), gv, image, hb, vb)
    significance = gs.transpose(4, 0, 2, 1, 3, 5).reshape(32, SIDE, SIDE)
    return (significance.astype(f32), scored[None], coef[:1, :41])


def solution(mesh):
    fine = Mesh(mesh.devices.reshape(8, 4, 2, 4), ("z", "x", "core", "y"))
    det = ("z", "x", "core")
    placed = (
        P(det, None, None),
        P(det, None, None),
        P("y", det, None),
        P("y", det, None),
        P("y", det),
        P("y", det),
        P("y", det),
        P("y", det),
        P(),
        P(),
        P("y", None),
        P("y", None),
    )
    return jax.shard_map(
        local,
        mesh=fine,
        in_specs=placed,
        out_specs=(P(det, None, None), P("y", det, None), P("y", det)),
        check_vma=False,
    )
```

```python
import jax, jax.numpy as jnp
from jax import lax
from jax.experimental import pallas as pl
from jax.experimental.pallas import tpu as pltpu

from jax.sharding import Mesh, PartitionSpec as P

HI = lax.Precision.HIGHEST
precise_mode = HI
RS = 520

def cut_body(rows_s, cols_s, fp_ref, sci_ref, var_ref, ps_ref, stk, sst, wst, hb_ref, vb_ref, sci32, var32):
    f32, bf16 = jnp.float32, jnp.bfloat16
    sci32[:256, :1024] = sci_ref[...].astype(f32)
    var32[:256, :1024] = var_ref[...].astype(f32)
    for s in range(4):
        y0 = rows_s[s]
        x0 = cols_s[s]
        xa = pl.multiple_of((x0 // 128) * 128, 128)
        rem = x0 - xa
        ya = pl.multiple_of((y0 // 8) * 8, 8)
        ry = y0 - ya
        t = pltpu.roll(fp_ref[pl.ds(ya, 168), pl.ds(xa, 384)], 168 - ry, 0)[:160]
        t = pltpu.roll(t, 384 - rem, 1)[:, :256]
        stk[s * 160:(s + 1) * 160, :] = t.astype(bf16)
        c = pltpu.roll(sci32[pl.ds(ya, 136), pl.ds(xa, 256)], 136 - ry, 0)[:128]
        sst[s * 128:(s + 1) * 128, :] = pltpu.roll(c, 256 - rem, 1)[:, :128]
        v = pltpu.roll(var32[pl.ds(ya, 136), pl.ds(xa, 256)], 136 - ry, 0)[:128]
        wst[s * 128:(s + 1) * 128, :] = jnp.sqrt(1.0 / pltpu.roll(v, 256 - rem, 1)[:, :128])

    def split(band):
        high = band.astype(bf16)
        return high, (band - high.astype(f32)).astype(bf16)

    h0, h1 = split(pltpu.roll(jnp.broadcast_to(ps_ref[0:1, :], (384, 512)), 0, 1, stride=1, stride_axis=0)[:, :128])
    hb_ref[:, :128] = h0
    hb_ref[:, 128:] = h1
    h0, h1 = split(pltpu.roll(jnp.broadcast_to(ps_ref[8:9, :], (256, 512)), 0, 1, stride=1, stride_axis=0)[:, :256])
    vb_ref[:, :256] = h0
    vb_ref[:, 256:512] = h1
    vb_ref[:, 512:] = h0


def cut_call(rows, cols, fp, sci, var, ps):
    f32, bf16 = jnp.float32, jnp.bfloat16
    sm = pl.BlockSpec(memory_space=pltpu.SMEM)
    vm = pl.BlockSpec(memory_space=pltpu.VMEM)
    return pl.pallas_call(
        cut_body,
        out_shape=(jax.ShapeDtypeStruct((640, 256), bf16), jax.ShapeDtypeStruct((512, 128), f32),
                   jax.ShapeDtypeStruct((512, 128), f32), jax.ShapeDtypeStruct((384, 256), bf16),
                   jax.ShapeDtypeStruct((256, 768), bf16)),
        in_specs=[sm, sm] + [vm] * 4,
        out_specs=(vm,) * 5,
        scratch_shapes=[pltpu.VMEM((264, 1152), f32), pltpu.VMEM((264, 1152), f32)],
        compiler_params=pltpu.CompilerParams(vmem_limit_bytes=60 << 20),
        name="cut",
    )(rows, cols, fp, sci, var, ps)


def fit_body(stk, sst, wst, fp_ref, sci_ref, cb_ref, rb_ref, bc_ref, br_ref, v_ref,
             coef_ref, diff_ref, img_ref, ks_ref, gv,
             sci32, dsg, wb, fs, conv, f128, rows32, ssem, rsem, lsem):
    f32, bf16 = jnp.float32, jnp.bfloat16
    net = Net(ssem, rsem)
    net.meet([net.at(dz=1), net.at(dz=-1), net.at(flip=True)])
    own = pltpu.make_async_copy(v_ref, gv.at[net.z, net.c], lsem.at[0])
    column = Column(net, v_ref, gv, 0, 128, 2)
    own.start()
    sci32[:256, :1024] = sci_ref[...].astype(f32)

    def per_basis(k, _):
        cb = jnp.broadcast_to(cb_ref[k][0:1], (128, 256))
        cb = pltpu.roll(cb, 0, 1, stride=1, stride_axis=0)[:, :160].astype(bf16)
        rb = jnp.broadcast_to(rb_ref[k][0:1], (256, 256))
        rb = pltpu.roll(rb, 0, 1, stride=1, stride_axis=0)[:, :128].astype(bf16)
        a = jnp.dot(stk[...], rb, preferred_element_type=f32).astype(bf16)
        a = jnp.concatenate([a[i * 160:(i + 1) * 160] for i in range(4)], axis=1)
        d = jnp.dot(cb, a, preferred_element_type=f32)
        for s in range(4):
            dsg[pl.ds(pl.multiple_of(k * RS + s * 128, 8), 128), :] = d[:, s * 128:(s + 1) * 128]
        return 0
    lax.fori_loop(0, 24, per_basis, 0)
    column.step(1)
    lax.fori_loop(24, 40, per_basis, 0)

    sub = lax.broadcasted_iota(jnp.int32, (8, 128), 0)

    def per_rows(g, acc):
        xs = []
        for q in range(8):
            r = g * 8 + q
            x = dsg[pl.ds(r, 40, stride=RS), :]
            srow = jnp.broadcast_to(sst[pl.ds(r, 1), :], (8, 128))
            extra = jnp.where(sub == 0, 1.0, jnp.where(sub == 1, srow, 0.0))
            x = jnp.concatenate([x, extra], axis=0)
            xs.append(x * jnp.broadcast_to(wst[pl.ds(r, 1), :], (48, 128)))
        x = jnp.concatenate(xs, axis=1)
        xh = x.astype(bf16)
        xl = (x - xh.astype(f32)).astype(bf16)
        nt = (((1,), (1,)), ((), ()))
        both = lax.dot_general(xh, jnp.concatenate([xh, xl], axis=0), nt, preferred_element_type=f32)
        return acc + both
    both = lax.fori_loop(0, 28, per_rows, jnp.zeros((48, 96), f32))
    column.step(2)
    both = lax.fori_loop(28, 64, per_rows, both)
    both = jnp.concatenate([both, jnp.zeros((48, 32), f32)], axis=1)
    cross = pltpu.roll(both, 80, 1)[:, :48]
    eye = (lax.broadcasted_iota(jnp.int32, (48, 48), 0) == lax.broadcasted_iota(jnp.int32, (48, 48), 1)).astype(f32)
    flip = lax.dot_general(cross, eye, (((0,), (0,)), ((), ())), precision=HI, preferred_element_type=f32)
    gram = both[:, :48] + cross + flip

    ri = lax.broadcasted_iota(jnp.int32, (48, 48), 0)
    ci = lax.broadcasted_iota(jnp.int32, (48, 48), 1)
    m = gram * (1.0 / 65536.0) + jnp.where((ri == ci) & (ri < 41), 0.01, 0.0)
    for n in range(41):
        prow = m[n:n + 1, :]
        pcol = m[:, n:n + 1]
        new = prow / m[n:n + 1, n:n + 1]
        m = jnp.where(ri == n, jnp.broadcast_to(new, (48, 48)), m - pcol * new)
    rcol = lax.broadcasted_iota(jnp.int32, (48, 1), 0)
    col = m[:, 41:42]
    row = jnp.sum(jnp.where(ri == ci, jnp.broadcast_to(col, (48, 48)), 0.0), axis=0, keepdims=True)
    coef_ref[...] = jnp.broadcast_to(jnp.pad(row, ((0, 0), (0, 80))), (8, 128))
    bg = m[40:41, 41:42]
    ccol = jnp.where(rcol < 40, col, 0.0)
    tn = (((0,), (0,)), ((), ()))
    ker = lax.dot_general(bc_ref[...] * ccol, br_ref[...], tn, precision=HI, preferred_element_type=f32)
    ker = ker[:24, :]
    ks = jnp.sum(ker, keepdims=True)
    ks_ref[...] = jnp.broadcast_to(ks * ks, (8, 128))
    wb[0, :, 128:] = jnp.zeros((256, 128), bf16)
    wb[21, :, :128] = jnp.zeros((256, 128), bf16)
    for dy in range(21):
        base = jnp.broadcast_to(ker[dy:dy + 1, :], (256, 256))
        band = pltpu.roll(base, 0, 1, stride=1, stride_axis=0)[:, :128].astype(bf16)
        wb[dy, :, :128] = band
        wb[dy + 1, :, 128:] = band
    for cc in range(9):
        sl = slice(cc * 128, (cc + 1) * 128)
        f128[cc] = fp_ref[:280, sl]
    for cc in range(9):
        sl = slice(cc * 128, (cc + 1) * 128)
        for dy in range(22):
            fs[dy, :, sl] = f128[cc, pl.ds(dy, 128, stride=2), :].astype(bf16)

    def per_col(c, _):
        c0 = pl.multiple_of(c * 128, 128)
        acc = jnp.zeros((128, 256), f32)
        for dy in range(22):
            acc = acc + jnp.dot(fs[dy, :, pl.ds(c0, 256)], wb[dy], preferred_element_type=f32)
        conv[pl.ds(0, 128, stride=2), :] = acc[:, :128]
        conv[pl.ds(1, 128, stride=2), :] = acc[:, 128:]
        for i in range(2):
            d = sci32[i * 128:(i + 1) * 128, pl.ds(c0, 128)] - conv[i * 128:(i + 1) * 128, :] - bg
            rows32[pl.ds(c + 8 * i, 128, stride=16), :] = d
            img_ref[i * 128:(i + 1) * 128, pl.ds(c0, 128)] = d.astype(bf16)
        return 0
    column.step(3)
    lax.fori_loop(0, 8, per_col, 0)
    diff_ref[...] = rows32[...].reshape(128, 16, 128).astype(bf16)
    column.step(4)
    column.last()
    own.wait()
    net.drain()

def fit_call(stk, sst, wst, fp, sci, cb, rb, bc, br, v):
    f32, bf16 = jnp.float32, jnp.bfloat16
    vm = pl.BlockSpec(memory_space=pltpu.VMEM)
    return pl.pallas_call(
        fit_body,
        out_shape=(jax.ShapeDtypeStruct((8, 128), f32), jax.ShapeDtypeStruct((128, 16, 128), bf16),
                   jax.ShapeDtypeStruct((256, 1024), bf16),
                   jax.ShapeDtypeStruct((8, 128), f32),
                   jax.ShapeDtypeStruct((8, 2, 128, 16, 128), bf16)),
        in_specs=[vm] * 10,
        out_specs=(vm,) * 4 + (pl.BlockSpec(memory_space=pltpu.HBM),),
        scratch_shapes=[
            pltpu.VMEM((264, 1152), f32), pltpu.VMEM((40 * RS, 128), f32),
            pltpu.VMEM((22, 256, 256), bf16), pltpu.VMEM((22, 128, 1152), bf16),
            pltpu.VMEM((256, 128), f32), pltpu.VMEM((9, 280, 128), f32),
            pltpu.VMEM((2048, 128), f32), pltpu.SemaphoreType.DMA((32,)), pltpu.SemaphoreType.DMA((32,)),
            pltpu.SemaphoreType.DMA((1,))],
        compiler_params=pltpu.CompilerParams(
            vmem_limit_bytes=60 * 1024 * 1024, collective_id=5, has_side_effects=True),
        name="fit",
    )(stk, sst, wst, fp, sci, cb, rb, bc, br, v)

def bands(basis_col, basis_row):
    col = jnp.pad(basis_col.astype(jnp.float32), ((0, 8), (0, 235)))
    row = jnp.pad(basis_row.astype(jnp.float32), ((0, 8), (0, 0)))
    rev = jnp.concatenate([row[:, :1], jnp.zeros((48, 235), jnp.float32), row[:, :0:-1]], axis=1)
    cb = col[:40, None, :]
    rb = rev[:40, None, :]
    return cb, rb, col[:, :128], rev


def score_rows(psf_down, psf_across):
    flat = jnp.concatenate([jnp.zeros((374,), jnp.float32), psf_across[::-1], jnp.zeros((117,), jnp.float32)])
    tall = jnp.concatenate([psf_down[10:], jnp.zeros((491,), jnp.float32), psf_down[:10]])
    return jnp.concatenate([jnp.broadcast_to(flat[None], (8, 512)), jnp.broadcast_to(tall[None], (8, 512))])


def pick_body(where_s, gt, out, sems):
    def copy(i):
        return pltpu.make_async_copy(gt.at[where_s[i]], out.at[i], sems.at[i])

    def begin(i, _):
        @pl.when(where_s[i] >= 0)
        def _():
            copy(i).start()

        @pl.when(where_s[i] < 0)
        def _():
            out[i] = jnp.zeros((128, 128), jnp.bfloat16)
        return 0

    def done(i, _):
        @pl.when(where_s[i] >= 0)
        def _():
            copy(i).wait()
        return 0

    lax.fori_loop(0, 64, begin, 0)
    lax.fori_loop(0, 64, done, 0)


def pick(where_at, gt):
    return pl.pallas_call(
        pick_body,
        out_shape=jax.ShapeDtypeStruct((64, 128, 128), jnp.bfloat16),
        in_specs=[pl.BlockSpec(memory_space=pltpu.SMEM), pl.BlockSpec(memory_space=pltpu.HBM)],
        out_specs=pl.BlockSpec(memory_space=pltpu.VMEM),
        scratch_shapes=[pltpu.SemaphoreType.DMA((64,))],
        compiler_params=pltpu.CompilerParams(vmem_limit_bytes=60 << 20),
        name="pick",
    )(where_at, gt)


def to_image(blocks, block_rows, block_cols):
    block_side = blocks.shape[-1]
    shaped = blocks.reshape(block_rows, block_cols, block_side, block_side).transpose(0, 2, 1, 3)
    return shaped.reshape(block_rows * block_side, block_cols * block_side)


MESH_ID = pl.DeviceIdType.MESH
SIDE = 128


class Net:
    def __init__(self, ssem, rsem):
        self.ssem, self.rsem, self.sent = ssem, rsem, []
        self.z, self.x, self.c, self.y = (lax.axis_index(a) for a in ("z", "x", "core", "y"))

    def at(self, dz=0, dx=0, dy=0, flip=False):
        c = 1 - self.c if flip else self.c
        return ((self.z + dz + 8) % 8, (self.x + dx + 4) % 4, c, (self.y + dy + 4) % 4)

    def meet(self, peers):
        barrier = pltpu.get_barrier_semaphore()
        for peer in peers:
            pl.semaphore_signal(barrier, inc=1, device_id=peer, device_id_type=MESH_ID)
        pl.semaphore_wait(barrier, len(peers))

    def send(self, src, dst, peer):
        i = len(self.sent)
        copy = pltpu.make_async_remote_copy(
            src_ref=src, dst_ref=dst, send_sem=self.ssem.at[i], recv_sem=self.rsem.at[i],
            device_id=peer, device_id_type=MESH_ID,
        )
        copy.start()
        self.sent.append(copy)
        return copy

    def drain(self):
        for copy in self.sent:
            copy.wait_send()


class ZRing:
    def __init__(self, net, own, out, pieces, arrive):
        self.net, self.out, self.pieces, self.arrive = net, out, pieces, arrive
        self.got = {}
        for p, (start, size) in enumerate(pieces):
            for d in (1, -1):
                self.got[d, 1, p] = net.send(
                    own.at[pl.ds(start, size)], out.at[net.z, net.c, pl.ds(start, size)], net.at(dz=d)
                )

    def part(self, p, d, s):
        start, size = self.pieces[p]
        if s < 4:
            return pl.ds(start, size)
        return pl.ds(start + (0 if d == 1 else size // 2), size // 2)

    def step(self, s):
        net = self.net
        for p in range(len(self.pieces)):
            for d in (1, -1):
                self.got[d, s, p].wait_recv()
                zs = (net.z - d * s + 8) % 8
                if s < 4:
                    ref = self.out.at[zs, net.c, self.part(p, d, s + 1)]
                    self.got[d, s + 1, p] = net.send(ref, ref, net.at(dz=d))
                self.arrive(p, d, s, zs, self.part(p, d, s))


class SmallRing:
    def __init__(self, net, own, out):
        self.net, self.out = net, out
        out[net.c, net.z] = own[...]
        self.got = {(d, 1): net.send(own, out.at[net.c, net.z], net.at(dz=d)) for d in (1, -1)}

    def step(self, s):
        net = self.net
        for d in (1, -1):
            if (d, s) not in self.got:
                continue
            self.got[d, s].wait_recv()
            zs = (net.z - d * s + 8) % 8
            if s + 1 <= (4 if d == 1 else 3):
                ref = self.out.at[net.c, zs]
                self.got[d, s + 1] = net.send(ref, ref, net.at(dz=d))

    def pair(self):
        ref = self.out.at[self.net.c]
        return self.net.send(ref, ref, self.net.at(flip=True))


class Ring4:
    def __init__(self, net, axis, src, dst, relay):
        self.net, self.dst, self.relay = net, dst, relay
        self.up = net.at(**{axis: 1})
        self.down = net.at(**{axis: -1})
        self.fa = net.send(src(2, 0), relay(0), self.up)
        self.fb = net.send(src(2, 1), relay(1), self.down)
        self.na = net.send(src(1, None), dst(0, None), self.up)
        self.nb = net.send(src(-1, None), dst(1, None), self.down)

    def pass_on(self):
        self.fa.wait_recv()
        self.ra = self.net.send(self.relay(0), self.dst(2, 0), self.up)
        self.fb.wait_recv()
        self.rb = self.net.send(self.relay(1), self.dst(2, 1), self.down)

    def finish(self):
        for copy in (self.na, self.nb, self.ra, self.rb):
            copy.wait_recv()


def comm_call(body, outs, spaces, scratch, copies, ident, name, in_spaces, side_bytes):
    def spec(space):
        return pl.BlockSpec(memory_space={"v": pltpu.VMEM, "a": pl.ANY, "h": pltpu.HBM}[space])

    return pl.pallas_call(
        body,
        out_shape=tuple(jax.ShapeDtypeStruct(s, d) for s, d in outs),
        in_specs=[spec(s) for s in in_spaces],
        out_specs=tuple(spec(s) for s in spaces),
        scratch_shapes=list(scratch)
        + [pltpu.SemaphoreType.DMA((copies,)), pltpu.SemaphoreType.DMA((copies,)), pltpu.SemaphoreType.DMA((2,))],
        compiler_params=pltpu.CompilerParams(
            collective_id=ident, has_side_effects=True, vmem_limit_bytes=side_bytes << 20
        ),
        name=name,
    )


def spread_body(t_ref, r_ref, gt, rz, rx, ssem, rsem, lsem):
    net = Net(ssem, rsem)
    z, x, c, y = net.z, net.x, net.c, net.y
    net.meet([net.at(dz=1), net.at(dz=-1), net.at(dy=1), net.at(dy=-1),
              net.at(dx=1), net.at(dx=-1), net.at(dx=2), net.at(flip=True)])
    own = pltpu.make_async_copy(t_ref, gt.at[z, c], lsem.at[0])
    small = SmallRing(net, r_ref, rz)
    rx[x] = r_ref[...]
    row = [net.send(r_ref, rx.at[x], net.at(dx=k)) for k in (1, -1, 2)]
    q0 = y * 8
    q1 = ((y + 1) % 4) * 8
    up = {}

    def arrive(p, d, s, zs, part):
        ref = gt.at[zs, c, part]
        up[p, d, s] = net.send(ref, ref, net.at(dy=1 if p % 2 == 0 else -1))

    ring = ZRing(net, t_ref, gt, [(q0, 4), (q1, 4), (q0 + 4, 4), (q1 + 4, 4)], arrive)
    own.start()
    ref = gt.at[z, c]
    pair = [net.send(t_ref, ref, net.at(flip=True))]

    def hand_over(s):
        for d in (1, -1):
            for p in range(4):
                up[p, d, s].wait_recv()
            if s < 4:
                ref = gt.at[(z - d * s + 8) % 8, c]
                pair.append(net.send(ref, ref, net.at(flip=True)))
        if s == 4:
            ref = gt.at[(z + 4) % 8, c]
            pair.append(net.send(ref, ref, net.at(flip=True)))

    for s in range(1, 5):
        ring.step(s)
        small.step(s)
        if s > 1:
            hand_over(s - 1)
    for copy in row:
        copy.wait_recv()
    small_pair = small.pair()
    hand_over(4)
    for copy in pair:
        copy.wait_recv()
    small_pair.wait_recv()
    own.wait()
    net.drain()


def spread(template, route):
    return comm_call(
        spread_body,
        [((8, 2, 32, SIDE, SIDE), jnp.bfloat16), ((2, 8, 8, 128), jnp.int32), ((4, 8, 128), jnp.int32)],
        "hvv", [], 84, 1, "spread", "vv", 60,
    )(template, route)


class Column:
    def __init__(self, net, own, out, base, size, pieces):
        self.net, self.out, self.base, self.size = net, out, base, size
        rows = pl.ds(base, size)
        self.pair = [net.send(own.at[rows], out.at[net.z, net.c, rows], net.at(flip=True))]
        cut = size // pieces
        self.ring = ZRing(net, own, out, [(base + i * cut, cut) for i in range(pieces)], self.arrive)
        self.step = self.ring.step

    def arrive(self, p, d, s, zs, part):
        if s < 4:
            ref = self.out.at[zs, self.net.c, part]
            self.pair.append(self.net.send(ref, ref, self.net.at(flip=True)))

    def last(self):
        ref = self.out.at[(self.net.z + 4) % 8, self.net.c, pl.ds(self.base, self.size)]
        self.pair.append(self.net.send(ref, ref, self.net.at(flip=True)))
        for copy in self.pair:
            copy.wait_recv()


def fetch_body(sel, xf, relay, ssem, rsem, lsem):
    net = Net(ssem, rsem)
    net.meet([net.at(dx=1), net.at(dx=-1)])

    def src(k, half):
        part = pl.ds(0, 16) if half is None else pl.ds(8 * half, 8)
        return sel.at[(net.x + k + 4) % 4, part]

    def dst(slot, half):
        return xf.at[slot] if half is None else xf.at[slot, pl.ds(8 * half, 8)]

    side = Ring4(net, "dx", src, dst, lambda i: relay.at[i])
    side.pass_on()
    side.finish()
    net.drain()


def fetch(sel):
    return comm_call(
        fetch_body,
        [((3, 16, SIDE, SIDE), jnp.bfloat16)],
        "v", [pltpu.VMEM((2, 8, SIDE, SIDE), jnp.bfloat16)], 8, 2, "fetch", "v", 60,
    )(sel)[0]


def reduce_scratch():
    def buf(*shape):
        return pltpu.VMEM((4,) + shape + (32, SIDE), jnp.bfloat16)

    return [buf(3, 32), buf(3, 8, 4), buf(2, 16), buf(2, 4, 4), buf(32), buf(8, 4),
            buf(3, 8), buf(3, 8), buf(2, 4), buf(2, 4)]


class Reduce:
    def __init__(self, net, part, base, bufs):
        (self.a0, self.b0, ra, rb, self.ha, self.hb, self.a1, self.b1, self.ra1, self.rb1) = bufs
        self.net, self.part, self.base = net, part, base
        x, y = net.x, net.y

        def src_a(k, half):
            rows = pl.ds(base, 32) if half is None else pl.ds(base + 16 * half, 16)
            return part.at[rows, (x + k + 4) % 4]

        def dst_a(slot, half):
            return self.a0.at[slot] if half is None else self.a0.at[slot, pl.ds(16 * half, 16)]

        def src_b(k, half):
            first = base + 32 + 8 * ((y + k + 4) % 4)
            return part.at[pl.ds(first, 8) if half is None else pl.ds(first + 4 * half, 4)]

        def dst_b(slot, half):
            return self.b0.at[slot] if half is None else self.b0.at[slot, pl.ds(4 * half, 4)]

        self.one = [Ring4(net, "dx", src_a, dst_a, lambda i: ra.at[i]),
                    Ring4(net, "dy", src_b, dst_b, lambda i: rb.at[i])]

    def pass_one(self):
        for ring in self.one:
            ring.pass_on()

    def stage_two(self):
        net = self.net
        x, y = net.x, net.y
        for ring in self.one:
            ring.finish()
        f32 = jnp.float32

        def add_a(i, _):
            total = self.part[self.base + i, x].astype(f32)
            for slot in range(3):
                total = total + self.a0[slot, i].astype(f32)
            self.ha[i] = total.astype(jnp.bfloat16)
            return 0

        def add_b(i, _):
            total = self.part[self.base + 32 + 8 * y + i].astype(f32)
            for slot in range(3):
                total = total + self.b0[slot, i].astype(f32)
            self.hb[i] = total.astype(jnp.bfloat16)
            return 0

        lax.fori_loop(0, 32, add_a, 0)
        lax.fori_loop(0, 8, add_b, 0)

        def src_a(k, half):
            first = 8 * ((y + k + 4) % 4)
            return self.ha.at[pl.ds(first, 8) if half is None else pl.ds(first + 4 * half, 4)]

        def dst_a(slot, half):
            return self.a1.at[slot] if half is None else self.a1.at[slot, pl.ds(4 * half, 4)]

        def src_b(k, half):
            return self.hb.at[pl.ds(0, 8) if half is None else pl.ds(4 * half, 4), (x + k + 4) % 4]

        def dst_b(slot, half):
            return self.b1.at[slot] if half is None else self.b1.at[slot, pl.ds(4 * half, 4)]

        self.two = [Ring4(net, "dy", src_a, dst_a, lambda i: self.ra1.at[i]),
                    Ring4(net, "dx", src_b, dst_b, lambda i: self.rb1.at[i])]

    def pass_two(self):
        for ring in self.two:
            ring.pass_on()

    def finish(self):
        for ring in self.two:
            ring.finish()

    def total(self, h, i):
        f32 = jnp.float32
        if h == 0:
            own, got = self.ha[8 * self.net.y + i], self.a1
        else:
            own, got = self.hb[i, self.net.x], self.b1
        total = own.astype(f32)
        for slot in range(3):
            total = total + got[slot, i].astype(f32)
        return total


def tail_body(dp, ks, hot, count, tq, gv, img, hb, vb, gs, score, gd, gk, vv, vpart, dpart, kx, ky, kown, kall, *rest):
    bufs, (ssem, rsem, lsem) = rest[:10], rest[10:]
    net = Net(ssem, rsem)
    x, y = net.x, net.y
    f32, bf16 = jnp.float32, jnp.bfloat16
    fetch_v = pltpu.make_async_copy(gv, vv, lsem.at[0])
    fetch_v.start()
    net.meet([net.at(dz=1), net.at(dz=-1), net.at(dx=1), net.at(dx=-1), net.at(dx=2),
              net.at(dy=1), net.at(dy=-1), net.at(dy=2), net.at(flip=True)])
    own = pltpu.make_async_copy(dp, gd.at[net.z, net.c], lsem.at[1])
    first = Column(net, dp, gd, 0, 64, 2)
    own.start()
    small = SmallRing(net, ks, gk)
    fetch_v.wait()

    def sums(column, part, base):
        def one(i, _):
            for u in (0, 2):
                p = base + 4 * i + u
                rows = [column[:, :, p + v].reshape(256, SIDE) for v in range(2)]
                got = jnp.dot(hot[...], jnp.concatenate(rows, axis=1), preferred_element_type=f32).astype(bf16)
                for v in range(2):
                    part[p + v] = got[:, v * SIDE:(v + 1) * SIDE].reshape(4, 32, SIDE)
            return 0

        lax.fori_loop(0, 16, one, 0)

    def scores(first_block):
        for c in (first_block, first_block + 1):
            low, high = max(c - 1, 0), min(c + 2, 8)
            window = hb[(low - c + 1) * SIDE:(high - c + 1) * SIDE]
            side = jnp.dot(img[:, low * SIDE:high * SIDE], window, preferred_element_type=f32)
            side = side[:, :SIDE] + side[:, SIDE:]
            top = side.astype(bf16)
            rest_ = (side - top.astype(f32)).astype(bf16)
            stack = jnp.concatenate([top, top, rest_], axis=0)
            score[:, c * SIDE:(c + 1) * SIDE] = jnp.dot(vb[...], stack, preferred_element_type=f32)

    def reduce(part, base, g):
        return Reduce(net, part, base, [b.at[g] for b in bufs])

    sums(vv, vpart, 0)
    v0 = reduce(vpart, 0, 0)
    first.step(1)
    small.step(1)
    sums(vv, vpart, 64)
    v1 = reduce(vpart, 64, 1)
    first.step(2)
    small.step(2)
    second = Column(net, dp, gd, 64, 64, 2)
    v0.pass_one()
    first.step(3)
    small.step(3)
    first.step(4)
    small.step(4)
    pair = small.pair()
    v1.pass_one()
    own.wait()
    second.step(1)
    v0.stage_two()
    first.last()
    sums(gd, dpart, 0)
    d0 = reduce(dpart, 0, 2)
    v1.stage_two()
    second.step(2)
    v0.pass_two()
    v1.pass_two()
    pair.wait_recv()
    total = gk[0, 0] * count[0]
    for i in range(1, 16):
        total = total + gk[i % 2, i // 2] * count[i]
    kown[...] = total
    kxs = [net.send(kown, kx.at[i], net.at(dx=k)) for i, k in enumerate((1, -1, 2))]
    d0.pass_one()
    second.step(3)
    for copy in kxs:
        copy.wait_recv()
    kall[...] = kown[...] + kx[0] + kx[1] + kx[2]
    kys = [net.send(kall, ky.at[i], net.at(dy=k)) for i, k in enumerate((1, -1, 2))]
    second.step(4)
    second.last()
    sums(gd, dpart, 64)
    d1 = reduce(dpart, 64, 3)
    d0.stage_two()
    for copy in kys:
        copy.wait_recv()
    ksum = kall[0:1, :] + ky[0, 0:1, :] + ky[1, 0:1, :] + ky[2, 0:1, :]
    lane = lax.broadcasted_iota(jnp.int32, (32, SIDE), 1)
    line = lax.broadcasted_iota(jnp.int32, (32, SIDE), 0)
    kcol = jnp.sum(jnp.where(lane == x * 32 + line, jnp.broadcast_to(ksum, (32, SIDE)), 0.0), axis=1, keepdims=True)
    up, down = net.at(dy=1), net.at(dy=-1)
    v0.finish()
    v1.finish()
    d1.pass_one()
    d0.pass_two()
    scores(0)

    def settle(diff, var, g):
        def put(i, _):
            for h in range(2):
                v = var.total(h, i) + kcol * tq[g, h, i].astype(f32)
                gs[g, y, h, i] = (diff.total(h, i) / jnp.sqrt(jnp.maximum(v, 1.0))).astype(bf16)
            return 0

        lax.fori_loop(0, 8, put, 0)
        mine = gs.at[g, y]
        return net.send(mine, mine, up), net.send(mine, mine, down)

    def relay(pair_of, g):
        a, b = pair_of
        a.wait_recv()
        ref = gs.at[g, (y + 3) % 4, 0]
        a2 = net.send(ref, ref, up)
        b.wait_recv()
        ref = gs.at[g, (y + 1) % 4, 1]
        return a2, net.send(ref, ref, down)

    d0.finish()
    out0 = settle(d0, v0, 0)
    scores(2)
    d1.stage_two()
    d1.pass_two()
    scores(4)
    far0 = relay(out0, 0)
    d1.finish()
    out1 = settle(d1, v1, 1)
    scores(6)
    far1 = relay(out1, 1)
    for copy in far0 + far1:
        copy.wait_recv()
    net.drain()


def tail(diff, squares, hot, count, tq, gv, img, hb, vb):
    f32, bf16 = jnp.float32, jnp.bfloat16
    tile = pltpu.VMEM((3, 8, 128), f32)
    return comm_call(
        tail_body,
        [((2, 4, 2, 8, 32, SIDE), bf16), ((256, 1024), f32)],
        "vv",
        [pltpu.VMEM((8, 2, SIDE, 16, SIDE), bf16), pltpu.VMEM((2, 8, 8, SIDE), f32),
         pltpu.VMEM((8, 2, SIDE, 16, SIDE), bf16), pltpu.VMEM((SIDE, 4, 32, SIDE), bf16),
         pltpu.VMEM((SIDE, 4, 32, SIDE), bf16), tile, tile, pltpu.VMEM((8, 128), f32), pltpu.VMEM((8, 128), f32)]
        + reduce_scratch(),
        184, 3, "tail", "vvvvvhvvv", 60,
    )(diff, squares, hot, count, tq, gv, img, hb, vb)


def local(
    template,
    template_var,
    science,
    science_var,
    routes_src,
    routes_blk,
    stamp_rows,
    stamp_cols,
    basis_col,
    basis_row,
    psf_col,
    psf_row,
):
    bf16, f32 = jnp.bfloat16, jnp.float32
    z, x, c, y = (lax.axis_index(a) for a in ("z", "x", "core", "y"))
    route = routes_src[0] * 32 + routes_blk[0]
    route = jnp.broadcast_to(jnp.pad(route, (0, 112))[None], (8, 128))
    gt, rz, rx = spread(template, route)
    wants = rx[:, 0, :16].reshape(64)
    owner = wants // 32
    here = (owner // 2) % 4 == x
    slot = (owner // 8) * 64 + (owner % 2) * 32 + wants % 32
    sel = pick(jnp.where(here, slot, -1), gt.reshape(512, SIDE, SIDE)).reshape(4, 16, SIDE, SIDE)
    svar = science_var[0].reshape(2, SIDE, 8, SIDE).transpose(1, 0, 2, 3).reshape(SIDE, 16, SIDE)
    xf = fetch(sel)
    frame = lax.dynamic_index_in_dim(sel, x, 0, keepdims=False) + xf[0] + xf[1] + xf[2]
    fp = jnp.pad(to_image(frame, 2, 8).astype(f32), ((10, 30), (10, 246)))
    stk, sst, wst, hb, vb = cut_call(
        stamp_rows[0], stamp_cols[0], fp, science[0], science_var[0], score_rows(psf_col[0], psf_row[0])
    )
    coef, diff, image, ks2, gv = fit_call(stk, sst, wst, fp, science[0], *bands(basis_col, basis_row), svar)
    goes = rz[:, :, 0, :16].transpose(1, 0, 2).reshape(256)
    owner = goes // 32
    ours = (owner // 8 == z) & (owner % 2 == c)
    target = jnp.where(ours, ((owner // 2) % 4) * 32 + goes % 32, -1)
    hot = target[None, :] == jnp.arange(SIDE)[:, None]
    count = jnp.sum(hot.reshape(SIDE, 16, 16).astype(f32), axis=2).T
    count = jnp.broadcast_to(count[:, None, :], (16, 8, SIDE))
    tq = lax.dynamic_index_in_dim(template_var.reshape(32, 2, 2, 4, 8, SIDE), y, 3, keepdims=False)
    gs, scored = tail(diff, ks2, hot.astype(bf16), count, tq.transpose(1, 2, 3, 0, 4), gv, image, hb, vb)
    significance = gs.transpose(4, 0, 2, 1, 3, 5).reshape(32, SIDE, SIDE)
    return (significance.astype(f32), scored[None], coef[:1, :41])


def solution(mesh):
    fine = Mesh(mesh.devices.reshape(8, 4, 2, 4), ("z", "x", "core", "y"))
    det = ("z", "x", "core")
    placed = (
        P(det, None, None),
        P(det, None, None),
        P("y", det, None),
        P("y", det, None),
        P("y", det),
        P("y", det),
        P("y", det),
        P("y", det),
        P(),
        P(),
        P("y", None),
        P("y", None),
    )
    return jax.shard_map(
        local,
        mesh=fine,
        in_specs=placed,
        out_specs=(P(det, None, None), P("y", det, None), P("y", det)),
        check_vma=False,
    )
```
